32 devices in a mesh: img: 8 (over z, x), band: 2 (over y), head: 2 (over core).
Axes of the slice: x: 2, y: 2, z: 4, core: 2. Of those that a mesh axis runs over, the one named last changes fastest.
Arguments:
- tokens: bfloat16 [8, 16, 16, 1152], P('img', 'band'), may hold values from -6 to 6
- timesteps: int32 [8], P('img'), may hold values from 0 to 999
- first_gain: float32 [1152], replicated, may hold values from 0.5 to 1.5
- first_shift: float32 [1152], replicated, may hold values from -3 to 3
- project_in: bfloat16 [1152, 3, 1152], P(None, None, 'head'), may hold values from -0.1875 to 0.1875
- time_weight: bfloat16 [1152, 2, 1152], P(None, None, 'head'), may hold values from -0.1875 to 0.1875
- bias_table: float32 [16, 25], P('head'), may hold values from -4 to 4
- bias_index: int32 [25], replicated, may hold values from 0 to 24, each once
- project_out: bfloat16 [1152, 1152], P('head'), may hold values from -0.875 to 0.875
- out_shift: float32 [1152], replicated, may hold values from -3 to 3
- second_gain: float32 [1152], replicated, may hold values from 0.5 to 1.5
- second_shift: float32 [1152], replicated, may hold values from -3 to 3
- up_weight: bfloat16 [1152, 4608], P(None, 'head'), may hold values from -0.1875 to 0.1875
- up_shift: float32 [4608], P('head'), may hold values from -3 to 3
- down_weight: bfloat16 [4608, 1152], P('head'), may hold values from -0.09375 to 0.09375
- down_shift: float32 [1152], replicated, may hold values from -3 to 3
- cotangent: bfloat16 [8, 16, 16, 1152], P('img', 'band'), may hold values from -6 to 6
Outputs:
- output: bfloat16 [8, 16, 16, 1152], P('img', 'band')
- tokens_grad: float32 [8, 16, 16, 1152], P('img', 'band')
- first_gain_grad: float32 [1152], replicated
- first_shift_grad: float32 [1152], replicated
- project_in_grad: float32 [1152, 3, 1152], P(('img', 'band'), None, 'head')
- time_weight_grad: float32 [1152, 2, 1152], P(('img', 'band'), None, 'head')
- bias_table_grad: float32 [16, 25], P('head')
- project_out_grad: float32 [1152, 1152], P('head', ('img', 'band'))
- out_shift_grad: float32 [1152], replicated
- second_gain_grad: float32 [1152], replicated
- second_shift_grad: float32 [1152], replicated
- up_weight_grad: float32 [1152, 4608], P(('img', 'band'), 'head')
- up_shift_grad: float32 [4608], P('head')
- down_weight_grad: float32 [4608, 1152], P('head', ('img', 'band'))
- down_shift_grad: float32 [1152], replicated
The draws below stay inside these ranges and needn't reach their ends.
Inputs may be any that keep to these rules, and one draw needn't show every extreme that they name: `bias_index`: each entry of the table appears exactly once.
All inputs are finite; a program needn't handle non-finite values.
Results may differ from the reference program's by a relative error of at most 0.014.
Values may be sent and summed in bfloat16 or wider, within the bound.
A program may use at most 256 MiB of HBM per device.

```python
import math
import jax
import jax.numpy as jnp
from jax import lax

D = 1152
HEADS = 16
HD = 72
FF = 4608
ROWS = 16
COLS = 16
WIN = 5
STEPS = 1000
BIAS_N = 25
IMAGES = 8


def place_ends(array, stream_key, smallest, largest):
    extent = array.shape
    place = [jax.random.randint(jax.random.fold_in(stream_key, axis), (), 0, extent[axis]) for axis in range(len(extent))]
    array = array.at[tuple(place)].set(smallest)
    longest = extent.index(max(extent))
    place[longest] = (place[longest] + 1) % extent[longest]
    return array.at[tuple(place)].set(largest)


def strengthened(drawn, own_key, source, target, parts, factor):
    owner, partner = [(jnp.arange(drawn.shape[position]) // (drawn.shape[position] // parts)).reshape([-1 if axis == position else 1 for axis in range(drawn.ndim)]) for position in (source, target)]
    chosen = jax.random.permutation(own_key, parts)[partner]
    strong = (owner == chosen) | (owner == (partner + parts // 2) % parts)
    return jnp.where(strong, factor * drawn, drawn)


def shard_levels(rng, shape, shards, least, high):
    def one(axis_at, parts):
        draws = jax.random.uniform(jax.random.fold_in(jax.random.fold_in(rng, 6), axis_at), (parts,), jnp.float32, least / len(shards), high / len(shards))
        return jnp.repeat(jnp.exp(draws), shape[axis_at] // parts).reshape((-1,) + (1,) * (len(shape) - axis_at - 1))

    level = one(*shards[0])
    for cut in shards[1:]:
        level = level * one(*cut)
    return level


def centred(key, dims, scale, limit, shards=(), kind=jnp.bfloat16):
    values = jax.random.normal(key, dims, jnp.float32) * scale
    if len(shards) > 0:
        values = shard_levels(key, dims, shards, -0.22, 0.18) * values
    return jnp.clip(values, min=-limit, max=limit).astype(kind)


def bell_draw_with(own_key, dims, scale, bound, shards, heavy, kind=jnp.bfloat16):
    entries = scale * jax.random.normal(own_key, dims, jnp.float32)
    if shards:
        entries = entries * shard_levels(own_key, dims, shards, -0.22, 0.18)
    return jnp.clip(strengthened(entries, jax.random.fold_in(own_key, 3), *heavy), -bound, bound).astype(kind)


def setup_inputs(seed: int = 0) -> dict:
    splits = jax.random.split(jax.random.key(seed), 18)
    return {
        "tokens": centred(splits[0], (IMAGES, ROWS, COLS, D), 1.0, 6.0, ((0, 8), (1, 2))),
        "timesteps": place_ends(jax.random.randint(splits[1], (IMAGES,), 0, STEPS), jax.random.fold_in(splits[1], 1), 0, STEPS - 1).astype(jnp.int32),
        "first_gain": jnp.clip(1.0 + 0.1 * jax.random.normal(splits[2], (D,), jnp.float32), 0.5, 1.5),
        "first_shift": centred(splits[3], (D,), 0.3, 3.0, (), jnp.float32),
        "project_in": centred(splits[4], (D, 3, D), D ** -0.5, 0.1875, ((2, 2),)),
        "time_weight": centred(splits[5], (D, 2, D), D ** -0.5, 0.1875, ((2, 2),)),
        "bias_table": centred(splits[6], (HEADS, BIAS_N), 1.0, 4.0, ((0, 2),), jnp.float32),
        "bias_index": jax.random.permutation(splits[7], BIAS_N).astype(jnp.int32),
        "project_out": centred(splits[8], (D, D), (D // 25) ** -0.5, 0.875, ((0, 2),)),
        "out_shift": centred(splits[9], (D,), 0.3, 3.0, (), jnp.float32),
        "second_gain": jnp.clip(1.0 + 0.1 * jax.random.normal(splits[10], (D,), jnp.float32), 0.5, 1.5),
        "second_shift": centred(splits[11], (D,), 0.3, 3.0, (), jnp.float32),
        "up_weight": centred(splits[12], (D, FF), D ** -0.5, 0.1875, ((1, 2),)),
        "up_shift": centred(splits[13], (FF,), 0.3, 3.0, ((0, 2),), jnp.float32),
        "down_weight": centred(splits[14], (FF, D), FF ** -0.5, 0.09375, ((0, 2),)),
        "down_shift": centred(splits[15], (D,), 0.3, 3.0, (), jnp.float32),
        "cotangent": bell_draw_with(splits[16], (IMAGES, ROWS, COLS, D), 1.0, 6.0, ((0, 8), (1, 2)), (0, 3, 8, 2.0)),
    }


@jax.custom_vjp
def low(v):
    return lax.optimization_barrier(v.astype(jnp.bfloat16)).astype(jnp.float32)

@jax.custom_vjp
def low_back(v):
    return v

def low_keep(v):
    return (low(v), None)

def low_pass(kept, grad):
    return (grad,)

def back_keep(v):
    return (v, None)

def back_low(kept, grad):
    return (low(grad),)
low.defvjp(low_keep, low_pass)
low_back.defvjp(back_keep, back_low)
epsilon = 1e-05
image_block = 8
highest = lax.Precision.HIGHEST
masked_score = -1000000000.0

def layer_norm(values, gain, shift):
    center = values - lax.optimization_barrier(jnp.mean(values, axis=-1, keepdims=True))
    spread = lax.optimization_barrier(jnp.mean(center * center, axis=-1, keepdims=True))
    return center * lax.rsqrt(spread + epsilon) * gain + shift

def time_features(timesteps, width):
    half = width // 2
    freqs = jnp.exp(jnp.arange(half, dtype=jnp.float32) * (-math.log(10000.0) / half))
    angles = timesteps.astype(jnp.float32)[:, None] * freqs[None, :]
    return jnp.concatenate([jnp.cos(angles), jnp.sin(angles)], axis=1)

def window_valid(row_start, row_count, column_count):
    reach = WIN // 2
    global_rows = row_start + jnp.arange(row_count, dtype=jnp.int32)
    columns = jnp.arange(column_count, dtype=jnp.int32)
    masks = []
    for tap in range(WIN * WIN):
        row_step = tap // WIN - reach
        col_step = tap % WIN - reach
        row_ok = (global_rows + row_step >= 0) & (global_rows + row_step < ROWS)
        col_ok = (columns + col_step >= 0) & (columns + col_step < COLS)
        masks.append(row_ok[:, None] & col_ok[None, :])
    return jnp.stack(masks, axis=-1)

def block_forward(inputs, first_gain, first_shift, project_in, time_weight, bias_table, project_out, out_shift, second_gain, second_shift, up_weight, up_shift, down_weight, down_shift, time_block, bias_index):
    group = inputs.shape[0]
    reach = WIN // 2
    first = low(layer_norm(inputs, first_gain, first_shift))
    mixed = jnp.einsum('grcd,dke->grcke', first, project_in, precision=highest)
    time_proj = jnp.einsum('gd,dke->gke', low(time_block), time_weight, precision=highest)
    query = low_back(low(mixed[..., 0, :] + time_proj[:, None, None, 0, :]))
    keys = low_back(low(mixed[..., 1, :]))
    values = low_back(low(mixed[..., 2, :] + time_proj[:, None, None, 1, :]))
    padding = ((0, 0), (reach, reach), (reach, reach), (0, 0))
    key_padded = jnp.pad(keys, padding)
    value_padded = jnp.pad(values, padding)
    key_window = jnp.stack([key_padded[:, tap // WIN:tap // WIN + ROWS, tap % WIN:tap % WIN + COLS] for tap in range(WIN * WIN)], axis=3)
    value_window = jnp.stack([value_padded[:, tap // WIN:tap // WIN + ROWS, tap % WIN:tap % WIN + COLS] for tap in range(WIN * WIN)], axis=3)
    key_window = key_window.reshape(group, ROWS, COLS, WIN * WIN, HEADS, HD)
    value_window = value_window.reshape(group, ROWS, COLS, WIN * WIN, HEADS, HD)
    query_heads = query.reshape(group, ROWS, COLS, 1, HEADS, HD)
    scores = lax.optimization_barrier(jnp.sum(query_heads * key_window, axis=-1)) * HD ** (-0.5)
    tap_bias = bias_table[:, bias_index]
    scores = scores + jnp.transpose(tap_bias)[None, None, None]
    valid = window_valid(0, ROWS, COLS)
    scores = jnp.where(valid[None, :, :, :, None], scores, masked_score)
    top = lax.optimization_barrier(jnp.max(scores, axis=3, keepdims=True))
    weights = jnp.exp(scores - top)
    probs = weights / lax.optimization_barrier(jnp.sum(weights, axis=3, keepdims=True))
    attended = lax.optimization_barrier(jnp.sum(probs[..., None] * value_window, axis=3))
    attended = low(attended.reshape(group, ROWS, COLS, D))
    resid = inputs + low_back(jnp.einsum('grcd,de->grce', attended, project_out, precision=highest)) + out_shift
    second = low(layer_norm(resid, second_gain, second_shift))
    upper = low_back(jnp.einsum('grcd,df->grcf', second, up_weight, precision=highest)) + up_shift
    active = low(jax.nn.gelu(upper, approximate=True))
    return resid + low_back(jnp.einsum('grcf,fd->grcd', active, down_weight, precision=highest)) + down_shift

def reference(tokens, timesteps, first_gain, first_shift, project_in, time_weight, bias_table, bias_index, project_out, out_shift, second_gain, second_shift, up_weight, up_shift, down_weight, down_shift, cotangent):
    params = (first_gain.astype(jnp.float32), first_shift.astype(jnp.float32), project_in.astype(jnp.float32), time_weight.astype(jnp.float32), bias_table.astype(jnp.float32), project_out.astype(jnp.float32), out_shift.astype(jnp.float32), second_gain.astype(jnp.float32), second_shift.astype(jnp.float32), up_weight.astype(jnp.float32), up_shift.astype(jnp.float32), down_weight.astype(jnp.float32), down_shift.astype(jnp.float32))
    blocks = IMAGES // image_block
    time_all = time_features(timesteps, D).reshape(blocks, image_block, D)
    token_blocks = tokens.astype(jnp.float32).reshape(blocks, image_block, ROWS, COLS, D)
    cot_blocks = cotangent.astype(jnp.float32).reshape(blocks, image_block, ROWS, COLS, D)

    def step(totals, item):
        token_block, time_block, cot_block = item

        def forward_only(inputs, *weights):
            return block_forward(inputs, *weights, time_block, bias_index)
        result, pull = jax.vjp(forward_only, token_block, *params)
        grads = pull(cot_block)
        totals = tuple((left + right for left, right in zip(totals, grads[1:])))
        return (totals, (result.astype(jnp.bfloat16), grads[0]))
    zeros = tuple((jnp.zeros_like(item) for item in params))
    totals, (outputs, input_grads) = lax.scan(step, zeros, (token_blocks, time_all, cot_blocks))
    return (outputs.reshape(IMAGES, ROWS, COLS, D), input_grads.reshape(IMAGES, ROWS, COLS, D), totals[0], totals[1], totals[2], totals[3], totals[4], totals[5], totals[6], totals[7], totals[8], totals[9], totals[10], totals[11], totals[12])
```

```python
import functools
import math

import jax
import jax.numpy as jnp
from jax import lax
from jax.experimental import pallas as pl
from jax.experimental.pallas import tpu as pltpu
from jax.sharding import PartitionSpec as P

HD = 72
ROWS = 16
COLS = 16
WIN = 5
REACH = WIN // 2
TAPS = WIN * WIN
HALO = REACH * COLS
KEYS = 256

EPSILON = 1e-05
MASKED = -1000000000.0
HIGHEST = lax.Precision.HIGHEST
MESH = pl.DeviceIdType.MESH
BF16 = jnp.bfloat16
F32 = jnp.float32
GELU_A = math.sqrt(2.0 / math.pi)
GELU_B = 0.044715


def dot_nn(a, b):
    return lax.dot_general(a, b, (((1,), (0,)), ((), ())), preferred_element_type=F32)


def dot_nt(a, b):
    return lax.dot_general(a, b, (((1,), (1,)), ((), ())), preferred_element_type=F32)


def dot_tn(a, b):
    return lax.dot_general(a, b, (((0,), (0,)), ((), ())), preferred_element_type=F32)


def normed(values):
    center = values - jnp.mean(values, axis=-1, keepdims=True)
    inv = lax.rsqrt(jnp.mean(center * center, axis=-1, keepdims=True) + EPSILON)
    return center * inv, inv


def normed_back(unit, inv, gain, grad):
    unit_grad = grad * gain
    return inv * (
        unit_grad
        - jnp.mean(unit_grad, axis=-1, keepdims=True)
        - unit * jnp.mean(unit_grad * unit, axis=-1, keepdims=True)
    )


def gelu_pair(u):
    square = u * u
    t = jnp.tanh(GELU_A * u * (1.0 + GELU_B * square))
    half = 0.5 * (1.0 + t)
    slope = half + (0.5 * GELU_A) * u * (1.0 - t * t) * (1.0 + (3.0 * GELU_B) * square)
    return u * half, slope


def column_sum(values):
    return jnp.sum(values, axis=0, keepdims=True)


def head_window(head, width):
    first = head * HD // 128 * 128
    last = min(-(-(head + 1) * HD // 128) * 128, width)
    return first, last


def main_kernel(
    tokens,
    cotangent,
    time_low,
    first_gain,
    first_shift,
    out_shift,
    second_gain,
    second_shift,
    up_shift,
    down_shift,
    bias_table,
    bias_index,
    in_hbm,
    time_hbm,
    out_hbm,
    up_hbm,
    down_hbm,
    output,
    tokens_grad,
    first_low,
    second_low,
    active_low,
    upper_low,
    attended_low,
    resid_low,
    mixed_grad,
    small_sums,
    bias_grad,
    in_w,
    time_w,
    out_w,
    up_w,
    down_w,
    halo_tokens,
    rows_low,
    query,
    keys,
    values,
    prob,
    key_grad,
    value_grad,
    attended_grad,
    query_grad,
    attended,
    resid,
    part_own,
    part_other,
    down_own,
    down_other,
    second_own,
    second_other,
    first_own,
    first_other,
    halo_own,
    halo_other,
    bias_tiles,
    weight_sems,
    send_sems,
    recv_sems,
):
    count = tokens.shape[0]
    local = query.shape[1]
    heads = bias_table.shape[0]
    hidden = up_shift.shape[1]
    scale = HD ** (-0.5)
    image = lax.axis_index("img")
    band = lax.axis_index("band")
    head_half = lax.axis_index("head")
    sibling = (image, band, 1 - head_half)
    beside = (image, 1 - band, head_half)

    weight_copies = [
        pltpu.make_async_copy(src, dst, weight_sems.at[i])
        for i, (src, dst) in enumerate(
            (
                (in_hbm, in_w),
                (time_hbm, time_w),
                (out_hbm, out_w),
                (up_hbm, up_w),
                (down_hbm, down_w),
            )
        )
    ]
    for copy in weight_copies:
        copy.start()

    barrier = pltpu.get_barrier_semaphore()
    for other in (sibling, beside):
        pl.semaphore_signal(barrier, inc=1, device_id=other, device_id_type=MESH)
    pl.semaphore_wait(barrier, 2)

    def remote(index, source, target, device):
        return pltpu.make_async_remote_copy(
            src_ref=source,
            dst_ref=target,
            send_sem=send_sems.at[index],
            recv_sem=recv_sems.at[index],
            device_id=device,
            device_id_type=MESH,
        )

    edge = pl.multiple_of((1 - band) * (count - HALO), HALO)
    token_copy = remote(0, tokens.at[pl.ds(edge, HALO)], halo_tokens, beside)
    token_copy.start()

    gain_1 = first_gain[...]
    shift_1 = first_shift[...]
    unit, _ = normed(tokens[...].astype(F32))
    own_low = (unit * gain_1 + shift_1).astype(BF16)
    first_low[...] = own_low
    rows_low[pl.ds(0, count)] = own_low
    token_copy.wait()
    unit, _ = normed(halo_tokens[...].astype(F32))
    rows_low[pl.ds(count, HALO)] = (unit * gain_1 + shift_1).astype(BF16)

    weight_copies[1].wait()
    time_proj = dot_nt(jnp.broadcast_to(time_low[...], (8, time_low.shape[1])), time_w[...])[0:1]
    weight_copies[0].wait()
    rows = rows_low[...]
    query[...] = (dot_nt(rows[:count], in_w[0:local]) + time_proj[:, :local]).astype(BF16)
    halo_at = pl.multiple_of((1 - band) * (count + HALO), HALO)
    blank_at = pl.multiple_of(band * (count + HALO), HALO)
    zero_rows = jnp.zeros((HALO, local), BF16)
    zero_tail = jnp.zeros((KEYS - count - 2 * HALO, local), BF16)
    for kept, projected in (
        (keys, dot_nt(rows, in_w[local : 2 * local])),
        (values, dot_nt(rows, in_w[2 * local : 3 * local]) + time_proj[:, local:]),
    ):
        projected = projected.astype(BF16)
        kept[pl.ds(HALO, count)] = projected[:count]
        kept[pl.ds(halo_at, HALO)] = projected[count:]
        kept[pl.ds(blank_at, HALO)] = zero_rows
        kept[pl.ds(count + 2 * HALO, KEYS - count - 2 * HALO)] = zero_tail

    lane = lax.broadcasted_iota(jnp.int32, (COLS, 128), 1)
    row = lax.broadcasted_iota(jnp.int32, (COLS, 128), 0)
    col_step = lane % COLS - row
    row_step = lane // COLS
    inside = (col_step >= -REACH) & (col_step <= REACH) & (row_step < WIN)
    tap_of = jnp.where(inside, row_step * WIN + col_step + REACH, -1)
    key_lane = lax.broadcasted_iota(jnp.int32, (1, KEYS), 1)
    absent = jnp.where(key_lane < HALO, 1 - band, 0) + jnp.where(
        (key_lane >= count + HALO) & (key_lane < count + 2 * HALO), band, 0
    )
    absent = absent.astype(F32) * MASKED
    masked_half = jnp.full((COLS, 128), MASKED, F32)
    bands_here = count // COLS

    def in_head(head, shape):
        first, _ = head_window(head, local)
        at = lax.broadcasted_iota(jnp.int32, shape, 1) + first
        return (at >= head * HD) & (at < (head + 1) * HD)

    attended[...] = jnp.zeros(attended.shape, F32)
    for head in range(heads):
        first, last = head_window(head, local)
        width = last - first
        own = in_head(head, (count, width))
        tile = jnp.full((COLS, 128), MASKED, F32)
        for tap in range(TAPS):
            tile = jnp.where(tap_of == tap, bias_table[head, bias_index[tap]], tile)
        tile = jnp.concatenate([tile, masked_half], axis=1)
        bias = jnp.concatenate(
            [tile] + [pltpu.roll(tile, COLS * r, 1) for r in range(1, bands_here)], axis=0
        )
        queries = jnp.where(own, query[:, first:last], jnp.zeros((), BF16))
        scores = dot_nt(queries, keys[:, first:last]) * scale + (bias + absent)
        top = jnp.max(scores, axis=-1, keepdims=True)
        weights = jnp.exp(scores - top)
        weights = weights * (1.0 / jnp.sum(weights, axis=-1, keepdims=True))
        prob[head] = weights
        mixed = dot_nn(weights.astype(BF16), values[:, first:last])
        attended[:, first:last] += jnp.where(own, mixed, 0.0)

    low = attended[...].astype(BF16)
    attended_low[...] = low
    weight_copies[2].wait()
    part_own[...] = dot_nn(low, out_w[...])
    part_copy = remote(1, part_own, part_other, sibling)
    part_copy.start()
    part_copy.wait()
    after = tokens[...].astype(F32) + (part_own[...] + part_other[...]) + out_shift[...]
    resid[...] = after
    unit, _ = normed(after)
    low = (unit * second_gain[...] + second_shift[...]).astype(BF16)
    second_low[...] = low

    weight_copies[3].wait()
    weight_copies[4].wait()
    step = 768
    down_sum = None
    second_sum = None
    for at in range(0, hidden, step):
        piece = slice(at, at + step)
        upper = dot_nn(second_low[...], up_w[:, piece]) + up_shift[:, piece]
        active, slope = gelu_pair(upper)
        active = active.astype(BF16)
        active_low[:, piece] = active
        term = dot_nn(active, down_w[piece])
        down_sum = term if down_sum is None else down_sum + term
        grad = dot_nt(cotangent[...], down_w[piece]) * slope
        upper_sum = column_sum(grad)
        if at + step <= 1152:
            small_sums[6:7, at : at + step] = upper_sum
        elif at >= 1152:
            small_sums[7:8, at - 1152 : at + step - 1152] = upper_sum
        else:
            small_sums[6:7, at:1152] = upper_sum[:, : 1152 - at]
            small_sums[7:8, 0 : at + step - 1152] = upper_sum[:, 1152 - at :]
        grad = grad.astype(BF16)
        upper_low[:, piece] = grad
        term = dot_nt(grad, up_w[:, piece])
        second_sum = term if second_sum is None else second_sum + term
    second_own[...] = second_sum.astype(BF16)
    second_copy = remote(2, second_own, second_other, sibling)
    second_copy.start()
    down_own[...] = down_sum.astype(BF16)
    down_copy = remote(3, down_own, down_other, sibling)
    down_copy.start()
    cot = cotangent[...].astype(F32)
    small_sums[5:6] = column_sum(cot)
    second_copy.wait()
    back = second_own[...].astype(F32) + second_other[...].astype(F32)
    unit, inv = normed(resid[...])
    small_sums[3:4] = column_sum(back * unit)
    small_sums[4:5] = column_sum(back)
    grad = cot + normed_back(unit, inv, second_gain[...], back)
    tokens_grad[...] = grad
    small_sums[2:3] = column_sum(grad)
    low = grad.astype(BF16)
    resid_low[...] = low
    attended_grad[...] = dot_nt(low, out_w[...]).astype(BF16)

    query_grad[...] = jnp.zeros(query_grad.shape, F32)
    key_grad[...] = jnp.zeros(key_grad.shape, F32)
    value_grad[...] = jnp.zeros(value_grad.shape, F32)
    for head in range(heads):
        first, last = head_window(head, local)
        width = last - first
        own = in_head(head, (count, width))
        nothing = jnp.zeros((), BF16)
        queries = jnp.where(own, query[:, first:last], nothing)
        grads = jnp.where(own, attended_grad[:, first:last], nothing)
        weights = prob[head]
        prob_grad = dot_nt(grads, values[:, first:last])
        value_grad[:, first:last] += dot_tn(weights.astype(BF16), grads)
        product = weights * prob_grad
        score_grad = product - weights * jnp.sum(product, axis=-1, keepdims=True)
        tile = score_grad[0:COLS]
        for r in range(1, bands_here):
            tile = tile + pltpu.roll(score_grad[r * COLS : (r + 1) * COLS], KEYS - COLS * r, 1)
        bias_tiles[head] = tile[:, :128]
        low = (score_grad * scale).astype(BF16)
        query_grad[:, first:last] += jnp.where(own, dot_nn(low, keys[:, first:last]), 0.0)
        key_grad[:, first:last] += dot_tn(low, queries)

    halo_own[:, :local] = key_grad[pl.ds(halo_at, HALO)].astype(BF16)
    halo_own[:, local:] = value_grad[pl.ds(halo_at, HALO)].astype(BF16)
    halo_copy = remote(4, halo_own, halo_other, beside)
    halo_copy.start()

    low = query_grad[...].astype(BF16)
    mixed_grad[:, :local] = low
    small_sums[8:9, :local] = column_sum(low.astype(F32))
    out_lane = lax.broadcasted_iota(jnp.int32, (heads, 128), 1)
    table_grad = jnp.zeros((heads, 128), F32)
    for dc in range(WIN):
        diagonal = inside & (col_step == dc - REACH)
        sums = jnp.sum(jnp.where(diagonal[None], bias_tiles[...], 0.0), axis=1)
        for dr in range(WIN):
            group = (out_lane >= dr * COLS) & (out_lane < (dr + 1) * COLS)
            total = jnp.sum(jnp.where(group, sums, 0.0), axis=-1, keepdims=True)
            table_grad = jnp.where(out_lane == bias_index[dr * WIN + dc], total, table_grad)
    bias_grad[...] = table_grad
    down_copy.wait()
    lowered = down_own[...].astype(F32) + down_other[...].astype(F32)
    output[...] = (resid[...] + lowered + down_shift[...]).astype(BF16)

    halo_copy.wait()
    edge_at = pl.multiple_of(HALO + edge, HALO)
    arrived = halo_other[...].astype(F32)
    key_grad[pl.ds(edge_at, HALO)] += arrived[:, :local]
    value_grad[pl.ds(edge_at, HALO)] += arrived[:, local:]
    mixed_grad[:, local : 2 * local] = key_grad[pl.ds(HALO, count)].astype(BF16)
    low = value_grad[pl.ds(HALO, count)].astype(BF16)
    mixed_grad[:, 2 * local :] = low
    small_sums[8:9, local:] = column_sum(low.astype(F32))
    small_sums[9:10] = time_low[...].astype(F32)
    small_sums[10:16] = jnp.zeros((6, small_sums.shape[1]), F32)

    first_own[...] = dot_nn(mixed_grad[...], in_w[...]).astype(BF16)
    first_copy = remote(5, first_own, first_other, sibling)
    first_copy.start()
    unit, inv = normed(tokens[...].astype(F32))
    first_copy.wait()
    back = first_own[...].astype(F32) + first_other[...].astype(F32)
    small_sums[0:1] = column_sum(back * unit)
    small_sums[1:2] = column_sum(back)
    tokens_grad[...] += normed_back(unit, inv, first_gain[...], back)


def main_path(tokens, cotangent, time_low, vectors, bias_table, bias_index, weights):
    count, width = tokens.shape
    local = weights[2].shape[0]
    hidden = weights[3].shape[1]
    heads = bias_table.shape[0]
    vmem = pl.BlockSpec(memory_space=pltpu.VMEM)
    smem = pl.BlockSpec(memory_space=pltpu.SMEM)
    anywhere = pl.BlockSpec(memory_space=pl.ANY)
    struct = jax.ShapeDtypeStruct
    outs = (
        struct((count, width), BF16),
        struct((count, width), F32),
        struct((count, width), BF16),
        struct((count, width), BF16),
        struct((count, hidden), BF16),
        struct((count, hidden), BF16),
        struct((count, local), BF16),
        struct((count, width), BF16),
        struct((count, 3 * local), BF16),
        struct((16, width), F32),
        struct((heads, 128), F32),
    )
    scratch = [
        *[pltpu.VMEM(w.shape, BF16) for w in weights],
        pltpu.VMEM((HALO, width), BF16),
        pltpu.VMEM((count + HALO, width), BF16),
        pltpu.VMEM((count, local), BF16),
        pltpu.VMEM((KEYS, local), BF16),
        pltpu.VMEM((KEYS, local), BF16),
        pltpu.VMEM((heads, count, KEYS), F32),
        pltpu.VMEM((KEYS, local), F32),
        pltpu.VMEM((KEYS, local), F32),
        pltpu.VMEM((count, local), BF16),
        pltpu.VMEM((count, local), F32),
        pltpu.VMEM((count, local), F32),
        pltpu.VMEM((count, width), F32),
        pltpu.VMEM((count, width), F32),
        pltpu.VMEM((count, width), F32),
        *[pltpu.VMEM((count, width), BF16) for _ in range(6)],
        pltpu.VMEM((HALO, 2 * local), BF16),
        pltpu.VMEM((HALO, 2 * local), BF16),
        pltpu.VMEM((heads, COLS, 128), F32),
        pltpu.SemaphoreType.DMA((5,)),
        pltpu.SemaphoreType.DMA((6,)),
        pltpu.SemaphoreType.DMA((6,)),
    ]
    return pl.pallas_call(
        main_kernel,
        out_shape=outs,
        in_specs=[vmem] * 10 + [smem] * 2 + [anywhere] * 5,
        out_specs=[vmem] * len(outs),
        scratch_shapes=scratch,
        name="main_path",
        compiler_params=pltpu.CompilerParams(
            collective_id=0, has_side_effects=True, vmem_limit_bytes=60 * 1024 * 1024
        ),
    )(tokens, cotangent, time_low, *vectors, bias_table, bias_index, *weights)


def time_features(timesteps, width):
    half = width // 2
    freqs = jnp.exp(jnp.arange(half, dtype=F32) * (-math.log(10000.0) / half))
    angles = timesteps.astype(F32)[:, None] * freqs[None, :]
    return jnp.concatenate([jnp.cos(angles), jnp.sin(angles)], axis=1)


def on_device(
    tokens,
    timesteps,
    first_gain,
    first_shift,
    project_in,
    time_weight,
    bias_table,
    bias_index,
    project_out,
    out_shift,
    second_gain,
    second_shift,
    up_weight,
    up_shift,
    down_weight,
    down_shift,
    cotangent,
):
    batch, band_rows, columns, width = tokens.shape
    local = project_in.shape[2]
    count = batch * band_rows * columns
    assert batch == 1 and columns == COLS
    time_low = time_features(timesteps, width).astype(BF16)
    in_rows = jnp.transpose(project_in, (1, 2, 0)).reshape(3 * local, width)
    time_rows = jnp.transpose(time_weight, (1, 2, 0)).reshape(2 * local, width)
    vectors = [
        v[None, :]
        for v in (first_gain, first_shift, out_shift, second_gain, second_shift, up_shift, down_shift)
    ]
    (
        output,
        tokens_grad,
        first_low,
        second_low,
        active_low,
        upper_low,
        attended_low,
        resid_low,
        mixed_grad,
        small_sums,
        bias_grad,
    ) = main_path(
        tokens.reshape(count, width),
        cotangent.reshape(count, width),
        time_low,
        vectors,
        bias_table,
        bias_index,
        (in_rows, time_rows, project_out, up_weight, down_weight),
    )
    axes = ("img", "band")
    grads_in = dot_tn(first_low, mixed_grad)
    grads_out = dot_tn(resid_low, attended_low)
    grads_up = dot_tn(second_low, upper_low)
    grads_down = dot_tn(cotangent.reshape(count, width), active_low)
    shares = [
        lax.psum_scatter(g.astype(BF16), axes, scatter_dimension=0, tiled=True).astype(F32)
        for g in (grads_in, grads_out, grads_up, grads_down)
    ]
    times = lax.all_gather(small_sums[8:10], axes, axis=0)
    here = lax.axis_index(axes) * shares[0].shape[0]
    time_cut = lax.dynamic_slice_in_dim(times[:, 1], here, shares[0].shape[0], axis=1)
    time_share = jnp.einsum("nd,nk->dk", time_cut, times[:, 0], precision=HIGHEST)
    sums = lax.psum((small_sums[:8], bias_grad), axes)
    small, bias_total = sums
    rows = shares[0].shape[0]
    return (
        output.reshape(tokens.shape),
        tokens_grad.reshape(tokens.shape),
        small[0],
        small[1],
        shares[0].reshape(rows, 3, local),
        time_share.reshape(rows, 2, local),
        bias_total[:, :TAPS],
        jnp.transpose(shares[1]),
        small[2],
        small[3],
        small[4],
        shares[2],
        small[6:8].reshape(-1)[: up_shift.shape[0]],
        jnp.transpose(shares[3]),
        small[5],
    )


def solution(mesh):
    return jax.shard_map(
        on_device,
        mesh=mesh,
        in_specs=(
            P("img", "band", None, None),
            P("img"),
            P(),
            P(),
            P(None, None, "head"),
            P(None, None, "head"),
            P("head", None),
            P(),
            P("head", None),
            P(),
            P(),
            P(),
            P(None, "head"),
            P("head"),
            P("head", None),
            P(),
            P("img", "band", None, None),
        ),
        out_specs=(
            P("img", "band", None, None),
            P("img", "band", None, None),
            P(),
            P(),
            P(("img", "band"), None, "head"),
            P(("img", "band"), None, "head"),
            P("head", None),
            P("head", ("img", "band")),
            P(),
            P(),
            P(),
            P(("img", "band"), "head"),
            P("head"),
            P("head", ("img", "band")),
            P(),
        ),
        check_vma=False,
    )
```

```python
import functools
import math
import types

import jax
import jax.numpy as jnp
from jax import lax
from jax.experimental import pallas as pl
from jax.experimental.pallas import tpu as pltpu
from jax.sharding import PartitionSpec as P

HD = 72
ROWS = 16
COLS = 16
WIN = 5
REACH = WIN // 2
TAPS = WIN * WIN
HALO = REACH * COLS
KEYS = 256

EPSILON = 1e-05
MASKED = -1000000000.0
HIGHEST = lax.Precision.HIGHEST
MESH = pl.DeviceIdType.MESH
BF16 = jnp.bfloat16
F32 = jnp.float32
GELU_A = math.sqrt(2.0 / math.pi)
GELU_B = 0.044715


def dot_nn(a, b):
    return lax.dot_general(a, b, (((1,), (0,)), ((), ())), preferred_element_type=F32)


def dot_nt(a, b):
    return lax.dot_general(a, b, (((1,), (1,)), ((), ())), preferred_element_type=F32)


def dot_tn(a, b):
    return lax.dot_general(a, b, (((0,), (0,)), ((), ())), preferred_element_type=F32)


def normed(values):
    center = values - jnp.mean(values, axis=-1, keepdims=True)
    inv = lax.rsqrt(jnp.mean(center * center, axis=-1, keepdims=True) + EPSILON)
    return center * inv, inv


def normed_back(unit, inv, gain, grad):
    unit_grad = grad * gain
    return inv * (
        unit_grad
        - jnp.mean(unit_grad, axis=-1, keepdims=True)
        - unit * jnp.mean(unit_grad * unit, axis=-1, keepdims=True)
    )


def gelu_pair(u):
    square = u * u
    t = jnp.tanh(GELU_A * u * (1.0 + GELU_B * square))
    half = 0.5 * (1.0 + t)
    slope = half + (0.5 * GELU_A) * u * (1.0 - t * t) * (1.0 + (3.0 * GELU_B) * square)
    return u * half, slope


def column_sum(values):
    return jnp.sum(values, axis=0, keepdims=True)


def head_window(head, width):
    first = head * HD // 128 * 128
    last = min(-(-(head + 1) * HD // 128) * 128, width)
    return first, last


def layer_kernel(names, meshed, *refs):
    r = types.SimpleNamespace(**dict(zip(names, refs, strict=True)))
    count, width = r.tokens.shape
    local = r.query.shape[1]
    heads = r.bias_table.shape[0]
    hidden = r.up_shift.shape[1]
    scale = HD ** (-0.5)
    image = lax.axis_index("img")
    band = lax.axis_index("band")
    half = lax.axis_index("head")
    sibling = (image, band, 1 - half)
    beside = (image, 1 - band, half)
    peers = [sibling, beside]
    if meshed:
        x, z = image % 2, image // 2
        across = z * 2 + 1 - x
        near_z, far_z, third_z = z + 1 - 2 * (z % 2), 3 - z, (z + 2) % 4
        plane = [(across, band, half), beside, (across, 1 - band, half)]
        near, far, third = ((at * 2 + x, band, half) for at in (near_z, far_z, third_z))
        peers = [sibling, *plane, near, far, third]

    weight_copies = [
        pltpu.make_async_copy(source, target, r.weight_sems.at[i])
        for i, (source, target) in enumerate(
            (
                (r.time_hbm, r.time_w),
                (r.in_hbm, r.in_w),
                (r.out_hbm, r.out_w),
                (r.up_hbm, r.up_w),
                (r.down_hbm, r.down_w),
            )
        )
    ]
    for copy in weight_copies:
        copy.start()

    barrier = pltpu.get_barrier_semaphore()
    for other in peers:
        pl.semaphore_signal(barrier, inc=1, device_id=other, device_id_type=MESH)

    def remote(index, source, target, device):
        return pltpu.make_async_remote_copy(
            src_ref=source,
            dst_ref=target,
            send_sem=r.send_sems.at[index],
            recv_sem=r.recv_sems.at[index],
            device_id=device,
            device_id_type=MESH,
        )

    def started(copies):
        for copy in copies:
            copy.start()
        return copies

    def finish(copies):
        for copy in copies:
            copy.wait()

    def spread(index, source, slots):
        return started([remote(index + k, source, slots.at[k], plane[k]) for k in range(3)])

    def spread_rows(index, turned, slots):
        rows = turned.shape[0] // 4
        return started(
            [
                remote(
                    index + k - 1,
                    turned.at[pl.ds(k * rows, rows)],
                    slots.at[:, pl.ds(k * count, count)],
                    plane[k - 1],
                )
                for k in range(1, 4)
            ]
        )

    unit, _ = normed(r.tokens[...].astype(F32))
    own_low = (unit * r.first_gain[...] + r.first_shift[...]).astype(BF16)
    r.first_low[...] = own_low
    r.rows_low[pl.ds(0, count)] = own_low

    pl.semaphore_wait(barrier, len(peers))
    edge = pl.multiple_of((1 - band) * (count - HALO), HALO)
    token_copy = remote(0, r.tokens.at[pl.ds(edge, HALO)], r.halo_tokens, beside)
    token_copy.start()
    if meshed:
        cot_copies = spread(6, r.cotangent, r.cot_all)
        rows4 = width // 4
        owners = rows4 // 4
        place = lax.broadcasted_iota(jnp.int32, (rows4, width), 0)
        place = place + (rows4 - owners) * (place // owners)
        place = lax.broadcasted_iota(jnp.int32, (rows4, width), 1) - place
        for k, spot in enumerate(
            (
                2 * x + band,
                2 * (1 - x) + band,
                2 * x + 1 - band,
                2 * (1 - x) + 1 - band,
            )
        ):
            r.perm[k * rows4 : (k + 1) * rows4] = (place == owners * spot).astype(F32).astype(BF16)
        r.first_turned[...] = dot_nt(r.perm[...], own_low).astype(BF16)
        r.first_all[:, 0:count] = r.first_turned[0:rows4]
        first_copies = spread_rows(9, r.first_turned, r.first_all)

    weight_copies[0].wait()
    time_rows = jnp.broadcast_to(r.time_low[...], (8, width))
    time_proj = dot_nt(time_rows, r.time_w[...])[0:1]
    token_copy.wait()
    unit, _ = normed(r.halo_tokens[...].astype(F32))
    halo_low = (unit * r.first_gain[...] + r.first_shift[...]).astype(BF16)
    r.rows_low[pl.ds(count, HALO)] = halo_low
    weight_copies[1].wait()
    rows = r.rows_low[...]
    r.query[...] = (dot_nt(rows[:count], r.in_w[0:local]) + time_proj[:, :local]).astype(BF16)
    halo_at = pl.multiple_of((1 - band) * (count + HALO), HALO)
    blank_at = pl.multiple_of(band * (count + HALO), HALO)
    tail = KEYS - count - 2 * HALO
    for kept, projected in (
        (r.keys, dot_nt(rows, r.in_w[local : 2 * local])),
        (r.values, dot_nt(rows, r.in_w[2 * local : 3 * local]) + time_proj[:, local:]),
    ):
        projected = projected.astype(BF16)
        kept[pl.ds(HALO, count)] = projected[:count]
        kept[pl.ds(halo_at, HALO)] = projected[count:]
        kept[pl.ds(blank_at, HALO)] = jnp.zeros((HALO, local), BF16)
        kept[pl.ds(count + 2 * HALO, tail)] = jnp.zeros((tail, local), BF16)

    lane = lax.broadcasted_iota(jnp.int32, (COLS, 128), 1)
    row = lax.broadcasted_iota(jnp.int32, (COLS, 128), 0)
    col_step = lane % COLS - row
    row_step = lane // COLS
    inside = (col_step >= -REACH) & (col_step <= REACH) & (row_step < WIN)
    tap_of = jnp.where(inside, row_step * WIN + col_step + REACH, -1)
    key_lane = lax.broadcasted_iota(jnp.int32, (1, KEYS), 1)
    absent = jnp.where(key_lane < HALO, 1 - band, 0) + jnp.where(
        (key_lane >= count + HALO) & (key_lane < count + 2 * HALO), band, 0
    )
    absent = absent.astype(F32) * MASKED
    masked_half = jnp.full((COLS, 128), MASKED, F32)
    bands_here = count // COLS
    nothing = jnp.zeros((), BF16)

    def in_head(head, shape):
        first, _ = head_window(head, local)
        at = lax.broadcasted_iota(jnp.int32, shape, 1) + first
        return (at >= head * HD) & (at < (head + 1) * HD)

    r.attended[...] = jnp.zeros(r.attended.shape, F32)
    for head in range(heads):
        first, last = head_window(head, local)
        own = in_head(head, (count, last - first))
        tile = jnp.full((COLS, 128), MASKED, F32)
        for tap in range(TAPS):
            tile = jnp.where(tap_of == tap, r.bias_table[head, r.bias_index[tap]], tile)
        tile = jnp.concatenate([tile, masked_half], axis=1)
        bias = jnp.concatenate(
            [tile] + [pltpu.roll(tile, COLS * k, 1) for k in range(1, bands_here)], axis=0
        )
        queries = jnp.where(own, r.query[:, first:last], nothing)
        scores = dot_nt(queries, r.keys[:, first:last]) * scale + (bias + absent)
        top = jnp.max(scores, axis=-1, keepdims=True)
        weights = jnp.exp(scores - top)
        weights = weights * (1.0 / jnp.sum(weights, axis=-1, keepdims=True))
        r.prob[head] = weights
        mixed = dot_nn(weights.astype(BF16), r.values[:, first:last])
        r.attended[:, first:last] += jnp.where(own, mixed, 0.0)

    attended_low = r.attended_all.at[0] if meshed else r.attended_low
    attended_low[...] = r.attended[...].astype(BF16)
    weight_copies[2].wait()
    r.part_own[...] = dot_nn(attended_low[...], r.out_w[...])
    part_copy = remote(1, r.part_own, r.part_other, sibling)
    part_copy.start()
    if meshed:
        attended_copies = spread(12, r.attended_all.at[0], r.attended_all.at[pl.ds(1, 3)])
    part_copy.wait()
    after = r.tokens[...].astype(F32) + (r.part_own[...] + r.part_other[...]) + r.out_shift[...]
    r.resid[...] = after
    unit, _ = normed(after)
    r.second_low[...] = (unit * r.second_gain[...] + r.second_shift[...]).astype(BF16)
    if meshed:
        second_copies = spread(15, r.second_low, r.second_all)

    weight_copies[3].wait()
    weight_copies[4].wait()
    step = hidden // 3
    down_sum = None
    second_sum = None
    for at in range(0, hidden, step):
        piece = slice(at, at + step)
        upper = dot_nn(r.second_low[...], r.up_w[:, piece]) + r.up_shift[:, piece]
        active, slope = gelu_pair(upper)
        active = active.astype(BF16)
        r.active_low[:, piece] = active
        term = dot_nn(active, r.down_w[piece])
        down_sum = term if down_sum is None else down_sum + term
        grad = dot_nt(r.cotangent[...], r.down_w[piece]) * slope
        sums = column_sum(grad)
        for line in range(-(-hidden // width)):
            low_at, high_at = max(at, line * width), min(at + step, (line + 1) * width)
            if low_at < high_at:
                r.small_own[6 + line : 7 + line, low_at - line * width : high_at - line * width] = (
                    sums[:, low_at - at : high_at - at]
                )
        grad = grad.astype(BF16)
        r.upper_low[:, piece] = grad
        term = dot_nt(grad, r.up_w[:, piece])
        second_sum = term if second_sum is None else second_sum + term
    r.second_own[...] = second_sum.astype(BF16)
    second_copy = remote(2, r.second_own, r.second_other, sibling)
    second_copy.start()
    r.down_own[...] = down_sum.astype(BF16)
    down_copy = remote(3, r.down_own, r.down_other, sibling)
    down_copy.start()
    cot = r.cotangent[...].astype(F32)
    r.small_own[5:6] = column_sum(cot)
    second_copy.wait()
    back = r.second_own[...].astype(F32) + r.second_other[...].astype(F32)
    unit, inv = normed(r.resid[...])
    r.small_own[3:4] = column_sum(back * unit)
    r.small_own[4:5] = column_sum(back)
    grad = cot + normed_back(unit, inv, r.second_gain[...], back)
    r.tokens_grad[...] = grad
    r.small_own[2:3] = column_sum(grad)
    r.resid_low[...] = grad.astype(BF16)
    r.attended_grad[...] = dot_nt(r.resid_low[...], r.out_w[...]).astype(BF16)
    if meshed:
        r.resid_turned[...] = dot_nt(r.perm[...], r.resid_low[...]).astype(BF16)
        r.resid_all[:, 0:count] = r.resid_turned[0:rows4]
        resid_copies = spread_rows(18, r.resid_turned, r.resid_all)

    r.query_grad[...] = jnp.zeros(r.query_grad.shape, F32)
    r.key_grad[...] = jnp.zeros(r.key_grad.shape, F32)
    r.value_grad[...] = jnp.zeros(r.value_grad.shape, F32)
    for head in range(heads):
        first, last = head_window(head, local)
        own = in_head(head, (count, last - first))
        queries = jnp.where(own, r.query[:, first:last], nothing)
        grads = jnp.where(own, r.attended_grad[:, first:last], nothing)
        weights = r.prob[head]
        prob_grad = dot_nt(grads, r.values[:, first:last])
        r.value_grad[:, first:last] += dot_tn(weights.astype(BF16), grads)
        product = weights * prob_grad
        score_grad = product - weights * jnp.sum(product, axis=-1, keepdims=True)
        tile = score_grad[0:COLS]
        for k in range(1, bands_here):
            tile = tile + pltpu.roll(score_grad[k * COLS : (k + 1) * COLS], KEYS - COLS * k, 1)
        r.bias_tiles[head] = tile[:, :128]
        low = (score_grad * scale).astype(BF16)
        r.query_grad[:, first:last] += jnp.where(own, dot_nn(low, r.keys[:, first:last]), 0.0)
        r.key_grad[:, first:last] += dot_tn(low, queries)

    r.halo_own[:, :local] = r.key_grad[pl.ds(halo_at, HALO)].astype(BF16)
    r.halo_own[:, local:] = r.value_grad[pl.ds(halo_at, HALO)].astype(BF16)
    halo_copy = remote(4, r.halo_own, r.halo_other, beside)
    halo_copy.start()

    query_low = r.query_all.at[0] if meshed else r.query_low
    pair_low = r.pair_all.at[0] if meshed else r.pair_low
    low = r.query_grad[...].astype(BF16)
    query_low[...] = low
    if meshed:
        query_copies = spread(21, r.query_all.at[0], r.query_all.at[pl.ds(1, 3)])
    r.small_own[8:9, :local] = column_sum(low.astype(F32))
    out_lane = lax.broadcasted_iota(jnp.int32, (heads, 128), 1)
    table_grad = jnp.zeros((heads, 128), F32)
    for dc in range(WIN):
        diagonal = inside & (col_step == dc - REACH)
        sums = jnp.sum(jnp.where(diagonal[None], r.bias_tiles[...], 0.0), axis=1)
        for dr in range(WIN):
            group = (out_lane >= dr * COLS) & (out_lane < (dr + 1) * COLS)
            total = jnp.sum(jnp.where(group, sums, 0.0), axis=-1, keepdims=True)
            table_grad = jnp.where(out_lane == r.bias_index[dr * WIN + dc], total, table_grad)
    r.small_own[9:10] = r.time_low[...].astype(F32)
    r.small_own[10:16] = jnp.zeros((6, width), F32)
    for head in range(heads):
        r.small_own[10:11, head * 128 : (head + 1) * 128] = table_grad[head : head + 1]
    down_copy.wait()
    lowered = r.down_own[...].astype(F32) + r.down_other[...].astype(F32)
    r.output[...] = (r.resid[...] + lowered + r.down_shift[...]).astype(BF16)

    halo_copy.wait()
    edge_at = pl.multiple_of(HALO + edge, HALO)
    arrived = r.halo_other[...].astype(F32)
    r.key_grad[pl.ds(edge_at, HALO)] += arrived[:, :local]
    r.value_grad[pl.ds(edge_at, HALO)] += arrived[:, local:]
    pair_low[:, :local] = r.key_grad[pl.ds(HALO, count)].astype(BF16)
    low = r.value_grad[pl.ds(HALO, count)].astype(BF16)
    pair_low[:, local:] = low
    if meshed:
        pair_copies = spread(24, r.pair_all.at[0], r.pair_all.at[pl.ds(1, 3)])
    r.small_own[8:9, local:] = column_sum(low.astype(F32))

    first_sum = dot_nn(query_low[...], r.in_w[0:local])
    first_sum = first_sum + dot_nn(pair_low[...], r.in_w[local:])
    r.first_own[...] = first_sum.astype(BF16)
    first_copy = remote(5, r.first_own, r.first_other, sibling)
    first_copy.start()
    unit, inv = normed(r.tokens[...].astype(F32))
    first_copy.wait()
    back = r.first_own[...].astype(F32) + r.first_other[...].astype(F32)
    r.small_own[0:1] = column_sum(back * unit)
    r.small_own[1:2] = column_sum(back)
    r.tokens_grad[...] += normed_back(unit, inv, r.first_gain[...], back)
    if not meshed:
        return

    small_copies = spread(27, r.small_own, r.small_plane)
    select = r.perm[0:rows4]
    others = 3 * count
    finish(cot_copies)
    cot_others = r.cot_all[...].reshape(others, width)
    r.cot_turned[:, :count] = dot_nt(select, r.cotangent[...]).astype(BF16)
    r.cot_turned[:, count:] = dot_nt(select, cot_others).astype(BF16)
    finish(second_copies)
    second_others = r.second_all[...].reshape(others, width)
    r.second_turned[:, :count] = dot_nt(select, r.second_low[...]).astype(BF16)
    r.second_turned[:, count:] = dot_nt(select, second_others).astype(BF16)

    part = step // 2

    def wide_first(t):
        return [
            remote(36 + 4 * t, r.wide_a.at[t, near_z], r.wide_a_in.at[t, 0], near),
            remote(37 + 4 * t, r.wide_a.at[t, 3 - near_z], r.wide_a_in.at[t, 1], near),
            remote(38 + 4 * t, r.wide_b.at[t, far_z], r.wide_b_in.at[t, 0], far),
            remote(39 + 4 * t, r.wide_b.at[t, far_z + 1 - 2 * (far_z % 2)], r.wide_b_in.at[t, 1], far),
        ]

    def wide_piece(t, carry):
        piece = pl.ds(pl.multiple_of(t * step, step), step)
        upper = dot_nn(r.second_all[...].reshape(others, width), r.up_w[:, piece])
        active, slope = gelu_pair(upper + r.up_shift[:, piece])
        grad = dot_nt(r.cot_all[...].reshape(others, width), r.down_w[piece]) * slope
        down = dot_nn(r.cot_turned[:, :count], r.active_low[:, piece])
        down = down + dot_nn(r.cot_turned[:, count:], active.astype(BF16))
        up = dot_nn(r.second_turned[:, :count], r.upper_low[:, piece])
        up = up + dot_nn(r.second_turned[:, count:], grad.astype(BF16))
        for k in range(4):
            cut = slice(k * owners, (k + 1) * owners)
            both = jnp.concatenate([down[cut], up[cut]], axis=0).astype(BF16)
            r.wide_a[t, k] = both[:, :part]
            r.wide_b[t, k] = both[:, part:]
        started(wide_first(t))
        return carry

    lax.fori_loop(0, 3, wide_piece, 0)

    finish(small_copies)
    small_sum = r.small_own[...]
    for k in range(3):
        small_sum = small_sum + r.small_plane[k]
    same_image = r.small_own[8:9] + r.small_plane[1, 8:9]
    other_image = r.small_plane[0, 8:9] + r.small_plane[2, 8:9]
    r.small_z[...] = small_sum
    r.small_z[8:9] = same_image
    r.small_z[9:10] = other_image
    r.small_z[11:12] = r.small_own[9:10]
    r.small_z[12:13] = r.small_plane[0, 9:10]
    ring = (near, far, third)
    ring_copies = started([remote(30 + k, r.small_z, r.small_ring.at[k], ring[k]) for k in range(3)])

    def wide_second(t):
        return [
            remote(52 + 2 * t, r.wide_a_sum.at[t], r.wide_a_last.at[t], far),
            remote(53 + 2 * t, r.wide_b_sum.at[t], r.wide_b_last.at[t], near),
        ]

    def joined(left, right):
        return left.astype(F32) + right.astype(F32)

    for t in range(3):
        finish(wide_first(t))
        r.wide_a_sum[t] = joined(r.wide_a[t, far_z], r.wide_a_in[t, 1]).astype(BF16)
        r.wide_b_sum[t] = joined(r.wide_b[t, near_z], r.wide_b_in[t, 1]).astype(BF16)
        started(wide_second(t))

    tokens4 = 4 * count
    finish(first_copies)
    finish(resid_copies)
    finish(attended_copies)
    finish(query_copies)
    narrow = dot_nn(r.resid_all[...], r.attended_all[...].reshape(tokens4, local))
    for k in range(4):
        r.narrow_a[k, :, :local] = narrow[k * owners : (k + 1) * owners].astype(BF16)
    narrow = dot_nn(r.first_all[...], r.query_all[...].reshape(tokens4, local))
    for k in range(4):
        r.narrow_a[k, :, local:] = narrow[k * owners : (k + 1) * owners].astype(BF16)
    narrow_a = started(
        [
            remote(58, r.narrow_a.at[near_z], r.narrow_a_in.at[0], near),
            remote(59, r.narrow_a.at[3 - near_z], r.narrow_a_in.at[1], near),
        ]
    )
    finish(pair_copies)
    narrow = dot_nn(r.first_all[...], r.pair_all[...].reshape(tokens4, 2 * local))
    for k in range(4):
        r.narrow_b[k] = narrow[k * owners : (k + 1) * owners].astype(BF16)
    narrow_b = started(
        [
            remote(60, r.narrow_b.at[far_z], r.narrow_b_in.at[0], far),
            remote(61, r.narrow_b.at[far_z + 1 - 2 * (far_z % 2)], r.narrow_b_in.at[1], far),
        ]
    )

    finish(ring_copies)
    small_sum = r.small_z[...]
    for k in range(3):
        small_sum = small_sum + r.small_ring[k]
    r.small_sums[...] = small_sum
    time_lines = [r.small_z[11:13]] + [r.small_ring[k, 11:13] for k in range(3)]
    time_lines = jnp.concatenate(time_lines, axis=0).astype(BF16)
    r.time_turned[...] = dot_nt(select, time_lines)
    time_cut = r.time_turned[pl.ds(pl.multiple_of(z * owners, 8), owners)]
    time_share = jnp.zeros((owners, width), F32)
    for k in range(4):
        source = r.small_z if k == 0 else r.small_ring.at[k - 1]
        for line in range(2):
            column = time_cut[:, 2 * k + line : 2 * k + line + 1]
            time_share = time_share + column * source[8 + line : 9 + line]
    r.time_share[0] = time_share[:, :local]
    r.time_share[1] = time_share[:, local:]

    for t in range(3):
        finish(wide_second(t))
        left = joined(r.wide_a[t, z], r.wide_a_in[t, 0]) + r.wide_a_last[t].astype(F32)
        right = joined(r.wide_b[t, z], r.wide_b_in[t, 0]) + r.wide_b_last[t].astype(F32)
        for at, total in ((t * step, left), (t * step + part, right)):
            r.down_share[:, at : at + part] = total[:owners]
            r.up_share[:, at : at + part] = total[owners:]

    finish(narrow_a)
    r.narrow_a_sum[...] = joined(r.narrow_a[far_z], r.narrow_a_in[1]).astype(BF16)
    last_a = started([remote(62, r.narrow_a_sum, r.narrow_a_last, far)])
    finish(narrow_b)
    r.narrow_b_sum[...] = joined(r.narrow_b[near_z], r.narrow_b_in[1]).astype(BF16)
    last_b = started([remote(63, r.narrow_b_sum, r.narrow_b_last, near)])
    finish(last_a)
    total = joined(r.narrow_a[z], r.narrow_a_in[0]) + r.narrow_a_last[...].astype(F32)
    r.out_share[...] = total[:, :local]
    r.in_share[0] = total[:, local:]
    finish(last_b)
    total = joined(r.narrow_b[z], r.narrow_b_in[0]) + r.narrow_b_last[...].astype(F32)
    r.in_share[1] = total[:, :local]
    r.in_share[2] = total[:, local:]


def layer_call(meshed, inputs, smalls, weights):
    count, width = inputs["tokens"].shape
    local = weights["out_hbm"].shape[0]
    hidden = weights["up_hbm"].shape[1]
    heads = smalls["bias_table"].shape[0]
    tokens4, rows4 = 4 * count, width // 4
    owners, part = rows4 // 4, hidden // 6
    outs = {"output": ((count, width), BF16), "tokens_grad": ((count, width), F32)}
    kept = {
        "first_low": ((count, width), BF16),
        "second_low": ((count, width), BF16),
        "active_low": ((count, hidden), BF16),
        "upper_low": ((count, hidden), BF16),
        "resid_low": ((count, width), BF16),
        "small_own": ((16, width), F32),
    }
    scratch = {
        "time_w": ((2 * local, width), BF16),
        "in_w": ((3 * local, width), BF16),
        "out_w": ((local, width), BF16),
        "up_w": ((width, hidden), BF16),
        "down_w": ((hidden, width), BF16),
        "halo_tokens": ((HALO, width), BF16),
        "rows_low": ((count + HALO, width), BF16),
        "query": ((count, local), BF16),
        "keys": ((KEYS, local), BF16),
        "values": ((KEYS, local), BF16),
        "prob": ((heads, count, KEYS), F32),
        "key_grad": ((KEYS, local), F32),
        "value_grad": ((KEYS, local), F32),
        "attended_grad": ((count, local), BF16),
        "query_grad": ((count, local), F32),
        "attended": ((count, local), F32),
        "resid": ((count, width), F32),
        "part_own": ((count, width), F32),
        "part_other": ((count, width), F32),
        "halo_own": ((HALO, 2 * local), BF16),
        "halo_other": ((HALO, 2 * local), BF16),
        "bias_tiles": ((heads, COLS, 128), F32),
    }
    for name in ("down", "second", "first"):
        scratch[name + "_own"] = ((count, width), BF16)
        scratch[name + "_other"] = ((count, width), BF16)
    if meshed:
        outs |= {
            "small_sums": ((16, width), F32),
            "in_share": ((3, owners, local), F32),
            "time_share": ((2, owners, local), F32),
            "out_share": ((owners, local), F32),
            "up_share": ((owners, hidden), F32),
            "down_share": ((owners, hidden), F32),
        }
        scratch |= kept
        scratch |= {
            "cot_all": ((3, count, width), BF16),
            "second_all": ((3, count, width), BF16),
            "attended_all": ((4, count, local), BF16),
            "query_all": ((4, count, local), BF16),
            "pair_all": ((4, count, 2 * local), BF16),
            "perm": ((width, width), BF16),
            "first_turned": ((width, count), BF16),
            "resid_turned": ((width, count), BF16),
            "first_all": ((rows4, tokens4), BF16),
            "resid_all": ((rows4, tokens4), BF16),
            "cot_turned": ((rows4, tokens4), BF16),
            "second_turned": ((rows4, tokens4), BF16),
            "small_plane": ((3, 16, width), F32),
            "small_z": ((16, width), F32),
            "small_ring": ((3, 16, width), F32),
            "time_turned": ((rows4, 8), F32),
        }
        for name in ("wide_a", "wide_b"):
            scratch[name] = ((3, 4, 2 * owners, part), BF16)
            scratch[name + "_in"] = ((3, 2, 2 * owners, part), BF16)
            scratch[name + "_sum"] = ((3, 2 * owners, part), BF16)
            scratch[name + "_last"] = ((3, 2 * owners, part), BF16)
        for name in ("narrow_a", "narrow_b"):
            scratch[name] = ((4, owners, 2 * local), BF16)
            scratch[name + "_in"] = ((2, owners, 2 * local), BF16)
            scratch[name + "_sum"] = ((owners, 2 * local), BF16)
            scratch[name + "_last"] = ((owners, 2 * local), BF16)
    else:
        outs |= kept
        outs |= {
            "attended_low": ((count, local), BF16),
            "query_low": ((count, local), BF16),
            "pair_low": ((count, 2 * local), BF16),
        }
    links = 64 if meshed else 6
    sems = {"weight_sems": 5, "send_sems": links, "recv_sems": links}
    vmem = pl.BlockSpec(memory_space=pltpu.VMEM)
    smem = pl.BlockSpec(memory_space=pltpu.SMEM)
    anywhere = pl.BlockSpec(memory_space=pl.ANY)
    names = [*inputs, *smalls, *weights, *outs, *scratch, *sems]
    results = pl.pallas_call(
        functools.partial(layer_kernel, names, meshed),
        out_shape=[jax.ShapeDtypeStruct(*shape) for shape in outs.values()],
        in_specs=[vmem] * len(inputs) + [smem] * len(smalls) + [anywhere] * len(weights),
        out_specs=[vmem] * len(outs),
        scratch_shapes=[pltpu.VMEM(*shape) for shape in scratch.values()]
        + [pltpu.SemaphoreType.DMA((number,)) for number in sems.values()],
        name="layer",
        compiler_params=pltpu.CompilerParams(
            collective_id=0, has_side_effects=True, vmem_limit_bytes=61 * 1024 * 1024
        ),
    )(*inputs.values(), *smalls.values(), *weights.values())
    return types.SimpleNamespace(**dict(zip(outs, results, strict=True)))


def time_features(timesteps, width):
    half = width // 2
    freqs = jnp.exp(jnp.arange(half, dtype=F32) * (-math.log(10000.0) / half))
    angles = timesteps.astype(F32)[:, None] * freqs[None, :]
    return jnp.concatenate([jnp.cos(angles), jnp.sin(angles)], axis=1)


def on_device(
    tokens,
    timesteps,
    first_gain,
    first_shift,
    project_in,
    time_weight,
    bias_table,
    bias_index,
    project_out,
    out_shift,
    second_gain,
    second_shift,
    up_weight,
    up_shift,
    down_weight,
    down_shift,
    cotangent,
):
    batch, band_rows, columns, width = tokens.shape
    local = project_in.shape[2]
    count = batch * band_rows * columns
    assert batch == 1 and columns == COLS
    meshed = lax.axis_size("img") == 8 and lax.axis_size("band") == 2
    cot = cotangent.reshape(count, width)
    inputs = {
        "tokens": tokens.reshape(count, width),
        "cotangent": cot,
        "time_low": time_features(timesteps, width).astype(BF16),
        "first_gain": first_gain[None],
        "first_shift": first_shift[None],
        "out_shift": out_shift[None],
        "second_gain": second_gain[None],
        "second_shift": second_shift[None],
        "up_shift": up_shift[None],
        "down_shift": down_shift[None],
    }
    smalls = {"bias_table": bias_table, "bias_index": bias_index}
    weights = {
        "time_hbm": jnp.transpose(time_weight, (1, 2, 0)).reshape(2 * local, width),
        "in_hbm": jnp.transpose(project_in, (1, 2, 0)).reshape(3 * local, width),
        "out_hbm": project_out,
        "up_hbm": up_weight,
        "down_hbm": down_weight,
    }
    r = layer_call(meshed, inputs, smalls, weights)
    if meshed:
        in_share = jnp.transpose(r.in_share, (1, 0, 2))
        time_share = jnp.transpose(r.time_share, (1, 0, 2))
        out_share, up_share, down_share = r.out_share, r.up_share, r.down_share
        small = r.small_sums
    else:
        axes = ("img", "band")
        grads = (
            dot_tn(r.first_low, jnp.concatenate([r.query_low, r.pair_low], axis=1)),
            dot_tn(r.resid_low, r.attended_low),
            dot_tn(r.second_low, r.upper_low),
            dot_tn(cot, r.active_low),
        )
        in_share, out_share, up_share, down_share = [
            lax.psum_scatter(g.astype(BF16), axes, scatter_dimension=0, tiled=True).astype(F32)
            for g in grads
        ]
        rows = in_share.shape[0]
        in_share = in_share.reshape(rows, 3, local)
        times = lax.all_gather(r.small_own[8:10], axes, axis=0)
        here = lax.axis_index(axes) * rows
        time_cut = lax.dynamic_slice_in_dim(times[:, 1], here, rows, axis=1)
        time_share = jnp.einsum("nd,nk->dk", time_cut, times[:, 0], precision=HIGHEST)
        time_share = time_share.reshape(rows, 2, local)
        small = lax.psum(r.small_own, axes)
    heads = bias_table.shape[0]
    return (
        r.output.reshape(tokens.shape),
        r.tokens_grad.reshape(tokens.shape),
        small[0],
        small[1],
        in_share,
        time_share,
        small[10, : heads * 128].reshape(heads, 128)[:, :TAPS],
        jnp.transpose(out_share),
        small[2],
        small[3],
        small[4],
        up_share,
        small[6:8].reshape(-1)[: up_shift.shape[0]],
        jnp.transpose(down_share),
        small[5],
    )


def solution(mesh):
    return jax.shard_map(
        on_device,
        mesh=mesh,
        in_specs=(
            P("img", "band", None, None),
            P("img"),
            P(),
            P(),
            P(None, None, "head"),
            P(None, None, "head"),
            P("head", None),
            P(),
            P("head", None),
            P(),
            P(),
            P(),
            P(None, "head"),
            P("head"),
            P("head", None),
            P(),
            P("img", "band", None, None),
        ),
        out_specs=(
            P("img", "band", None, None),
            P("img", "band", None, None),
            P(),
            P(),
            P(("img", "band"), None, "head"),
            P(("img", "band"), None, "head"),
            P("head", None),
            P("head", ("img", "band")),
            P(),
            P(),
            P(),
            P(("img", "band"), "head"),
            P("head"),
            P("head", ("img", "band")),
            P(),
        ),
        check_vma=False,
    )
```

```python
import functools
import math
import types

import jax
import jax.numpy as jnp
from jax import lax
from jax.experimental import pallas as pl
from jax.experimental.pallas import tpu as pltpu
from jax.sharding import PartitionSpec as P

HD = 72
ROWS = 16
COLS = 16
WIN = 5
REACH = WIN // 2
TAPS = WIN * WIN
HALO = REACH * COLS
KEYS = 256

EPSILON = 1e-05
MASKED = -1000000000.0
HIGHEST = lax.Precision.HIGHEST
MESH = pl.DeviceIdType.MESH
BF16 = jnp.bfloat16
F32 = jnp.float32
GELU_A = math.sqrt(2.0 / math.pi)
GELU_B = 0.044715


def dot_nn(a, b):
    return lax.dot_general(a, b, (((1,), (0,)), ((), ())), preferred_element_type=F32)


def dot_nt(a, b):
    return lax.dot_general(a, b, (((1,), (1,)), ((), ())), preferred_element_type=F32)


def dot_tn(a, b):
    return lax.dot_general(a, b, (((0,), (0,)), ((), ())), preferred_element_type=F32)


def normed(values):
    center = values - jnp.mean(values, axis=-1, keepdims=True)
    inv = lax.rsqrt(jnp.mean(center * center, axis=-1, keepdims=True) + EPSILON)
    return center * inv, inv


def normed_back(unit, inv, gain, grad):
    unit_grad = grad * gain
    return inv * (
        unit_grad
        - jnp.mean(unit_grad, axis=-1, keepdims=True)
        - unit * jnp.mean(unit_grad * unit, axis=-1, keepdims=True)
    )


def gelu_pair(u):
    square = u * u
    t = jnp.tanh(GELU_A * u * (1.0 + GELU_B * square))
    half = 0.5 * (1.0 + t)
    slope = half + (0.5 * GELU_A) * u * (1.0 - t * t) * (1.0 + (3.0 * GELU_B) * square)
    return u * half, slope


def column_sum(values):
    return jnp.sum(values, axis=0, keepdims=True)


def line_of(vector, piece=slice(None)):
    return vector[piece][None, :]


def head_window(head, width):
    first = head * HD // 128 * 128
    last = min(-(-(head + 1) * HD // 128) * 128, width)
    return first, last


def layer_kernel(names, meshed, *refs):
    r = types.SimpleNamespace(**dict(zip(names, refs, strict=True)))
    count, width = r.tokens.shape
    local = r.query.shape[1]
    heads = r.bias_table.shape[0]
    hidden = r.up_shift.shape[0]
    scale = HD ** (-0.5)
    image = lax.axis_index("img")
    band = lax.axis_index("band")
    half = lax.axis_index("head")
    sibling = (image, band, 1 - half)
    beside = (image, 1 - band, half)
    peers = [sibling, beside]
    if meshed:
        x, z = image % 2, image // 2
        across = z * 2 + 1 - x
        plane = [(across, band, half), beside, (across, 1 - band, half)]
        spot = 2 * x + band
        spots = [2 * (1 - x) + band, 2 * x + 1 - band, 2 * (1 - x) + 1 - band]
        heights = [z + 1 - 2 * (z % 2), 3 - z, (z + 2) % 4]
        column = [(at * 2 + x, band, half) for at in heights]
        peers = [sibling, *plane, *column]

    weight_copies = [
        pltpu.make_async_copy(source, target, r.weight_sems.at[i])
        for i, (source, target) in enumerate(
            (
                (r.time_hbm, r.time_w),
                (r.in_hbm, r.in_w),
                (r.out_hbm, r.out_w),
                (r.up_hbm, r.up_w),
                (r.down_hbm, r.down_w),
            )
        )
    ]
    for copy in weight_copies:
        copy.start()

    barrier = pltpu.get_barrier_semaphore()
    for other in peers:
        pl.semaphore_signal(barrier, inc=1, device_id=other, device_id_type=MESH)

    used = [0]

    def links(number):
        used[0] += number
        return used[0] - number

    def remote(index, source, target, device):
        return pltpu.make_async_remote_copy(
            src_ref=source,
            dst_ref=target,
            send_sem=r.send_sems.at[index],
            recv_sem=r.recv_sems.at[index],
            device_id=device,
            device_id_type=MESH,
        )

    def started(copies):
        for copy in copies:
            copy.start()
        return copies

    def sent(source, target, device):
        return started([remote(links(1), source, target, device)])

    def finish(copies):
        for copy in copies:
            copy.wait()

    def spread(source, slots, group):
        base = links(3)
        return started([remote(base + k, source, slots.at[k], group[k]) for k in range(3)])

    def deal(source, lanes):
        base = links(3)
        return started(
            [
                remote(
                    base + k,
                    source.at[:, pl.ds(pl.multiple_of(spots[k] * 128, 128), 128)],
                    r.mixed_all.at[k + 1, :, pl.ds(lanes, 128)],
                    plane[k],
                )
                for k in range(3)
            ]
        )

    def column_first(name):
        part, arrived = getattr(r, name + "_part"), getattr(r, name + "_in")
        base = links(2)
        return started(
            [remote(base + k, part.at[heights[k]], arrived.at[k], column[0]) for k in range(2)]
        )

    def column_second(name):
        part, arrived = getattr(r, name + "_part"), getattr(r, name + "_in")
        summed = getattr(r, name + "_sum")
        summed[...] = joined(part[heights[2]], arrived[1]).astype(BF16)
        return sent(summed, getattr(r, name + "_last"), column[2])

    def column_total(name):
        part, arrived = getattr(r, name + "_part"), getattr(r, name + "_in")
        return joined(part[z], arrived[0]) + getattr(r, name + "_last")[...].astype(F32)

    def joined(left, right):
        return left.astype(F32) + right.astype(F32)

    def keep_part(name, values):
        part = getattr(r, name + "_part")
        part[...] = values.astype(BF16).reshape(part.shape)

    def hand_out(stage, slots):
        base = links(3)
        return started(
            [remote(base + k, stage.at[spots[k]], slots.at[spot], plane[k]) for k in range(3)]
        )

    if meshed:
        mine = pl.ds(pl.multiple_of(half * (count // 2), count // 2), count // 2)
        full = local // 128 * 128
        own_lanes = pl.ds(pl.multiple_of(spot * 128, 128), 128)

    def spread_half(source, slots, group):
        base = links(3)
        return started(
            [remote(base + k, source.at[mine], slots.at[k, mine], group[k]) for k in range(3)]
        )

    def pass_half(slots):
        return sent(slots.at[:, mine], slots.at[:, mine], sibling)

    unit, _ = normed(r.tokens[...].astype(F32))
    own_low = (unit * line_of(r.first_gain) + line_of(r.first_shift)).astype(BF16)
    r.first_low[...] = own_low

    pl.semaphore_wait(barrier, len(peers))
    edge = pl.multiple_of((1 - band) * (count - HALO), HALO)
    token_copy = sent(r.tokens.at[pl.ds(edge, HALO)], r.halo_tokens, beside)
    if meshed:
        cot_copies = spread_half(r.cotangent, r.cot_all, column)
        r.first_all[0] = own_low
        first_copies = spread_half(r.first_low, r.first_all.at[pl.ds(1, 3)], plane)
        rows4 = width // 4
        owners = rows4 // 4
        place = lax.broadcasted_iota(jnp.int32, (rows4, width), 1)
        place = place - lax.broadcasted_iota(jnp.int32, (rows4, width), 0)
        r.select[...] = (place == rows4 * z).astype(F32).astype(BF16)
    weight_copies[0].wait()
    time_rows = jnp.broadcast_to(r.time_low[...], (8, width))
    time_proj = dot_nt(time_rows, r.time_w[...])[0:1]
    halo_at = pl.multiple_of((1 - band) * (count + HALO), HALO)
    blank_at = pl.multiple_of(band * (count + HALO), HALO)
    tail = KEYS - count - 2 * HALO
    weight_copies[1].wait()
    r.query[...] = (dot_nt(own_low, r.in_w[0:local]) + time_proj[:, :local]).astype(BF16)
    r.keys[pl.ds(HALO, count)] = dot_nt(own_low, r.in_w[local : 2 * local]).astype(BF16)
    projected = dot_nt(own_low, r.in_w[2 * local : 3 * local]) + time_proj[:, local:]
    r.values[pl.ds(HALO, count)] = projected.astype(BF16)
    for kept in (r.keys, r.values):
        kept[pl.ds(blank_at, HALO)] = jnp.zeros((HALO, local), BF16)
        kept[pl.ds(count + 2 * HALO, tail)] = jnp.zeros((tail, local), BF16)
    finish(token_copy)
    unit, _ = normed(r.halo_tokens[...].astype(F32))
    halo_low = (unit * line_of(r.first_gain) + line_of(r.first_shift)).astype(BF16)
    r.keys[pl.ds(halo_at, HALO)] = dot_nt(halo_low, r.in_w[local : 2 * local]).astype(BF16)
    projected = dot_nt(halo_low, r.in_w[2 * local : 3 * local]) + time_proj[:, local:]
    r.values[pl.ds(halo_at, HALO)] = projected.astype(BF16)

    lane = lax.broadcasted_iota(jnp.int32, (COLS, 128), 1)
    row = lax.broadcasted_iota(jnp.int32, (COLS, 128), 0)
    col_step = lane % COLS - row
    row_step = lane // COLS
    inside = (col_step >= -REACH) & (col_step <= REACH) & (row_step < WIN)
    tap_of = jnp.where(inside, row_step * WIN + col_step + REACH, -1)
    key_lane = lax.broadcasted_iota(jnp.int32, (1, KEYS), 1)
    absent = jnp.where(key_lane < HALO, 1 - band, 0) + jnp.where(
        (key_lane >= count + HALO) & (key_lane < count + 2 * HALO), band, 0
    )
    absent = absent.astype(F32) * MASKED
    masked_half = jnp.full((COLS, 128), MASKED, F32)
    bands_here = count // COLS
    nothing = jnp.zeros((), BF16)

    def in_head(head, shape):
        first, _ = head_window(head, local)
        at = lax.broadcasted_iota(jnp.int32, shape, 1) + first
        return (at >= head * HD) & (at < (head + 1) * HD)

    r.attended[...] = jnp.zeros(r.attended.shape, F32)
    for head in range(heads):
        first, last = head_window(head, local)
        own = in_head(head, (count, last - first))
        tile = jnp.full((COLS, 128), MASKED, F32)
        for tap in range(TAPS):
            tile = jnp.where(tap_of == tap, r.bias_table[head, r.bias_index[tap]], tile)
        tile = jnp.concatenate([tile, masked_half], axis=1)
        bias = jnp.concatenate(
            [tile] + [pltpu.roll(tile, COLS * k, 1) for k in range(1, bands_here)], axis=0
        )
        queries = jnp.where(own, r.query[:, first:last], nothing)
        scores = dot_nt(queries, r.keys[:, first:last]) * scale + (bias + absent)
        top = jnp.max(scores, axis=-1, keepdims=True)
        weights = jnp.exp(scores - top)
        weights = weights * (1.0 / jnp.sum(weights, axis=-1, keepdims=True))
        r.prob[head] = weights
        mixed = dot_nn(weights.astype(BF16), r.values[:, first:last])
        r.attended[:, first:last] += jnp.where(own, mixed, 0.0)

    r.attended_low[...] = r.attended[...].astype(BF16)
    weight_copies[2].wait()
    r.part_own[...] = dot_nn(r.attended_low[...], r.out_w[...])
    part_copy = sent(r.part_own, r.part_other, sibling)
    if meshed:
        r.attended_all[0] = r.attended_low[...]
        attended_copies = spread(r.attended_low, r.attended_all.at[pl.ds(1, 3)], plane)
        r.rest[...] = jnp.zeros(r.rest.shape, BF16)
        r.back_stage[...] = jnp.zeros(r.back_stage.shape, BF16)
        r.small_half[6:8] = jnp.zeros((2, width), F32)
    finish(part_copy)
    after = r.tokens[...].astype(F32) + (r.part_own[...] + r.part_other[...]) + line_of(r.out_shift)
    r.resid[...] = after
    unit, _ = normed(after)
    r.second_low[...] = (unit * line_of(r.second_gain) + line_of(r.second_shift)).astype(BF16)
    if meshed:
        second_copies = spread_half(r.second_low, r.second_all, column)

    if meshed:
        finish(first_copies)
        first_copies = pass_half(r.first_all.at[pl.ds(1, 3)])
    weight_copies[3].wait()
    weight_copies[4].wait()
    step = hidden // 3
    down_sum = None
    second_sum = None
    for at in range(0, hidden, step):
        piece = slice(at, at + step)
        upper = dot_nn(r.second_low[...], r.up_w[:, piece]) + line_of(r.up_shift, piece)
        active, slope = gelu_pair(upper)
        active = active.astype(BF16)
        r.active_low[:, piece] = active
        term = dot_nn(active, r.down_w[piece])
        down_sum = term if down_sum is None else down_sum + term
        grad = dot_nt(r.cotangent[...], r.down_w[piece]) * slope
        sums = column_sum(grad)
        for line in range(-(-hidden // width)):
            low_at, high_at = max(at, line * width), min(at + step, (line + 1) * width)
            if low_at < high_at:
                r.small_own[6 + line : 7 + line, low_at - line * width : high_at - line * width] = (
                    sums[:, low_at - at : high_at - at]
                )
        grad = grad.astype(BF16)
        r.upper_low[:, piece] = grad
        term = dot_nt(grad, r.up_w[:, piece])
        second_sum = term if second_sum is None else second_sum + term
    r.second_own[...] = second_sum.astype(BF16)
    second_copy = sent(r.second_own, r.second_other, sibling)
    r.down_own[...] = down_sum.astype(BF16)
    down_copy = sent(r.down_own, r.down_other, sibling)
    if meshed:
        finish(cot_copies)
        cot_copies = pass_half(r.cot_all)
        finish(first_copies)
        r.first_flat[...] = jnp.transpose(r.first_all[...].reshape(4 * count, width))
    cot = r.cotangent[...].astype(F32)
    r.small_own[5:6] = column_sum(cot)
    finish(second_copy)
    back = r.second_own[...].astype(F32) + r.second_other[...].astype(F32)
    unit, inv = normed(r.resid[...])
    r.small_own[3:4] = column_sum(back * unit)
    r.small_own[4:5] = column_sum(back)
    grad = cot + normed_back(unit, inv, line_of(r.second_gain), back)
    r.tokens_grad[...] = grad
    r.small_own[2:3] = column_sum(grad)
    r.resid_low[...] = grad.astype(BF16)
    r.attended_grad[...] = dot_nt(r.resid_low[...], r.out_w[...]).astype(BF16)
    if meshed:
        r.resid_turned[...] = jnp.transpose(grad)
        for k, at in enumerate([spot] + spots):
            lines = [
                r.resid_turned[pl.ds(pl.multiple_of(line * rows4 + owners * at, 8), owners)]
                for line in range(4)
            ]
            r.resid_stage[k] = jnp.concatenate(lines, axis=0).astype(BF16)
        r.resid_all[:, 0:count] = r.resid_stage[0]
        base = links(3)
        resid_copies = started(
            [
                remote(
                    base + k,
                    r.resid_stage.at[k + 1],
                    r.resid_all.at[:, pl.ds((k + 1) * count, count)],
                    plane[k],
                )
                for k in range(3)
            ]
        )
    r.query_grad[...] = jnp.zeros(r.query_grad.shape, F32)
    r.key_grad[...] = jnp.zeros(r.key_grad.shape, F32)
    r.value_grad[...] = jnp.zeros(r.value_grad.shape, F32)
    for head in range(heads):
        first, last = head_window(head, local)
        own = in_head(head, (count, last - first))
        queries = jnp.where(own, r.query[:, first:last], nothing)
        grads = jnp.where(own, r.attended_grad[:, first:last], nothing)
        weights = r.prob[head]
        prob_grad = dot_nt(grads, r.values[:, first:last])
        r.value_grad[:, first:last] += dot_tn(weights.astype(BF16), grads)
        product = weights * prob_grad
        score_grad = product - weights * jnp.sum(product, axis=-1, keepdims=True)
        tile = score_grad[0:COLS]
        for k in range(1, bands_here):
            tile = tile + pltpu.roll(score_grad[k * COLS : (k + 1) * COLS], KEYS - COLS * k, 1)
        r.bias_tiles[head] = tile[:, :128]
        low = (score_grad * scale).astype(BF16)
        r.query_grad[:, first:last] += jnp.where(own, dot_nn(low, r.keys[:, first:last]), 0.0)
        r.key_grad[:, first:last] += dot_tn(low, queries)

    r.halo_own[:, :local] = r.key_grad[pl.ds(halo_at, HALO)].astype(BF16)
    r.halo_own[:, local:] = r.value_grad[pl.ds(halo_at, HALO)].astype(BF16)
    halo_copy = sent(r.halo_own, r.halo_other, beside)
    low = r.query_grad[...].astype(BF16)
    r.query_low[...] = low
    if meshed:
        r.mixed_all[0, :, 128:256] = r.query_low[:, own_lanes]
        query_copies = deal(r.query_low, 128)
        r.rest[1, :, : local - full] = low[:, full:]
    r.small_own[8:9, :local] = column_sum(low.astype(F32))
    out_lane = lax.broadcasted_iota(jnp.int32, (heads, 128), 1)
    table_grad = jnp.zeros((heads, 128), F32)
    for dc in range(WIN):
        diagonal = inside & (col_step == dc - REACH)
        sums = jnp.sum(jnp.where(diagonal[None], r.bias_tiles[...], 0.0), axis=1)
        for dr in range(WIN):
            group = (out_lane >= dr * COLS) & (out_lane < (dr + 1) * COLS)
            total = jnp.sum(jnp.where(group, sums, 0.0), axis=-1, keepdims=True)
            table_grad = jnp.where(out_lane == r.bias_index[dr * WIN + dc], total, table_grad)
    r.small_own[9:10] = r.time_low[...].astype(F32)
    r.small_own[10:16] = jnp.zeros((6, width), F32)
    for head in range(heads):
        r.small_own[10:11, head * 128 : (head + 1) * 128] = table_grad[head : head + 1]
    finish(down_copy)
    lowered = r.down_own[...].astype(F32) + r.down_other[...].astype(F32)
    r.output[...] = (r.resid[...] + lowered + line_of(r.down_shift)).astype(BF16)

    others = 3 * count
    if meshed:
        finish(cot_copies)
        cot_others = r.cot_all[...].reshape(others, width)
        r.cot_turned[:, :count] = dot_nt(r.select[...], r.cotangent[...]).astype(BF16)
        r.cot_turned[:, count:] = dot_nt(r.select[...], cot_others).astype(BF16)
    first_sum = dot_nn(r.query_low[...], r.in_w[0:local])
    unit, inv = normed(r.tokens[...].astype(F32))
    tokens4 = 4 * count
    if meshed:
        finish(attended_copies)
        finish(resid_copies)
        keep_part(
            "attended", dot_nn(r.resid_all[...], r.attended_all[...].reshape(tokens4, local))
        )
        attended_copies = column_first("attended")
    finish(halo_copy)
    edge_at = pl.multiple_of(HALO + edge, HALO)
    arrived = r.halo_other[...].astype(F32)
    r.key_grad[pl.ds(edge_at, HALO)] += arrived[:, :local]
    r.value_grad[pl.ds(edge_at, HALO)] += arrived[:, local:]
    low = r.key_grad[pl.ds(HALO, count)].astype(BF16)
    r.key_low[...] = low
    if meshed:
        r.mixed_all[0, :, 256:384] = r.key_low[:, own_lanes]
        key_copies = deal(r.key_low, 256)
        r.rest[2, :, : local - full] = low[:, full:]
    low = r.value_grad[pl.ds(HALO, count)].astype(BF16)
    r.value_low[...] = low
    if meshed:
        r.mixed_all[0, :, 384:512] = r.value_low[:, own_lanes]
        value_copies = deal(r.value_low, 384)
        r.rest[3, :, : local - full] = low[:, full:]
        r.mixed_all[0, :, 512:640] = r.rest[spot]
        base = links(3)
        rest_copies = started(
            [
                remote(
                    base + k,
                    r.rest.at[spots[k]],
                    r.mixed_all.at[k + 1, :, pl.ds(512, 128)],
                    plane[k],
                )
                for k in range(3)
            ]
        )
    r.small_own[8:9, local:] = column_sum(low.astype(F32))

    if meshed:
        finish(second_copies)
        second_copies = pass_half(r.second_all)
    first_sum = first_sum + dot_nn(r.key_low[...], r.in_w[local : 2 * local])
    first_sum = first_sum + dot_nn(r.value_low[...], r.in_w[2 * local :])
    r.first_own[...] = first_sum.astype(BF16)
    first_copy = sent(r.first_own, r.first_other, sibling)

    def mixed(start, stop):
        return r.mixed_all[:, :, start:stop].reshape(tokens4, stop - start)

    if meshed:
        finish(query_copies)
        keep_part("query", dot_nn(r.first_flat[...], mixed(128, 256)))
        query_copies = column_first("query")
    finish(first_copy)
    back = r.first_own[...].astype(F32) + r.first_other[...].astype(F32)
    r.small_own[0:1] = column_sum(back * unit)
    r.small_own[1:2] = column_sum(back)
    r.tokens_grad[...] += normed_back(unit, inv, line_of(r.first_gain), back)
    if not meshed:
        return

    r.small_send[0:3] = jnp.where(half == 0, r.small_own[0:3], r.small_own[3:6])
    r.small_send[3:5] = r.small_own[6:8]
    r.small_send[5:6] = r.small_own[10:11]
    r.small_send[6:8] = r.small_own[8:10]
    small_copies = spread(r.small_send, r.small_plane, plane)
    finish(second_copies)
    second_others = r.second_all[...].reshape(others, width)
    r.second_turned[:, :count] = dot_nt(r.select[...], r.second_low[...]).astype(BF16)
    r.second_turned[:, count:] = dot_nt(r.select[...], second_others).astype(BF16)

    finish(key_copies)
    finish(value_copies)
    keep_part("pair", dot_nn(r.first_flat[...], mixed(256, 512)))
    pair_copies = column_first("pair")

    part = step // 2
    near, far = plane[:2]

    def wide_first(t):
        base = links(4)
        return started(
            [
                remote(base, r.wide_a.at[t, spots[0]], r.wide_a_in.at[t, 0], near),
                remote(base + 1, r.wide_a.at[t, spots[2]], r.wide_a_in.at[t, 1], near),
                remote(base + 2, r.wide_b.at[t, spots[1]], r.wide_b_in.at[t, 0], far),
                remote(base + 3, r.wide_b.at[t, spots[2]], r.wide_b_in.at[t, 1], far),
            ]
        )

    def wide_piece(t):
        piece = slice(t * step, (t + 1) * step)
        upper = dot_nn(r.second_all[...].reshape(others, width), r.up_w[:, piece])
        active, slope = gelu_pair(upper + line_of(r.up_shift, piece))
        grad = dot_nt(r.cot_all[...].reshape(others, width), r.down_w[piece]) * slope
        down = dot_nn(r.cot_turned[:, :count], r.active_low[:, piece])
        down = down + dot_nn(r.cot_turned[:, count:], active.astype(BF16))
        up = dot_nn(r.second_turned[:, :count], r.upper_low[:, piece])
        up = up + dot_nn(r.second_turned[:, count:], grad.astype(BF16))
        for k in range(4):
            rows_here = slice(k * owners, (k + 1) * owners)
            both = jnp.concatenate([down[rows_here], up[rows_here]], axis=0).astype(BF16)
            r.wide_a[t, k] = both[:, :part]
            r.wide_b[t, k] = both[:, part:]
        return wide_first(t)

    def wide_second(t):
        finish(wide_copies[t])
        r.wide_a_sum[t] = joined(r.wide_a[t, spots[1]], r.wide_a_in[t, 1]).astype(BF16)
        r.wide_b_sum[t] = joined(r.wide_b[t, spots[0]], r.wide_b_in[t, 1]).astype(BF16)
        return sent(r.wide_a_sum.at[t], r.wide_a_last.at[t], far) + sent(
            r.wide_b_sum.at[t], r.wide_b_last.at[t], near
        )

    wide_copies = [wide_piece(0)]
    finish(rest_copies)
    term = dot_nn(r.first_flat[...], mixed(512, 640))
    for k in range(4):
        upper_half = term[k * rows4 : k * rows4 + rows4 // 2, : local - full]
        lower_half = term[k * rows4 + rows4 // 2 : (k + 1) * rows4, : local - full]
        r.rest_part[k] = jnp.concatenate([upper_half, lower_half], axis=1).astype(BF16)
    rest_copies = column_first("rest")
    finish(attended_copies)
    attended_copies = column_second("attended")
    finish(query_copies)
    query_copies = column_second("query")
    wide_copies.append(wide_piece(1))
    finish(small_copies)
    small_sum = r.small_send[0:6]
    for k in range(3):
        small_sum = small_sum + r.small_plane[k, 0:6]
    r.small_z[0:6] = small_sum
    r.small_z[6:7] = r.small_send[6:7] + r.small_plane[1, 6:7]
    r.small_z[7:8] = r.small_plane[0, 6:7] + r.small_plane[2, 6:7]
    r.small_z[8:9] = r.small_send[7:8]
    r.small_z[9:10] = r.small_plane[0, 7:8]
    column_copies = spread(r.small_z, r.small_column, column)
    wide_copies.append(wide_piece(2))
    finish(pair_copies)
    pair_copies = column_second("pair")
    finish(rest_copies)
    rest_copies = column_second("rest")
    last_copies = [wide_second(0)]
    last_copies.append(wide_second(1))
    finish(attended_copies)
    r.out_share[...] = column_total("attended")
    finish(query_copies)
    total = column_total("query")
    for k in range(4):
        r.back_stage[k, :, :128] = total[k * owners : (k + 1) * owners].astype(BF16)
    last_copies.append(wide_second(2))
    finish(pair_copies)
    total = column_total("pair")
    for k in range(4):
        r.back_stage[k, :, 128:384] = total[k * owners : (k + 1) * owners].astype(BF16)
    finish(rest_copies)
    total = column_total("rest")
    for k in range(4):
        lanes = slice(k // 2 * (local - full), (k // 2 + 1) * (local - full))
        rows_here = slice(k % 2 * owners, (k % 2 + 1) * owners)
        r.back_stage[k, :, 384 : 384 + local - full] = total[rows_here, lanes].astype(BF16)
    r.back_done[spot] = r.back_stage[spot]
    back_copies = hand_out(r.back_stage, r.back_done)
    finish(column_copies)
    small_sum = r.small_z[0:6]
    for k in range(3):
        small_sum = small_sum + r.small_column[k, 0:6]
    r.small_half[0:6] = small_sum
    small_copies = sent(r.small_half, r.small_other, sibling)
    time_lines = [r.small_z[8:10]] + [r.small_column[k, 8:10] for k in range(3)]
    time_lines = jnp.concatenate(time_lines, axis=0).astype(BF16)
    r.time_turned[...] = dot_nt(r.select[...], time_lines)
    time_cut = r.time_turned[pl.ds(pl.multiple_of(spot * owners, 8), owners)]
    time_share = jnp.zeros((owners, width), F32)
    for k in range(4):
        source = r.small_z if k == 0 else r.small_column.at[k - 1]
        for line in range(2):
            factor = time_cut[:, 2 * k + line : 2 * k + line + 1]
            time_share = time_share + factor * source[6 + line : 7 + line]
    r.time_share[0] = time_share[:, :local]
    r.time_share[1] = time_share[:, local:]

    def wide_total(t):
        finish(last_copies[t])
        left = joined(r.wide_a[t, spot], r.wide_a_in[t, 0]) + r.wide_a_last[t].astype(F32)
        right = joined(r.wide_b[t, spot], r.wide_b_in[t, 0]) + r.wide_b_last[t].astype(F32)
        for at, total in ((t * step, left), (t * step + part, right)):
            r.down_share[:, at : at + part] = total[:owners]
            r.up_share[:, at : at + part] = total[owners:]

    wide_total(0)
    wide_total(1)
    finish(small_copies)
    low_half, high_half = r.small_half[0:3], r.small_other[0:3]
    r.small_sums[0:3] = jnp.where(half == 0, low_half, high_half)
    r.small_sums[3:6] = jnp.where(half == 0, high_half, low_half)
    r.small_sums[6:8] = r.small_half[3:5]
    r.small_sums[8:16] = jnp.broadcast_to(r.small_half[5:6], (8, width))
    finish(back_copies)
    for k in range(4):
        piece = slice(k * 128, (k + 1) * 128)
        for line in range(3):
            lanes = slice(line * 128, (line + 1) * 128)
            r.in_share[line, :, piece] = r.back_done[k, :, lanes].astype(F32)
        if k > 0:
            rest = r.back_done[k, :, 384 : 384 + local - full].astype(F32)
            r.in_share[k - 1, :, full:] = rest
    wide_total(2)


def final_kernel(heads, names, *refs):
    r = types.SimpleNamespace(**dict(zip(names, refs, strict=True)))
    copies = [
        pltpu.make_async_copy(source, target, r.sems.at[i])
        for i, (source, target) in enumerate(
            (
                (r.output, r.output_done),
                (r.tokens_grad, r.tokens_done),
                (r.in_share, r.in_done),
                (r.out_share, r.out_done),
                (r.up_share, r.up_done),
                (r.down_share, r.down_done),
            )
        )
    ]
    for copy in copies:
        copy.start()
    width = r.small_sums.shape[1]
    for line, target in enumerate(
        (
            r.first_gain_done,
            r.first_shift_done,
            r.out_shift_done,
            r.second_gain_done,
            r.second_shift_done,
            r.down_shift_done,
        )
    ):
        target[...] = r.small_sums[line]
    for line in range(r.up_shift_done.shape[0] // width):
        r.up_shift_done[line * width : (line + 1) * width] = r.small_sums[6 + line]
    for head in range(heads):
        r.bias_done[head : head + 1] = r.small_sums[8:9, head * 128 : head * 128 + TAPS]
    local = r.time_share.shape[2]
    for k in range(2):
        r.time_done[:, k, :] = r.time_share[k]
    for copy in copies:
        copy.wait()


def final_call(results, heads, hidden):
    inputs = dict(
        output=results.output,
        tokens_grad=results.tokens_grad,
        in_share=results.in_share,
        out_share=results.out_share,
        up_share=results.up_share,
        down_share=results.down_share,
        small_sums=results.small_sums,
        time_share=results.time_share,
    )
    width = results.small_sums.shape[1]
    _, owners, local = results.time_share.shape
    struct = jax.ShapeDtypeStruct
    line = struct((width,), F32)
    outs = dict(
        output_done=struct(results.output.shape, BF16),
        tokens_done=struct(results.tokens_grad.shape, F32),
        in_done=struct(results.in_share.shape, F32),
        out_done=struct(results.out_share.shape, F32),
        up_done=struct(results.up_share.shape, F32),
        down_done=struct(results.down_share.shape, F32),
        first_gain_done=line,
        first_shift_done=line,
        out_shift_done=line,
        second_gain_done=line,
        second_shift_done=line,
        down_shift_done=line,
        up_shift_done=struct((hidden,), F32),
        bias_done=struct((heads, TAPS), F32),
        time_done=struct((owners, 2, local), F32),
    )
    vmem = pl.BlockSpec(memory_space=pltpu.VMEM)
    hbm = pl.BlockSpec(memory_space=pltpu.HBM)
    done = pl.pallas_call(
        functools.partial(final_kernel, heads, [*inputs, *outs, "sems"]),
        out_shape=list(outs.values()),
        in_specs=[vmem] * 8,
        out_specs=[hbm] * 6 + [vmem] * (len(outs) - 6),
        scratch_shapes=[pltpu.SemaphoreType.DMA((6,))],
        name="final",
        compiler_params=pltpu.CompilerParams(vmem_limit_bytes=61 * 1024 * 1024),
    )(*inputs.values())
    return types.SimpleNamespace(**dict(zip(outs, done, strict=True)))


def layer_call(meshed, inputs, smalls, weights):
    count, width = inputs["tokens"].shape
    local = weights["out_hbm"].shape[0]
    hidden = weights["up_hbm"].shape[1]
    heads = smalls["bias_table"].shape[0]
    tokens4, rows4 = 4 * count, width // 4
    owners, part = rows4 // 4, hidden // 6
    outs = dict(output=((count, width), BF16), tokens_grad=((count, width), F32))
    kept = dict(
        first_low=((count, width), BF16),
        second_low=((count, width), BF16),
        active_low=((count, hidden), BF16),
        upper_low=((count, hidden), BF16),
        resid_low=((count, width), BF16),
        attended_low=((count, local), BF16),
        query_low=((count, local), BF16),
        key_low=((count, local), BF16),
        value_low=((count, local), BF16),
        small_own=((16, width), F32),
    )
    scratch = dict(
        time_w=((2 * local, width), BF16),
        in_w=((3 * local, width), BF16),
        out_w=((local, width), BF16),
        up_w=((width, hidden), BF16),
        down_w=((hidden, width), BF16),
        halo_tokens=((HALO, width), BF16),
        query=((count, local), BF16),
        keys=((KEYS, local), BF16),
        values=((KEYS, local), BF16),
        prob=((heads, count, KEYS), F32),
        key_grad=((KEYS, local), F32),
        value_grad=((KEYS, local), F32),
        attended_grad=((count, local), BF16),
        query_grad=((count, local), F32),
        attended=((count, local), F32),
        resid=((count, width), F32),
        part_own=((count, width), F32),
        part_other=((count, width), F32),
        halo_own=((HALO, 2 * local), BF16),
        halo_other=((HALO, 2 * local), BF16),
        bias_tiles=((heads, COLS, 128), F32),
    )
    scratch |= dict(
        down_own=((count, width), BF16),
        down_other=((count, width), BF16),
        second_own=((count, width), BF16),
        second_other=((count, width), BF16),
        first_own=((count, width), BF16),
        first_other=((count, width), BF16),
    )
    if meshed:
        outs |= dict(
            small_sums=((16, width), F32),
            in_share=((3, owners, local), F32),
            time_share=((2, owners, local), F32),
            out_share=((owners, local), F32),
            up_share=((owners, hidden), F32),
            down_share=((owners, hidden), F32),
        )
        scratch |= kept
        scratch |= dict(
            cot_all=((3, count, width), BF16),
            second_all=((3, count, width), BF16),
            first_all=((4, count, width), BF16),
            first_flat=((width, tokens4), BF16),
            attended_all=((4, count, local), BF16),
            resid_turned=((width, count), F32),
            resid_stage=((4, rows4, count), BF16),
            resid_all=((rows4, tokens4), BF16),
            select=((rows4, width), BF16),
            cot_turned=((rows4, tokens4), BF16),
            second_turned=((rows4, tokens4), BF16),
            small_send=((8, width), F32),
            small_plane=((3, 8, width), F32),
            small_z=((10, width), F32),
            small_column=((3, 10, width), F32),
            small_half=((8, width), F32),
            small_other=((8, width), F32),
            time_turned=((rows4, 8), F32),
            mixed_all=((4, count, 640), BF16),
            rest=((4, count, 128), BF16),
            back_stage=((4, owners, 512), BF16),
            back_done=((4, owners, 512), BF16),
        )
        for name, rows, wide in (
            ("attended", owners, local),
            ("query", rows4, 128),
            ("pair", rows4, 256),
            ("rest", rows4 // 2, 128),
        ):
            scratch[name + "_part"] = ((4, rows, wide), BF16)
            scratch[name + "_in"] = ((2, rows, wide), BF16)
            scratch[name + "_sum"] = ((rows, wide), BF16)
            scratch[name + "_last"] = ((rows, wide), BF16)
        for name in ("wide_a", "wide_b"):
            scratch[name] = ((3, 4, 2 * owners, part), BF16)
            scratch[name + "_in"] = ((3, 2, 2 * owners, part), BF16)
            scratch[name + "_sum"] = ((3, 2 * owners, part), BF16)
            scratch[name + "_last"] = ((3, 2 * owners, part), BF16)
    else:
        outs |= kept
    links = 80 if meshed else 6
    sems = dict(weight_sems=5, send_sems=links, recv_sems=links)
    vmem = pl.BlockSpec(memory_space=pltpu.VMEM)
    smem = pl.BlockSpec(memory_space=pltpu.SMEM)
    anywhere = pl.BlockSpec(memory_space=pl.ANY)
    names = [*inputs, *smalls, *weights, *outs, *scratch, *sems]
    results = pl.pallas_call(
        functools.partial(layer_kernel, names, meshed),
        out_shape=[jax.ShapeDtypeStruct(*shape) for shape in outs.values()],
        in_specs=[vmem] * len(inputs) + [smem] * len(smalls) + [anywhere] * len(weights),
        out_specs=[vmem] * len(outs),
        scratch_shapes=[pltpu.VMEM(*shape) for shape in scratch.values()]
        + [pltpu.SemaphoreType.DMA((number,)) for number in sems.values()],
        name="layer",
        compiler_params=pltpu.CompilerParams(
            collective_id=0, has_side_effects=True, vmem_limit_bytes=61 * 1024 * 1024
        ),
    )(*inputs.values(), *smalls.values(), *weights.values())
    return types.SimpleNamespace(**dict(zip(outs, results, strict=True)))


def time_features(timesteps, width):
    half = width // 2
    freqs = jnp.exp(jnp.arange(half, dtype=F32) * (-math.log(10000.0) / half))
    angles = timesteps.astype(F32)[:, None] * freqs[None, :]
    return jnp.concatenate([jnp.cos(angles), jnp.sin(angles)], axis=1)


def on_device(
    tokens,
    timesteps,
    first_gain,
    first_shift,
    project_in,
    time_weight,
    bias_table,
    bias_index,
    project_out,
    out_shift,
    second_gain,
    second_shift,
    up_weight,
    up_shift,
    down_weight,
    down_shift,
    cotangent,
):
    batch, band_rows, columns, width = tokens.shape
    local = project_in.shape[2]
    count = batch * band_rows * columns
    assert batch == 1 and columns == COLS
    meshed = lax.axis_size("img") == 8 and lax.axis_size("band") == 2
    cot = cotangent.reshape(count, width)
    inputs = dict(
        tokens=tokens.reshape(count, width),
        cotangent=cot,
        time_low=time_features(timesteps, width).astype(BF16),
        first_gain=first_gain,
        first_shift=first_shift,
        out_shift=out_shift,
        second_gain=second_gain,
        second_shift=second_shift,
        up_shift=up_shift,
        down_shift=down_shift,
    )
    smalls = dict(bias_table=bias_table, bias_index=bias_index)
    weights = dict(
        time_hbm=jnp.transpose(time_weight, (1, 2, 0)).reshape(2 * local, width),
        in_hbm=jnp.transpose(project_in, (1, 2, 0)).reshape(3 * local, width),
        out_hbm=project_out,
        up_hbm=up_weight,
        down_hbm=down_weight,
    )
    r = layer_call(meshed, inputs, smalls, weights)
    heads = bias_table.shape[0]
    if meshed:
        f = final_call(r, heads, up_shift.shape[0])
        return (
            f.output_done.reshape(tokens.shape),
            f.tokens_done.reshape(tokens.shape),
            f.first_gain_done,
            f.first_shift_done,
            jnp.transpose(f.in_done, (1, 0, 2)),
            f.time_done,
            f.bias_done,
            jnp.transpose(f.out_done),
            f.out_shift_done,
            f.second_gain_done,
            f.second_shift_done,
            f.up_done,
            f.up_shift_done,
            jnp.transpose(f.down_done),
            f.down_shift_done,
        )
    axes = ("img", "band")
    grads = (
        dot_tn(r.first_low, jnp.concatenate([r.query_low, r.key_low, r.value_low], axis=1)),
        dot_tn(r.resid_low, r.attended_low),
        dot_tn(r.second_low, r.upper_low),
        dot_tn(cot, r.active_low),
    )
    in_share, out_share, up_share, down_share = [
        lax.psum_scatter(g.astype(BF16), axes, scatter_dimension=0, tiled=True).astype(F32)
        for g in grads
    ]
    rows = in_share.shape[0]
    in_share = in_share.reshape(rows, 3, local)
    times = lax.all_gather(r.small_own[8:10], axes, axis=0)
    here = lax.axis_index(axes) * rows
    time_cut = lax.dynamic_slice_in_dim(times[:, 1], here, rows, axis=1)
    time_share = jnp.einsum("nd,nk->dk", time_cut, times[:, 0], precision=HIGHEST)
    time_share = time_share.reshape(rows, 2, local)
    small = lax.psum(r.small_own, axes)
    return (
        r.output.reshape(tokens.shape),
        r.tokens_grad.reshape(tokens.shape),
        small[0],
        small[1],
        in_share,
        time_share,
        small[10, : heads * 128].reshape(heads, 128)[:, :TAPS],
        jnp.transpose(out_share),
        small[2],
        small[3],
        small[4],
        up_share,
        small[6:8].reshape(-1)[: up_shift.shape[0]],
        jnp.transpose(down_share),
        small[5],
    )


def solution(mesh):
    return jax.shard_map(
        on_device,
        mesh=mesh,
        in_specs=(
            P("img", "band", None, None),
            P("img"),
            P(),
            P(),
            P(None, None, "head"),
            P(None, None, "head"),
            P("head", None),
            P(),
            P("head", None),
            P(),
            P(),
            P(),
            P(None, "head"),
            P("head"),
            P("head", None),
            P(),
            P("img", "band", None, None),
        ),
        out_specs=(
            P("img", "band", None, None),
            P("img", "band", None, None),
            P(),
            P(),
            P(("img", "band"), None, "head"),
            P(("img", "band"), None, "head"),
            P("head", None),
            P("head", ("img", "band")),
            P(),
            P(),
            P(),
            P(("img", "band"), "head"),
            P("head"),
            P("head", ("img", "band")),
            P(),
        ),
        check_vma=False,
    )
```

```python
import functools
import math
import types

import jax
import jax.numpy as jnp
import numpy as np
from jax import lax
from jax.experimental import pallas as pl
from jax.experimental.pallas import tpu as pltpu
from jax.sharding import PartitionSpec as P

HD = 72
ROWS = 16
COLS = 16
WIN = 5
REACH = WIN // 2
TAPS = WIN * WIN
HALO = REACH * COLS
KEYS = 256

EPSILON = 1e-05
MASKED = -1000000000.0
HIGHEST = lax.Precision.HIGHEST
MESH = pl.DeviceIdType.MESH
BF16 = jnp.bfloat16
F32 = jnp.float32
GELU_A = math.sqrt(2.0 / math.pi)
GELU_B = 0.044715
TURN = (6.28125, 0.0019350051879882812, 3.019916e-07)


def dot_nn(a, b):
    return lax.dot_general(a, b, (((1,), (0,)), ((), ())), preferred_element_type=F32)


def dot_nt(a, b):
    return lax.dot_general(a, b, (((1,), (1,)), ((), ())), preferred_element_type=F32)


def dot_tn(a, b):
    return lax.dot_general(a, b, (((0,), (0,)), ((), ())), preferred_element_type=F32)


def normed(values):
    center = values - jnp.mean(values, axis=-1, keepdims=True)
    inv = lax.rsqrt(jnp.mean(center * center, axis=-1, keepdims=True) + EPSILON)
    return center * inv, inv


def normed_back(unit, inv, gain, grad):
    unit_grad = grad * gain
    return inv * (
        unit_grad
        - jnp.mean(unit_grad, axis=-1, keepdims=True)
        - unit * jnp.mean(unit_grad * unit, axis=-1, keepdims=True)
    )


def gelu_pair(u):
    square = u * u
    t = jnp.tanh(GELU_A * u * (1.0 + GELU_B * square))
    half = 0.5 * (1.0 + t)
    slope = half + (0.5 * GELU_A) * u * (1.0 - t * t) * (1.0 + (3.0 * GELU_B) * square)
    return u * half, slope


def column_sum(values):
    return jnp.sum(values, axis=0, keepdims=True)


def cos_sin(angle):
    turns = jnp.floor(angle * (0.5 / math.pi) + 0.5)
    rest = ((angle - turns * TURN[0]) - turns * TURN[1]) - turns * TURN[2]
    square = rest * rest
    cosine = jnp.full(angle.shape, 1.0 / math.factorial(18), F32)
    sine = jnp.full(angle.shape, 1.0 / math.factorial(19), F32)
    for power in range(16, -1, -2):
        cosine = 1.0 / math.factorial(power) - cosine * square
        sine = 1.0 / math.factorial(power + 1) - sine * square
    return cosine, sine * rest


def line_of(vector, piece=slice(None)):
    return vector[piece][None, :]


def head_window(head, width):
    first = head * HD // 128 * 128
    last = min(-(-(head + 1) * HD // 128) * 128, width)
    return first, last


def layer_kernel(names, inputs, small_names, weight_names, meshed, *refs):
    r = types.SimpleNamespace(**dict(zip(names, refs, strict=True)))
    count, width = r.tokens.shape
    local = r.query.shape[1]
    heads = r.bias_table.shape[0]
    hidden = r.up_shift.shape[0]
    scale = HD ** (-0.5)
    image = lax.axis_index("img")
    band = lax.axis_index("band")
    half = lax.axis_index("head")
    sibling = (image, band, 1 - half)
    beside = (image, 1 - band, half)
    peers = [sibling, beside]
    if meshed:
        x, z = image % 2, image // 2
        across = z * 2 + 1 - x
        plane = [(across, band, half), beside, (across, 1 - band, half)]
        spot = 2 * x + band
        spots = [2 * (1 - x) + band, 2 * x + 1 - band, 2 * (1 - x) + 1 - band]
        heights = [z + 1 - 2 * (z % 2), 3 - z, (z + 2) % 4]
        column = [(at * 2 + x, band, half) for at in heights]
        peers = [sibling, *plane, *column]

    loads = {}
    for name in (*inputs[:4], *small_names, *weight_names[:2], *inputs[4:], *weight_names[2:]):
        source, target = getattr(r, name + "_hbm"), getattr(r, name)
        loads[name] = pltpu.make_async_copy(source, target, r.load_sems.at[len(loads)])
        loads[name].start()

    def loaded(*wanted):
        for name in wanted:
            loads.pop(name).wait()

    barrier = pltpu.get_barrier_semaphore()
    for other in peers:
        pl.semaphore_signal(barrier, inc=1, device_id=other, device_id_type=MESH)

    used = [0]

    def links(number):
        used[0] += number
        assert used[0] <= r.send_sems.shape[0]
        return used[0] - number

    def remote(index, source, target, device):
        return pltpu.make_async_remote_copy(
            src_ref=source,
            dst_ref=target,
            send_sem=r.send_sems.at[index],
            recv_sem=r.recv_sems.at[index],
            device_id=device,
            device_id_type=MESH,
        )

    def started(copies):
        for copy in copies:
            copy.start()
        return copies

    def sent(source, target, device):
        return started([remote(links(1), source, target, device)])

    def finish(copies):
        for copy in copies:
            copy.wait()

    def spread(source, slots, group):
        base = links(3)
        return started([remote(base + k, source, slots.at[k], group[k]) for k in range(3)])

    def deal(source, lanes):
        base = links(3)
        return started(
            [
                remote(
                    base + k,
                    source.at[:, pl.ds(pl.multiple_of(spots[k] * 128, 128), 128)],
                    r.mixed_all.at[k + 1, :, pl.ds(lanes, 128)],
                    plane[k],
                )
                for k in range(3)
            ]
        )

    def column_first(name):
        part, arrived = getattr(r, name + "_part"), getattr(r, name + "_in")
        base = links(2)
        return started(
            [remote(base + k, part.at[heights[k]], arrived.at[k], column[0]) for k in range(2)]
        )

    def column_second(name):
        part, arrived = getattr(r, name + "_part"), getattr(r, name + "_in")
        summed = getattr(r, name + "_sum")
        summed[...] = joined(part[heights[2]], arrived[1]).astype(BF16)
        return sent(summed, getattr(r, name + "_last"), column[2])

    def column_total(name):
        part, arrived = getattr(r, name + "_part"), getattr(r, name + "_in")
        return joined(part[z], arrived[0]) + getattr(r, name + "_last")[...].astype(F32)

    def joined(left, right):
        return left.astype(F32) + right.astype(F32)

    def keep_part(name, values):
        part = getattr(r, name + "_part")
        part[...] = values.astype(BF16).reshape(part.shape)

    def hand_out(stage, slots):
        base = links(3)
        return started(
            [remote(base + k, stage.at[spots[k]], slots.at[spot], plane[k]) for k in range(3)]
        )

    if meshed:
        mine = pl.ds(pl.multiple_of(half * (count // 2), count // 2), count // 2)
        full = local // 128 * 128
        own_lanes = pl.ds(pl.multiple_of(spot * 128, 128), 128)

    def spread_half(source, slots, group):
        base = links(3)
        return started(
            [remote(base + k, source.at[mine], slots.at[k, mine], group[k]) for k in range(3)]
        )

    def pass_half(slots, slot, number):
        part = slots.at[pl.ds(slot, number), mine]
        return sent(part, part, sibling)

    loaded(*inputs[:3])
    unit, _ = normed(r.tokens[...].astype(F32))
    own_low = (unit * line_of(r.first_gain) + line_of(r.first_shift)).astype(BF16)
    r.first_low[...] = own_low

    loaded(inputs[3])
    angle = r.step_index[0].astype(F32) * line_of(r.frequencies)
    cosine, sine = cos_sin(angle)
    r.time_low[:, : width // 2] = cosine.astype(BF16)
    r.time_low[:, width // 2 :] = sine.astype(BF16)
    pl.semaphore_wait(barrier, len(peers))
    edge = pl.multiple_of((1 - band) * (count - HALO), HALO)
    token_copy = sent(r.tokens.at[pl.ds(edge, HALO)], r.halo_tokens, beside)
    loaded(inputs[4])
    if meshed:
        cot_copies = spread_half(r.cotangent, r.cot_all, column)
        r.first_all[0] = own_low
        first_copies = spread_half(r.first_low, r.first_all.at[pl.ds(1, 3)], plane)
        rows4 = width // 4
        owners = rows4 // 4
        place = lax.broadcasted_iota(jnp.int32, (rows4, width), 1)
        place = place - lax.broadcasted_iota(jnp.int32, (rows4, width), 0)
        r.select[...] = (place == rows4 * z).astype(F32).astype(BF16)
    loaded(weight_names[0])
    time_rows = jnp.broadcast_to(r.time_low[...], (8, width))
    time_proj = dot_nt(time_rows, r.time_w[...])[0:1]
    halo_at = pl.multiple_of((1 - band) * (count + HALO), HALO)
    blank_at = pl.multiple_of(band * (count + HALO), HALO)
    tail = KEYS - count - 2 * HALO
    loaded(weight_names[1])
    r.query[...] = (dot_nt(own_low, r.in_w[0:local]) + time_proj[:, :local]).astype(BF16)
    r.keys[pl.ds(HALO, count)] = dot_nt(own_low, r.in_w[local : 2 * local]).astype(BF16)
    projected = dot_nt(own_low, r.in_w[2 * local : 3 * local]) + time_proj[:, local:]
    r.values[pl.ds(HALO, count)] = projected.astype(BF16)
    for kept in (r.keys, r.values):
        kept[pl.ds(blank_at, HALO)] = jnp.zeros((HALO, local), BF16)
        kept[pl.ds(count + 2 * HALO, tail)] = jnp.zeros((tail, local), BF16)
    finish(token_copy)
    unit, _ = normed(r.halo_tokens[...].astype(F32))
    halo_low = (unit * line_of(r.first_gain) + line_of(r.first_shift)).astype(BF16)
    r.keys[pl.ds(halo_at, HALO)] = dot_nt(halo_low, r.in_w[local : 2 * local]).astype(BF16)
    projected = dot_nt(halo_low, r.in_w[2 * local : 3 * local]) + time_proj[:, local:]
    r.values[pl.ds(halo_at, HALO)] = projected.astype(BF16)

    loaded(*small_names)
    lane = lax.broadcasted_iota(jnp.int32, (COLS, 128), 1)
    row = lax.broadcasted_iota(jnp.int32, (COLS, 128), 0)
    col_step = lane % COLS - row
    row_step = lane // COLS
    inside = (col_step >= -REACH) & (col_step <= REACH) & (row_step < WIN)
    tap_of = jnp.where(inside, row_step * WIN + col_step + REACH, -1)
    key_lane = lax.broadcasted_iota(jnp.int32, (1, KEYS), 1)
    absent = jnp.where(key_lane < HALO, 1 - band, 0) + jnp.where(
        (key_lane >= count + HALO) & (key_lane < count + 2 * HALO), band, 0
    )
    absent = absent.astype(F32) * MASKED
    masked_half = jnp.full((COLS, 128), MASKED, F32)
    bands_here = count // COLS
    nothing = jnp.zeros((), BF16)

    def in_head(head, shape):
        first, _ = head_window(head, local)
        at = lax.broadcasted_iota(jnp.int32, shape, 1) + first
        return (at >= head * HD) & (at < (head + 1) * HD)

    r.attended[...] = jnp.zeros(r.attended.shape, F32)
    for head in range(heads):
        first, last = head_window(head, local)
        own = in_head(head, (count, last - first))
        tile = jnp.full((COLS, 128), MASKED, F32)
        for tap in range(TAPS):
            tile = jnp.where(tap_of == tap, r.bias_table[head, r.bias_index[tap]], tile)
        tile = jnp.concatenate([tile, masked_half], axis=1)
        bias = jnp.concatenate(
            [tile] + [pltpu.roll(tile, COLS * k, 1) for k in range(1, bands_here)], axis=0
        )
        queries = jnp.where(own, r.query[:, first:last], nothing)
        scores = dot_nt(queries, r.keys[:, first:last]) * scale + (bias + absent)
        top = jnp.max(scores, axis=-1, keepdims=True)
        weights = jnp.exp(scores - top)
        weights = weights * (1.0 / jnp.sum(weights, axis=-1, keepdims=True))
        r.prob[head] = weights
        mixed = dot_nn(weights.astype(BF16), r.values[:, first:last])
        r.attended[:, first:last] += jnp.where(own, mixed, 0.0)

    r.attended_low[...] = r.attended[...].astype(BF16)
    loaded(weight_names[2], *inputs[5:8])
    r.part_own[...] = dot_nn(r.attended_low[...], r.out_w[...])
    part_copy = sent(r.part_own, r.part_other, sibling)
    if meshed:
        r.attended_all[0] = r.attended_low[...]
        attended_copies = spread(r.attended_low, r.attended_all.at[pl.ds(1, 3)], plane)
        r.rest[...] = jnp.zeros(r.rest.shape, BF16)
        r.back_stage[...] = jnp.zeros(r.back_stage.shape, BF16)
        r.small_half[6:8] = jnp.zeros((2, width), F32)
    loaded(*weight_names[3:], *inputs[8:])
    r.active_grad[...] = dot_nt(r.cotangent[...], r.down_w[...])
    finish(part_copy)
    after = r.tokens[...].astype(F32) + (r.part_own[...] + r.part_other[...]) + line_of(r.out_shift)
    r.resid[...] = after
    unit, _ = normed(after)
    r.second_low[...] = (unit * line_of(r.second_gain) + line_of(r.second_shift)).astype(BF16)
    if meshed:
        second_copies = spread_half(r.second_low, r.second_all, column)

    if meshed:
        finish(first_copies)
        first_copies = pass_half(r.first_all, 1, 3)
    step = hidden // 3
    second_sum = None
    for at in range(0, hidden, step):
        piece = slice(at, at + step)
        upper = dot_nn(r.second_low[...], r.up_w[:, piece]) + line_of(r.up_shift, piece)
        active, slope = gelu_pair(upper)
        active = active.astype(BF16)
        r.active_low[0:count, piece] = active
        grad = r.active_grad[:, piece] * slope
        sums = column_sum(grad)
        for line in range(-(-hidden // width)):
            low_at, high_at = max(at, line * width), min(at + step, (line + 1) * width)
            if low_at < high_at:
                r.small_own[6 + line : 7 + line, low_at - line * width : high_at - line * width] = (
                    sums[:, low_at - at : high_at - at]
                )
        grad = grad.astype(BF16)
        r.upper_low[0:count, piece] = grad
        term = dot_nt(grad, r.up_w[:, piece])
        second_sum = term if second_sum is None else second_sum + term
    r.second_own[...] = second_sum.astype(BF16)
    second_copy = sent(r.second_own, r.second_other, sibling)
    r.down_own[...] = dot_nn(r.active_low[0:count], r.down_w[...]).astype(BF16)
    down_copy = sent(r.down_own, r.down_other, sibling)
    if meshed:
        finish(first_copies)
        r.first_flat[...] = jnp.transpose(r.first_all[...].reshape(4 * count, width))
    cot = r.cotangent[...].astype(F32)
    r.small_own[5:6] = column_sum(cot)
    finish(second_copy)
    back = r.second_own[...].astype(F32) + r.second_other[...].astype(F32)
    unit, inv = normed(r.resid[...])
    r.small_own[3:4] = column_sum(back * unit)
    r.small_own[4:5] = column_sum(back)
    grad = cot + normed_back(unit, inv, line_of(r.second_gain), back)
    r.tokens_grad[...] = grad
    r.small_own[2:3] = column_sum(grad)
    r.resid_low[...] = grad.astype(BF16)
    r.attended_grad[...] = dot_nt(r.resid_low[...], r.out_w[...]).astype(BF16)
    r.query_grad[...] = jnp.zeros(r.query_grad.shape, F32)
    r.key_grad[...] = jnp.zeros(r.key_grad.shape, F32)
    r.value_grad[...] = jnp.zeros(r.value_grad.shape, F32)
    for head in range(heads):
        first, last = head_window(head, local)
        own = in_head(head, (count, last - first))
        queries = jnp.where(own, r.query[:, first:last], nothing)
        grads = jnp.where(own, r.attended_grad[:, first:last], nothing)
        weights = r.prob[head]
        prob_grad = dot_nt(grads, r.values[:, first:last])
        r.value_grad[:, first:last] += dot_tn(weights.astype(BF16), grads)
        product = weights * prob_grad
        score_grad = product - weights * jnp.sum(product, axis=-1, keepdims=True)
        tile = score_grad[0:COLS]
        for k in range(1, bands_here):
            tile = tile + pltpu.roll(score_grad[k * COLS : (k + 1) * COLS], KEYS - COLS * k, 1)
        r.bias_tiles[head] = tile[:, :128]
        low = (score_grad * scale).astype(BF16)
        r.query_grad[:, first:last] += jnp.where(own, dot_nn(low, r.keys[:, first:last]), 0.0)
        r.key_grad[:, first:last] += dot_tn(low, queries)

    if meshed:
        finish(cot_copies[:1] + second_copies[:1])
        near_copies = pass_half(r.cot_all, 0, 1) + pass_half(r.second_all, 0, 1)
    r.halo_own[:, :local] = r.key_grad[pl.ds(halo_at, HALO)].astype(BF16)
    r.halo_own[:, local:] = r.value_grad[pl.ds(halo_at, HALO)].astype(BF16)
    halo_copy = sent(r.halo_own, r.halo_other, beside)
    low = r.query_grad[...].astype(BF16)
    r.query_low[...] = low
    if meshed:
        r.mixed_all[0, :, 128:256] = r.query_low[:, own_lanes]
        query_copies = deal(r.query_low, 128)
        r.rest[1, :, : local - full] = low[:, full:]
    r.small_own[8:9, :local] = column_sum(low.astype(F32))
    out_lane = lax.broadcasted_iota(jnp.int32, (heads, 128), 1)
    table_grad = jnp.zeros((heads, 128), F32)
    for dc in range(WIN):
        diagonal = inside & (col_step == dc - REACH)
        sums = jnp.sum(jnp.where(diagonal[None], r.bias_tiles[...], 0.0), axis=1)
        for dr in range(WIN):
            group = (out_lane >= dr * COLS) & (out_lane < (dr + 1) * COLS)
            total = jnp.sum(jnp.where(group, sums, 0.0), axis=-1, keepdims=True)
            table_grad = jnp.where(out_lane == r.bias_index[dr * WIN + dc], total, table_grad)
    r.small_own[9:10] = r.time_low[...].astype(F32)
    r.small_own[10:16] = jnp.zeros((6, width), F32)
    for head in range(heads):
        r.small_own[10:11, head * 128 : (head + 1) * 128] = table_grad[head : head + 1]
    finish(down_copy)
    lowered = r.down_own[...].astype(F32) + r.down_other[...].astype(F32)
    r.output[...] = (r.resid[...] + lowered + line_of(r.down_shift)).astype(BF16)

    if meshed:
        r.resid_turned[...] = jnp.transpose(r.tokens_grad[...])
        for k, at in enumerate([spot] + spots):
            lines = [
                r.resid_turned[pl.ds(pl.multiple_of(line * rows4 + owners * at, 8), owners)]
                for line in range(4)
            ]
            r.resid_stage[k] = jnp.concatenate(lines, axis=0).astype(BF16)
        r.resid_all[:, 0:count] = r.resid_stage[0]
        base = links(3)
        resid_copies = started(
            [
                remote(
                    base + k,
                    r.resid_stage.at[k + 1],
                    r.resid_all.at[:, pl.ds((k + 1) * count, count)],
                    plane[k],
                )
                for k in range(3)
            ]
        )
    first_sum = dot_nn(r.query_low[...], r.in_w[0:local])
    unit, inv = normed(r.tokens[...].astype(F32))
    tokens4 = 4 * count
    if meshed:
        finish(near_copies)

        def near_piece(t):
            piece = slice(t * step, (t + 1) * step)
            upper = dot_nn(r.second_all[0], r.up_w[:, piece]) + line_of(r.up_shift, piece)
            active, slope = gelu_pair(upper)
            r.active_low[count:, piece] = active.astype(BF16)
            grad = dot_nt(r.cot_all[0], r.down_w[piece]) * slope
            r.upper_low[count:, piece] = grad.astype(BF16)

        near_piece(0)
        near_piece(1)
    finish(halo_copy)
    if meshed:
        finish(cot_copies[1:])
        cot_copies = pass_half(r.cot_all, 1, 2)
    edge_at = pl.multiple_of(HALO + edge, HALO)
    arrived = r.halo_other[...].astype(F32)
    r.key_grad[pl.ds(edge_at, HALO)] += arrived[:, :local]
    r.value_grad[pl.ds(edge_at, HALO)] += arrived[:, local:]
    low = r.key_grad[pl.ds(HALO, count)].astype(BF16)
    r.key_low[...] = low
    if meshed:
        r.mixed_all[0, :, 256:384] = r.key_low[:, own_lanes]
        key_copies = deal(r.key_low, 256)
        r.rest[2, :, : local - full] = low[:, full:]
    low = r.value_grad[pl.ds(HALO, count)].astype(BF16)
    r.value_low[...] = low
    if meshed:
        r.mixed_all[0, :, 384:512] = r.value_low[:, own_lanes]
        value_copies = deal(r.value_low, 384)
        r.rest[3, :, : local - full] = low[:, full:]
        r.mixed_all[0, :, 512:640] = r.rest[spot]
        base = links(3)
        rest_copies = started(
            [
                remote(
                    base + k,
                    r.rest.at[spots[k]],
                    r.mixed_all.at[k + 1, :, pl.ds(512, 128)],
                    plane[k],
                )
                for k in range(3)
            ]
        )
    r.small_own[8:9, local:] = column_sum(low.astype(F32))

    first_sum = first_sum + dot_nn(r.key_low[...], r.in_w[local : 2 * local])
    first_sum = first_sum + dot_nn(r.value_low[...], r.in_w[2 * local :])
    r.first_own[...] = first_sum.astype(BF16)
    first_copy = sent(r.first_own, r.first_other, sibling)

    def mixed(start, stop):
        return r.mixed_all[:, :, start:stop].reshape(tokens4, stop - start)

    if meshed:
        finish(query_copies)
        keep_part("query", dot_nn(r.first_flat[...], mixed(128, 256)))
        query_copies = column_first("query")
    if meshed:
        finish(second_copies[1:])
        far_copies = pass_half(r.second_all, 1, 2)
    finish(first_copy)
    back = r.first_own[...].astype(F32) + r.first_other[...].astype(F32)
    r.small_own[0:1] = column_sum(back * unit)
    r.small_own[1:2] = column_sum(back)
    r.tokens_grad[...] += normed_back(unit, inv, line_of(r.first_gain), back)
    if not meshed:
        return

    part = step // 2
    near, far = plane[:2]

    def wide_first(t):
        base = links(4)
        return started(
            [
                remote(base, r.wide_a.at[t, spots[0]], r.wide_a_in.at[t, 0], near),
                remote(base + 1, r.wide_a.at[t, spots[2]], r.wide_a_in.at[t, 1], near),
                remote(base + 2, r.wide_b.at[t, spots[1]], r.wide_b_in.at[t, 0], far),
                remote(base + 3, r.wide_b.at[t, spots[2]], r.wide_b_in.at[t, 1], far),
            ]
        )

    def wide_piece(t):
        piece = slice(t * step, (t + 1) * step)
        upper = dot_nn(r.second_all[1:].reshape(2 * count, width), r.up_w[:, piece])
        active, slope = gelu_pair(upper + line_of(r.up_shift, piece))
        grad = dot_nt(r.cot_all[1:].reshape(2 * count, width), r.down_w[piece]) * slope
        down = dot_nn(r.cot_turned[:, : 2 * count], r.active_low[:, piece])
        down = down + dot_nn(r.cot_turned[:, 2 * count :], active.astype(BF16))
        up = dot_nn(r.second_turned[:, : 2 * count], r.upper_low[:, piece])
        up = up + dot_nn(r.second_turned[:, 2 * count :], grad.astype(BF16))
        for k in range(4):
            rows_here = slice(k * owners, (k + 1) * owners)
            both = jnp.concatenate([down[rows_here], up[rows_here]], axis=0).astype(BF16)
            r.wide_a[t, k] = both[:, :part]
            r.wide_b[t, k] = both[:, part:]
        return wide_first(t)

    def wide_second(t):
        finish(wide_copies[t])
        r.wide_a_sum[t] = joined(r.wide_a[t, spots[1]], r.wide_a_in[t, 1]).astype(BF16)
        r.wide_b_sum[t] = joined(r.wide_b[t, spots[0]], r.wide_b_in[t, 1]).astype(BF16)
        return sent(r.wide_a_sum.at[t], r.wide_a_last.at[t], far) + sent(
            r.wide_b_sum.at[t], r.wide_b_last.at[t], near
        )

    def wide_total(t):
        finish(last_copies[t])
        left = joined(r.wide_a[t, spot], r.wide_a_in[t, 0]) + r.wide_a_last[t].astype(F32)
        right = joined(r.wide_b[t, spot], r.wide_b_in[t, 0]) + r.wide_b_last[t].astype(F32)
        for at, total in ((t * step, left), (t * step + part, right)):
            r.down_share[:, at : at + part] = total[:owners]
            r.up_share[:, at : at + part] = total[owners:]

    r.small_send[0:3] = jnp.where(half == 0, r.small_own[0:3], r.small_own[3:6])
    r.small_send[3:5] = r.small_own[6:8]
    r.small_send[5:6] = r.small_own[10:11]
    r.small_send[6:8] = r.small_own[8:10]
    small_copies = spread(r.small_send, r.small_plane, plane)
    finish(cot_copies)
    others = 3 * count
    cot_others = r.cot_all[...].reshape(others, width)
    r.cot_turned[:, :count] = dot_nt(r.select[...], r.cotangent[...]).astype(BF16)
    r.cot_turned[:, count:] = dot_nt(r.select[...], cot_others).astype(BF16)
    near_piece(2)
    finish(key_copies)
    keep_part("key", dot_nn(r.first_flat[...], mixed(256, 384)))
    key_copies = column_first("key")
    finish(query_copies)
    query_copies = column_second("query")
    finish(far_copies)
    second_others = r.second_all[...].reshape(others, width)
    r.second_turned[:, :count] = dot_nt(r.select[...], r.second_low[...]).astype(BF16)
    r.second_turned[:, count:] = dot_nt(r.select[...], second_others).astype(BF16)
    wide_copies = [wide_piece(0)]
    finish(value_copies)
    keep_part("value", dot_nn(r.first_flat[...], mixed(384, 512)))
    value_copies = column_first("value")
    wide_copies.append(wide_piece(1))
    finish(rest_copies)
    term = dot_nn(r.first_flat[...], mixed(512, 640))
    for k in range(4):
        upper_half = term[k * rows4 : k * rows4 + rows4 // 2, : local - full]
        lower_half = term[k * rows4 + rows4 // 2 : (k + 1) * rows4, : local - full]
        r.rest_part[k] = jnp.concatenate([upper_half, lower_half], axis=1).astype(BF16)
    base = links(3)
    rest_copies = started(
        [remote(base + k, r.rest_part.at[heights[k]], r.rest_in.at[k], column[k]) for k in range(3)]
    )
    finish(key_copies)
    key_copies = column_second("key")
    finish(small_copies)
    small_sum = r.small_send[0:6]
    for k in range(3):
        small_sum = small_sum + r.small_plane[k, 0:6]
    r.small_z[0:6] = small_sum
    r.small_z[6:7] = r.small_send[6:7] + r.small_plane[1, 6:7]
    r.small_z[7:8] = r.small_plane[0, 6:7] + r.small_plane[2, 6:7]
    r.small_z[8:9] = r.small_send[7:8]
    r.small_z[9:10] = r.small_plane[0, 7:8]
    column_copies = spread(r.small_z, r.small_column, column)
    wide_copies.append(wide_piece(2))
    finish(value_copies)
    value_copies = column_second("value")
    finish(attended_copies)
    finish(resid_copies)
    keep_part("attended", dot_nn(r.resid_all[...], r.attended_all[...].reshape(tokens4, local)))
    attended_copies = column_first("attended")
    last_copies = [wide_second(0)]
    finish(query_copies)
    total = column_total("query")
    for k in range(4):
        r.front_stage[k] = total[k * owners : (k + 1) * owners].astype(BF16)
    r.front_done[spot] = r.front_stage[spot]
    front_copies = hand_out(r.front_stage, r.front_done)
    finish(rest_copies)
    total = joined(r.rest_part[z], r.rest_in[0]) + joined(r.rest_in[1], r.rest_in[2])
    for k in range(4):
        lanes = slice(k // 2 * (local - full), (k // 2 + 1) * (local - full))
        rows_here = slice(k % 2 * owners, (k % 2 + 1) * owners)
        r.back_stage[k, :, 256 : 256 + local - full] = total[rows_here, lanes].astype(BF16)
    last_copies.append(wide_second(1))
    finish(key_copies)
    total = column_total("key")
    for k in range(4):
        r.back_stage[k, :, :128] = total[k * owners : (k + 1) * owners].astype(BF16)
    last_copies.append(wide_second(2))
    finish(value_copies)
    total = column_total("value")
    for k in range(4):
        r.back_stage[k, :, 128:256] = total[k * owners : (k + 1) * owners].astype(BF16)
    r.back_done[spot] = r.back_stage[spot]
    back_copies = hand_out(r.back_stage, r.back_done)
    finish(attended_copies)
    attended_copies = column_second("attended")
    finish(column_copies)
    small_sum = r.small_z[0:6]
    for k in range(3):
        small_sum = small_sum + r.small_column[k, 0:6]
    r.small_half[0:6] = small_sum
    small_copies = sent(r.small_half, r.small_other, sibling)
    time_lines = [r.small_z[8:10]] + [r.small_column[k, 8:10] for k in range(3)]
    time_lines = jnp.concatenate(time_lines, axis=0).astype(BF16)
    r.time_turned[...] = dot_nt(r.select[...], time_lines)
    time_cut = r.time_turned[pl.ds(pl.multiple_of(spot * owners, 8), owners)]
    time_share = jnp.zeros((owners, width), F32)
    for k in range(4):
        source = r.small_z if k == 0 else r.small_column.at[k - 1]
        for line in range(2):
            factor = time_cut[:, 2 * k + line : 2 * k + line + 1]
            time_share = time_share + factor * source[6 + line : 7 + line]
    r.time_share[0] = time_share[:, :local]
    r.time_share[1] = time_share[:, local:]
    wide_total(0)
    wide_total(1)
    finish(small_copies)
    low_half, high_half = r.small_half[0:3], r.small_other[0:3]
    r.small_sums[0:3] = jnp.where(half == 0, low_half, high_half)
    r.small_sums[3:6] = jnp.where(half == 0, high_half, low_half)
    r.small_sums[6:8] = r.small_half[3:5]
    r.small_sums[8:16] = jnp.broadcast_to(r.small_half[5:6], (8, width))
    finish(front_copies)
    for k in range(4):
        r.in_share[0, :, k * 128 : (k + 1) * 128] = r.front_done[k].astype(F32)
    finish(attended_copies)
    r.out_share[...] = column_total("attended")
    wide_total(2)
    finish(back_copies)
    for k in range(4):
        for line in range(2):
            lanes = slice(line * 128, (line + 1) * 128)
            share = r.back_done[k, :, lanes].astype(F32)
            r.in_share[1 + line, :, k * 128 : (k + 1) * 128] = share
        if k > 0:
            rest = r.back_done[k, :, 256 : 256 + local - full].astype(F32)
            r.in_share[k - 1, :, full:] = rest


def final_kernel(heads, names, *refs):
    r = types.SimpleNamespace(**dict(zip(names, refs, strict=True)))
    copies = [
        pltpu.make_async_copy(source, target, r.sems.at[i])
        for i, (source, target) in enumerate(
            (
                (r.output, r.output_done),
                (r.tokens_grad, r.tokens_done),
                (r.in_share, r.in_done),
                (r.out_share, r.out_done),
                (r.up_share, r.up_done),
                (r.down_share, r.down_done),
            )
        )
    ]
    for copy in copies:
        copy.start()
    width = r.small_sums.shape[1]
    for line, target in enumerate(
        (
            r.first_gain_done,
            r.first_shift_done,
            r.out_shift_done,
            r.second_gain_done,
            r.second_shift_done,
            r.down_shift_done,
        )
    ):
        target[...] = r.small_sums[line]
    for line in range(r.up_shift_done.shape[0] // width):
        r.up_shift_done[line * width : (line + 1) * width] = r.small_sums[6 + line]
    for head in range(heads):
        r.bias_done[head : head + 1] = r.small_sums[8:9, head * 128 : head * 128 + TAPS]
    local = r.time_share.shape[2]
    for k in range(2):
        r.time_done[:, k, :] = r.time_share[k]
    for copy in copies:
        copy.wait()


def final_call(results, heads, hidden):
    inputs = dict(
        output=results.output,
        tokens_grad=results.tokens_grad,
        in_share=results.in_share,
        out_share=results.out_share,
        up_share=results.up_share,
        down_share=results.down_share,
        small_sums=results.small_sums,
        time_share=results.time_share,
    )
    width = results.small_sums.shape[1]
    _, owners, local = results.time_share.shape
    struct = jax.ShapeDtypeStruct
    line = struct((width,), F32)
    outs = dict(
        output_done=struct(results.output.shape, BF16),
        tokens_done=struct(results.tokens_grad.shape, F32),
        in_done=struct(results.in_share.shape, F32),
        out_done=struct(results.out_share.shape, F32),
        up_done=struct(results.up_share.shape, F32),
        down_done=struct(results.down_share.shape, F32),
        first_gain_done=line,
        first_shift_done=line,
        out_shift_done=line,
        second_gain_done=line,
        second_shift_done=line,
        down_shift_done=line,
        up_shift_done=struct((hidden,), F32),
        bias_done=struct((heads, TAPS), F32),
        time_done=struct((owners, 2, local), F32),
    )
    vmem = pl.BlockSpec(memory_space=pltpu.VMEM)
    hbm = pl.BlockSpec(memory_space=pltpu.HBM)
    done = pl.pallas_call(
        functools.partial(final_kernel, heads, [*inputs, *outs, "sems"]),
        out_shape=list(outs.values()),
        in_specs=[vmem] * 8,
        out_specs=[hbm] * 6 + [vmem] * (len(outs) - 6),
        scratch_shapes=[pltpu.SemaphoreType.DMA((6,))],
        name="final",
        compiler_params=pltpu.CompilerParams(vmem_limit_bytes=8 * 1024 * 1024),
    )(*inputs.values())
    return types.SimpleNamespace(**dict(zip(outs, done, strict=True)))


def layer_call(meshed, timesteps, inputs, smalls, weights):
    count, width = inputs["tokens"].shape
    local = weights["out_w"].shape[0]
    hidden = weights["up_w"].shape[1]
    heads = smalls["bias_table"].shape[0]
    tokens4, rows4 = 4 * count, width // 4
    owners, part = rows4 // 4, hidden // 6
    outs = dict(output=((count, width), BF16), tokens_grad=((count, width), F32))
    feed_rows = 2 * count if meshed else count
    kept = dict(
        first_low=((count, width), BF16),
        second_low=((count, width), BF16),
        active_low=((feed_rows, hidden), BF16),
        upper_low=((feed_rows, hidden), BF16),
        resid_low=((count, width), BF16),
        attended_low=((count, local), BF16),
        query_low=((count, local), BF16),
        key_low=((count, local), BF16),
        value_low=((count, local), BF16),
        small_own=((16, width), F32),
    )
    loads = inputs | weights
    scratch = {name: (array.shape, array.dtype) for name, array in loads.items()}
    scratch |= dict(
        time_low=((1, width), BF16),
        halo_tokens=((HALO, width), BF16),
        query=((count, local), BF16),
        keys=((KEYS, local), BF16),
        values=((KEYS, local), BF16),
        prob=((heads, count, KEYS), F32),
        key_grad=((KEYS, local), F32),
        value_grad=((KEYS, local), F32),
        attended_grad=((count, local), BF16),
        query_grad=((count, local), F32),
        attended=((count, local), F32),
        active_grad=((count, hidden), F32),
        resid=((count, width), F32),
        part_own=((count, width), F32),
        part_other=((count, width), F32),
        halo_own=((HALO, 2 * local), BF16),
        halo_other=((HALO, 2 * local), BF16),
        bias_tiles=((heads, COLS, 128), F32),
    )
    scratch |= dict(
        down_own=((count, width), BF16),
        down_other=((count, width), BF16),
        second_own=((count, width), BF16),
        second_other=((count, width), BF16),
        first_own=((count, width), BF16),
        first_other=((count, width), BF16),
    )
    if meshed:
        outs |= dict(
            small_sums=((16, width), F32),
            in_share=((3, owners, local), F32),
            time_share=((2, owners, local), F32),
            out_share=((owners, local), F32),
            up_share=((owners, hidden), F32),
            down_share=((owners, hidden), F32),
        )
        scratch |= kept
        scratch |= dict(
            cot_all=((3, count, width), BF16),
            second_all=((3, count, width), BF16),
            first_all=((4, count, width), BF16),
            first_flat=((width, tokens4), BF16),
            attended_all=((4, count, local), BF16),
            resid_turned=((width, count), F32),
            resid_stage=((4, rows4, count), BF16),
            resid_all=((rows4, tokens4), BF16),
            select=((rows4, width), BF16),
            cot_turned=((rows4, tokens4), BF16),
            second_turned=((rows4, tokens4), BF16),
            small_send=((8, width), F32),
            small_plane=((3, 8, width), F32),
            small_z=((10, width), F32),
            small_column=((3, 10, width), F32),
            small_half=((8, width), F32),
            small_other=((8, width), F32),
            time_turned=((rows4, 8), F32),
            mixed_all=((4, count, 640), BF16),
            rest=((4, count, 128), BF16),
            rest_part=((4, rows4 // 2, 128), BF16),
            rest_in=((3, rows4 // 2, 128), BF16),
            front_stage=((4, owners, 128), BF16),
            front_done=((4, owners, 128), BF16),
            back_stage=((4, owners, 384), BF16),
            back_done=((4, owners, 384), BF16),
        )
        for name, rows, wide in (
            ("attended", owners, local),
            ("query", rows4, 128),
            ("key", rows4, 128),
            ("value", rows4, 128),
        ):
            scratch[name + "_part"] = ((4, rows, wide), BF16)
            scratch[name + "_in"] = ((2, rows, wide), BF16)
            scratch[name + "_sum"] = ((rows, wide), BF16)
            scratch[name + "_last"] = ((rows, wide), BF16)
        for name in ("wide_a", "wide_b"):
            scratch[name] = ((3, 4, 2 * owners, part), BF16)
            scratch[name + "_in"] = ((3, 2, 2 * owners, part), BF16)
            scratch[name + "_sum"] = ((3, 2 * owners, part), BF16)
            scratch[name + "_last"] = ((3, 2 * owners, part), BF16)
    else:
        outs |= kept
    links = 96 if meshed else 6
    sems = dict(load_sems=len(loads | smalls), send_sems=links, recv_sems=links)
    vmem = pl.BlockSpec(memory_space=pltpu.VMEM)
    smem = pl.BlockSpec(memory_space=pltpu.SMEM)
    hbm = pl.BlockSpec(memory_space=pltpu.HBM)
    names = [name + "_hbm" for name in (*loads, *smalls)]
    names = ["step_index", *names, *outs, *smalls, *scratch, *sems]
    results = pl.pallas_call(
        functools.partial(layer_kernel, names, [*inputs], [*smalls], [*weights], meshed),
        out_shape=[jax.ShapeDtypeStruct(*shape) for shape in outs.values()],
        in_specs=[smem] + [hbm] * len(loads | smalls),
        out_specs=[vmem] * len(outs),
        scratch_shapes=[pltpu.SMEM(array.shape, array.dtype) for array in smalls.values()]
        + [pltpu.VMEM(*shape) for shape in scratch.values()]
        + [pltpu.SemaphoreType.DMA((number,)) for number in sems.values()],
        name="layer",
        compiler_params=pltpu.CompilerParams(
            collective_id=0, has_side_effects=True, vmem_limit_bytes=50 * 1024 * 1024
        ),
    )(
        timesteps,
        *[
            pltpu.with_memory_space_constraint(array, pltpu.HBM)
            for array in (loads | smalls).values()
        ],
    )
    return types.SimpleNamespace(**dict(zip(outs, results, strict=True)))


def on_device(
    tokens,
    timesteps,
    first_gain,
    first_shift,
    project_in,
    time_weight,
    bias_table,
    bias_index,
    project_out,
    out_shift,
    second_gain,
    second_shift,
    up_weight,
    up_shift,
    down_weight,
    down_shift,
    cotangent,
):
    batch, band_rows, columns, width = tokens.shape
    local = project_in.shape[2]
    count = batch * band_rows * columns
    assert batch == 1 and columns == COLS
    half = width // 2
    frequencies = np.exp(np.arange(half) * (-math.log(10000.0) / half)).astype(np.float32)
    meshed = lax.axis_size("img") == 8 and lax.axis_size("band") == 2
    cot = cotangent.reshape(count, width)
    inputs = dict(
        tokens=tokens.reshape(count, width),
        first_gain=first_gain,
        first_shift=first_shift,
        frequencies=jnp.asarray(frequencies),
        cotangent=cot,
        out_shift=out_shift,
        second_gain=second_gain,
        second_shift=second_shift,
        up_shift=up_shift,
        down_shift=down_shift,
    )
    smalls = dict(bias_table=bias_table, bias_index=bias_index)
    weights = dict(
        time_w=jnp.transpose(time_weight, (1, 2, 0)).reshape(2 * local, width),
        in_w=jnp.transpose(project_in, (1, 2, 0)).reshape(3 * local, width),
        out_w=project_out,
        up_w=up_weight,
        down_w=down_weight,
    )
    r = layer_call(meshed, timesteps, inputs, smalls, weights)
    heads = bias_table.shape[0]
    if meshed:
        f = final_call(r, heads, up_shift.shape[0])
        return (
            f.output_done.reshape(tokens.shape),
            f.tokens_done.reshape(tokens.shape),
            f.first_gain_done,
            f.first_shift_done,
            jnp.transpose(f.in_done, (1, 0, 2)),
            f.time_done,
            f.bias_done,
            jnp.transpose(f.out_done),
            f.out_shift_done,
            f.second_gain_done,
            f.second_shift_done,
            f.up_done,
            f.up_shift_done,
            jnp.transpose(f.down_done),
            f.down_shift_done,
        )
    axes = ("img", "band")
    grads = (
        dot_tn(r.first_low, jnp.concatenate([r.query_low, r.key_low, r.value_low], axis=1)),
        dot_tn(r.resid_low, r.attended_low),
        dot_tn(r.second_low, r.upper_low),
        dot_tn(cot, r.active_low),
    )
    in_share, out_share, up_share, down_share = [
        lax.psum_scatter(g.astype(BF16), axes, scatter_dimension=0, tiled=True).astype(F32)
        for g in grads
    ]
    rows = in_share.shape[0]
    in_share = in_share.reshape(rows, 3, local)
    times = lax.all_gather(r.small_own[8:10], axes, axis=0)
    here = lax.axis_index(axes) * rows
    time_cut = lax.dynamic_slice_in_dim(times[:, 1], here, rows, axis=1)
    time_share = jnp.einsum("nd,nk->dk", time_cut, times[:, 0], precision=HIGHEST)
    time_share = time_share.reshape(rows, 2, local)
    small = lax.psum(r.small_own, axes)
    return (
        r.output.reshape(tokens.shape),
        r.tokens_grad.reshape(tokens.shape),
        small[0],
        small[1],
        in_share,
        time_share,
        small[10, : heads * 128].reshape(heads, 128)[:, :TAPS],
        jnp.transpose(out_share),
        small[2],
        small[3],
        small[4],
        up_share,
        small[6:8].reshape(-1)[: up_shift.shape[0]],
        jnp.transpose(down_share),
        small[5],
    )


def solution(mesh):
    return jax.shard_map(
        on_device,
        mesh=mesh,
        in_specs=(
            P("img", "band", None, None),
            P("img"),
            P(),
            P(),
            P(None, None, "head"),
            P(None, None, "head"),
            P("head", None),
            P(),
            P("head", None),
            P(),
            P(),
            P(),
            P(None, "head"),
            P("head"),
            P("head", None),
            P(),
            P("img", "band", None, None),
        ),
        out_specs=(
            P("img", "band", None, None),
            P("img", "band", None, None),
            P(),
            P(),
            P(("img", "band"), None, "head"),
            P(("img", "band"), None, "head"),
            P("head", None),
            P("head", ("img", "band")),
            P(),
            P(),
            P(),
            P(("img", "band"), "head"),
            P("head"),
            P("head", ("img", "band")),
            P(),
        ),
        check_vma=False,
    )
```

```python
import functools
import math
import types

import jax
import jax.numpy as jnp
import numpy as np
from jax import lax
from jax.experimental import pallas as pl
from jax.experimental.pallas import tpu as pltpu
from jax.sharding import PartitionSpec as P

HD = 72
ROWS = 16
COLS = 16
WIN = 5
REACH = WIN // 2
TAPS = WIN * WIN
HALO = REACH * COLS
KEYS = 256

EPSILON = 1e-05
MASKED = -1000000000.0
HIGHEST = lax.Precision.HIGHEST
MESH = pl.DeviceIdType.MESH
BF16 = jnp.bfloat16
F32 = jnp.float32
GELU_A = math.sqrt(2.0 / math.pi)
GELU_B = 0.044715
MARK = 100
WIDE_TILES = (256, 512, 768, 512, 256)
TURN = (6.28125, 0.0019350051879882812, 3.019916e-07)


def dot_nn(a, b):
    return lax.dot_general(a, b, (((1,), (0,)), ((), ())), preferred_element_type=F32)


def dot_nt(a, b):
    return lax.dot_general(a, b, (((1,), (1,)), ((), ())), preferred_element_type=F32)


def dot_tn(a, b):
    return lax.dot_general(a, b, (((0,), (0,)), ((), ())), preferred_element_type=F32)


def normed(values):
    center = values - jnp.mean(values, axis=-1, keepdims=True)
    inv = lax.rsqrt(jnp.mean(center * center, axis=-1, keepdims=True) + EPSILON)
    return center * inv, inv


def normed_back(unit, inv, gain, grad):
    unit_grad = grad * gain
    return inv * (
        unit_grad
        - jnp.mean(unit_grad, axis=-1, keepdims=True)
        - unit * jnp.mean(unit_grad * unit, axis=-1, keepdims=True)
    )


def gelu_pair(u):
    square = u * u
    t = jnp.tanh(GELU_A * u * (1.0 + GELU_B * square))
    half = 0.5 * (1.0 + t)
    slope = half + (0.5 * GELU_A) * u * (1.0 - t * t) * (1.0 + (3.0 * GELU_B) * square)
    return u * half, slope


def column_sum(values):
    return jnp.sum(values, axis=0, keepdims=True)


def cos_sin(angle):
    turns = jnp.floor(angle * (0.5 / math.pi) + 0.5)
    rest = ((angle - turns * TURN[0]) - turns * TURN[1]) - turns * TURN[2]
    square = rest * rest
    cosine = jnp.full(angle.shape, 1.0 / math.factorial(18), F32)
    sine = jnp.full(angle.shape, 1.0 / math.factorial(19), F32)
    for power in range(16, -1, -2):
        cosine = 1.0 / math.factorial(power) - cosine * square
        sine = 1.0 / math.factorial(power + 1) - sine * square
    return cosine, sine * rest


def line_of(vector, piece=slice(None)):
    return vector[piece][None, :]


def head_window(head, width):
    first = head * HD // 128 * 128
    last = min(-(-(head + 1) * HD // 128) * 128, width)
    return first, last


def layer_kernel(names, inputs, small_names, weight_names, meshed, *refs):
    r = types.SimpleNamespace(**dict(zip(names, refs, strict=True)))
    count, width = r.tokens.shape
    local = r.query.shape[1]
    heads = r.bias_table.shape[0]
    hidden = r.up_shift.shape[0]
    scale = HD ** (-0.5)
    image = lax.axis_index("img")
    band = lax.axis_index("band")
    half = lax.axis_index("head")
    sibling = (image, band, 1 - half)
    beside = (image, 1 - band, half)
    peers = [sibling, beside]
    if meshed:
        x, z = image % 2, image // 2
        across = z * 2 + 1 - x
        plane = [(across, band, half), beside, (across, 1 - band, half)]
        spot = 2 * x + band
        spots = [2 * (1 - x) + band, 2 * x + 1 - band, 2 * (1 - x) + 1 - band]
        heights = [z + 1 - 2 * (z % 2), 3 - z, (z + 2) % 4]
        column = [(at * 2 + x, band, half) for at in heights]
        peers = [sibling, *plane, *column]

    loads = {}
    for name in (*inputs[:4], *small_names, *weight_names[:2], *inputs[4:], *weight_names[2:]):
        source, target = getattr(r, name + "_hbm"), getattr(r, name)
        loads[name] = pltpu.make_async_copy(source, target, r.load_sems.at[len(loads)])
        loads[name].start()

    def loaded(*wanted):
        for name in wanted:
            loads.pop(name).wait()

    barrier = pltpu.get_barrier_semaphore()
    for other in peers:
        pl.semaphore_signal(barrier, inc=1, device_id=other, device_id_type=MESH)

    used = [0]

    def links(number):
        used[0] += number
        assert used[0] <= r.send_sems.shape[0]
        return used[0] - number

    def remote(index, source, target, device):
        return pltpu.make_async_remote_copy(
            src_ref=source,
            dst_ref=target,
            send_sem=r.send_sems.at[index],
            recv_sem=r.recv_sems.at[index],
            device_id=device,
            device_id_type=MESH,
        )

    def started(copies):
        for copy in copies:
            copy.start()
        return copies

    def sent(source, target, device):
        return started([remote(links(1), source, target, device)])

    def finish(copies):
        for copy in copies:
            copy.wait()

    def spread(source, slots, group):
        base = links(3)
        return started([remote(base + k, source, slots.at[k], group[k]) for k in range(3)])

    def deal(source, lanes):
        base = links(3)
        return started(
            [
                remote(
                    base + k,
                    source.at[:, pl.ds(pl.multiple_of(spots[k] * 128, 128), 128)],
                    r.mixed_all.at[k + 1, :, pl.ds(lanes, 128)],
                    plane[k],
                )
                for k in range(3)
            ]
        )

    def column_first(name):
        part, arrived = getattr(r, name + "_part"), getattr(r, name + "_in")
        base = links(2)
        return started(
            [remote(base + k, part.at[heights[k]], arrived.at[k], column[0]) for k in range(2)]
        )

    def column_second(name):
        part, arrived = getattr(r, name + "_part"), getattr(r, name + "_in")
        summed = getattr(r, name + "_sum")
        summed[...] = joined(part[heights[2]], arrived[1]).astype(BF16)
        return sent(summed, getattr(r, name + "_last"), column[2])

    def column_total(name):
        part, arrived = getattr(r, name + "_part"), getattr(r, name + "_in")
        return joined(part[z], arrived[0]) + getattr(r, name + "_last")[...].astype(F32)

    def joined(left, right):
        return left.astype(F32) + right.astype(F32)

    def keep_part(name, values):
        part = getattr(r, name + "_part")
        part[...] = values.astype(BF16).reshape(part.shape)

    def hand_out(stage, slots):
        base = links(3)
        return started(
            [remote(base + k, stage.at[spots[k]], slots.at[spot], plane[k]) for k in range(3)]
        )

    if meshed:
        mine = pl.ds(pl.multiple_of(half * (count // 2), count // 2), count // 2)
        full = local // 128 * 128
        own_lanes = pl.ds(pl.multiple_of(spot * 128, 128), 128)

    def spread_half(source, slots, group):
        base = links(3)
        return started(
            [remote(base + k, source.at[mine], slots.at[k, mine], group[k]) for k in range(3)]
        )

    def pass_half(slots, slot, number):
        part = slots.at[pl.ds(slot, number), mine]
        return sent(part, part, sibling)

    loaded(*inputs[:3])
    unit, _ = normed(r.tokens[...].astype(F32))
    own_low = (unit * line_of(r.first_gain) + line_of(r.first_shift)).astype(BF16)
    r.first_low[...] = own_low

    loaded(inputs[3])
    angle = r.step_index[0].astype(F32) * line_of(r.frequencies)
    cosine, sine = cos_sin(angle)
    r.time_low[:, : width // 2] = cosine.astype(BF16)
    r.time_low[:, width // 2 :] = sine.astype(BF16)
    pl.semaphore_wait(barrier, len(peers))
    edge = pl.multiple_of((1 - band) * (count - HALO), HALO)
    token_copy = sent(r.tokens.at[pl.ds(edge, HALO)], r.halo_tokens, beside)
    loaded(inputs[4])
    if meshed:
        cot_copies = spread_half(r.cotangent, r.cot_all, column)
        r.first_all[0] = own_low
        first_copies = spread_half(r.first_low, r.first_all.at[pl.ds(1, 3)], plane)
        rows4 = width // 4
        owners = rows4 // 4
        cot_flat = r.time_w.at[:, pl.ds(0, 4 * count)]
        second_flat = r.time_w.at[:, pl.ds(4 * count, 4 * count)]
        own_rows = pl.ds(pl.multiple_of(z * rows4, 32), rows4)
    loaded(weight_names[0])
    time_rows = jnp.broadcast_to(r.time_low[...], (8, width))
    time_proj = dot_nt(time_rows, r.time_w[...])[0:1]
    halo_at = pl.multiple_of((1 - band) * (count + HALO), HALO)
    blank_at = pl.multiple_of(band * (count + HALO), HALO)
    tail = KEYS - count - 2 * HALO
    loaded(weight_names[1])
    r.query[...] = (dot_nt(own_low, r.in_w[0:local]) + time_proj[:, :local]).astype(BF16)
    r.keys[pl.ds(HALO, count)] = dot_nt(own_low, r.in_w[local : 2 * local]).astype(BF16)
    projected = dot_nt(own_low, r.in_w[2 * local : 3 * local]) + time_proj[:, local:]
    r.values[pl.ds(HALO, count)] = projected.astype(BF16)
    for kept in (r.keys, r.values):
        kept[pl.ds(blank_at, HALO)] = jnp.zeros((HALO, local), BF16)
        kept[pl.ds(count + 2 * HALO, tail)] = jnp.zeros((tail, local), BF16)
    finish(token_copy)
    unit, _ = normed(r.halo_tokens[...].astype(F32))
    halo_low = (unit * line_of(r.first_gain) + line_of(r.first_shift)).astype(BF16)
    r.keys[pl.ds(halo_at, HALO)] = dot_nt(halo_low, r.in_w[local : 2 * local]).astype(BF16)
    projected = dot_nt(halo_low, r.in_w[2 * local : 3 * local]) + time_proj[:, local:]
    r.values[pl.ds(halo_at, HALO)] = projected.astype(BF16)

    loaded(*small_names)
    lane = lax.broadcasted_iota(jnp.int32, (COLS, 128), 1)
    row = lax.broadcasted_iota(jnp.int32, (COLS, 128), 0)
    col_step = lane % COLS - row
    row_step = lane // COLS
    inside = (col_step >= -REACH) & (col_step <= REACH) & (row_step < WIN)
    tap_of = jnp.where(inside, row_step * WIN + col_step + REACH, -1)
    key_lane = lax.broadcasted_iota(jnp.int32, (1, KEYS), 1)
    absent = jnp.where(key_lane < HALO, 1 - band, 0) + jnp.where(
        (key_lane >= count + HALO) & (key_lane < count + 2 * HALO), band, 0
    )
    absent = absent.astype(F32) * MASKED
    masked_half = jnp.full((COLS, 128), MASKED, F32)
    bands_here = count // COLS
    nothing = jnp.zeros((), BF16)

    def in_head(head, shape):
        first, _ = head_window(head, local)
        at = lax.broadcasted_iota(jnp.int32, shape, 1) + first
        return (at >= head * HD) & (at < (head + 1) * HD)

    r.attended[...] = jnp.zeros(r.attended.shape, F32)
    for head in range(heads):
        first, last = head_window(head, local)
        own = in_head(head, (count, last - first))
        tile = jnp.full((COLS, 128), MASKED, F32)
        for tap in range(TAPS):
            tile = jnp.where(tap_of == tap, r.bias_table[head, r.bias_index[tap]], tile)
        tile = jnp.concatenate([tile, masked_half], axis=1)
        bias = jnp.concatenate(
            [tile] + [pltpu.roll(tile, COLS * k, 1) for k in range(1, bands_here)], axis=0
        )
        queries = jnp.where(own, r.query[:, first:last], nothing)
        scores = dot_nt(queries, r.keys[:, first:last]) * scale + (bias + absent)
        top = jnp.max(scores, axis=-1, keepdims=True)
        weights = jnp.exp(scores - top)
        weights = weights * (1.0 / jnp.sum(weights, axis=-1, keepdims=True))
        r.prob[head] = weights
        mixed = dot_nn(weights.astype(BF16), r.values[:, first:last])
        r.attended[:, first:last] += jnp.where(own, mixed, 0.0)

    r.attended_low[...] = r.attended[...].astype(BF16)
    loaded(weight_names[2], *inputs[5:8])
    r.part_own[...] = dot_nn(r.attended_low[...], r.out_w[...])
    part_copy = sent(r.part_own, r.part_other, sibling)
    if meshed:
        r.attended_all[0] = r.attended_low[...]
        attended_copies = spread(r.attended_low, r.attended_all.at[pl.ds(1, 3)], plane)
        r.rest[...] = jnp.zeros(r.rest.shape, BF16)
        r.back_stage[...] = jnp.zeros(r.back_stage.shape, BF16)
        r.small_half[6:8] = jnp.zeros((2, width), F32)
    loaded(*weight_names[3:], *inputs[8:])
    r.active_grad[...] = dot_nt(r.cotangent[...], r.down_w[...])
    if meshed:
        cot_flat[:, :count] = jnp.transpose(r.cotangent[...])
    finish(part_copy)
    after = r.tokens[...].astype(F32) + (r.part_own[...] + r.part_other[...]) + line_of(r.out_shift)
    r.resid[...] = after
    unit, _ = normed(after)
    r.second_low[...] = (unit * line_of(r.second_gain) + line_of(r.second_shift)).astype(BF16)
    if meshed:
        second_copies = spread_half(r.second_low, r.second_all, column)

    if meshed:
        finish(first_copies)
        first_copies = pass_half(r.first_all, 1, 3)
    step = hidden // 3
    tiles = WIDE_TILES
    second_sum = None
    for at in range(0, hidden, step):
        piece = slice(at, at + step)
        upper = dot_nn(r.second_low[...], r.up_w[:, piece]) + line_of(r.up_shift, piece)
        active, slope = gelu_pair(upper)
        active = active.astype(BF16)
        r.active_low[0:count, piece] = active
        grad = r.active_grad[:, piece] * slope
        sums = column_sum(grad)
        for line in range(-(-hidden // width)):
            low_at, high_at = max(at, line * width), min(at + step, (line + 1) * width)
            if low_at < high_at:
                r.small_own[6 + line : 7 + line, low_at - line * width : high_at - line * width] = (
                    sums[:, low_at - at : high_at - at]
                )
        grad = grad.astype(BF16)
        r.upper_low[0:count, piece] = grad
        term = dot_nt(grad, r.up_w[:, piece])
        second_sum = term if second_sum is None else second_sum + term
    r.second_own[...] = second_sum.astype(BF16)
    second_copy = sent(r.second_own, r.second_other, sibling)
    r.down_own[...] = dot_nn(r.active_low[0:count], r.down_w[...]).astype(BF16)
    down_copy = sent(r.down_own, r.down_other, sibling)
    if meshed:
        finish(first_copies)
        r.first_flat[...] = jnp.transpose(r.first_all[...].reshape(4 * count, width))
        second_flat[:, :count] = jnp.transpose(r.second_low[...])
    cot = r.cotangent[...].astype(F32)
    r.small_own[5:6] = column_sum(cot)
    finish(second_copy)
    back = r.second_own[...].astype(F32) + r.second_other[...].astype(F32)
    unit, inv = normed(r.resid[...])
    r.small_own[3:4] = column_sum(back * unit)
    r.small_own[4:5] = column_sum(back)
    grad = cot + normed_back(unit, inv, line_of(r.second_gain), back)
    r.tokens_grad[...] = grad
    r.small_own[2:3] = column_sum(grad)
    r.resid_low[...] = grad.astype(BF16)
    r.attended_grad[...] = dot_nt(r.resid_low[...], r.out_w[...]).astype(BF16)
    r.query_grad[...] = jnp.zeros(r.query_grad.shape, F32)
    r.key_grad[...] = jnp.zeros(r.key_grad.shape, F32)
    r.value_grad[...] = jnp.zeros(r.value_grad.shape, F32)
    for head in range(heads):
        first, last = head_window(head, local)
        own = in_head(head, (count, last - first))
        queries = jnp.where(own, r.query[:, first:last], nothing)
        grads = jnp.where(own, r.attended_grad[:, first:last], nothing)
        weights = r.prob[head]
        prob_grad = dot_nt(grads, r.values[:, first:last])
        r.value_grad[:, first:last] += dot_tn(weights.astype(BF16), grads)
        product = weights * prob_grad
        score_grad = product - weights * jnp.sum(product, axis=-1, keepdims=True)
        tile = score_grad[0:COLS]
        for k in range(1, bands_here):
            tile = tile + pltpu.roll(score_grad[k * COLS : (k + 1) * COLS], KEYS - COLS * k, 1)
        r.bias_tiles[head] = tile[:, :128]
        low = (score_grad * scale).astype(BF16)
        r.query_grad[:, first:last] += jnp.where(own, dot_nn(low, r.keys[:, first:last]), 0.0)
        r.key_grad[:, first:last] += dot_tn(low, queries)

    if meshed:
        finish(cot_copies[:1] + second_copies[:1])
        near_copies = pass_half(r.cot_all, 0, 1) + pass_half(r.second_all, 0, 1)
    r.halo_own[:, :local] = r.key_grad[pl.ds(halo_at, HALO)].astype(BF16)
    r.halo_own[:, local:] = r.value_grad[pl.ds(halo_at, HALO)].astype(BF16)
    halo_copy = sent(r.halo_own, r.halo_other, beside)
    low = r.query_grad[...].astype(BF16)
    r.query_low[...] = low
    if meshed:
        r.mixed_all[0, :, 128:256] = r.query_low[:, own_lanes]
        query_copies = deal(r.query_low, 128)
        r.rest[1, :, : local - full] = low[:, full:]
    r.small_own[8:9, :local] = column_sum(low.astype(F32))
    out_lane = lax.broadcasted_iota(jnp.int32, (heads, 128), 1)
    table_grad = jnp.zeros((heads, 128), F32)
    for dc in range(WIN):
        diagonal = inside & (col_step == dc - REACH)
        sums = jnp.sum(jnp.where(diagonal[None], r.bias_tiles[...], 0.0), axis=1)
        for dr in range(WIN):
            group = (out_lane >= dr * COLS) & (out_lane < (dr + 1) * COLS)
            total = jnp.sum(jnp.where(group, sums, 0.0), axis=-1, keepdims=True)
            table_grad = jnp.where(out_lane == r.bias_index[dr * WIN + dc], total, table_grad)
    r.small_own[9:10] = r.time_low[...].astype(F32)
    r.small_own[10:16] = jnp.zeros((6, width), F32)
    for head in range(heads):
        r.small_own[10:11, head * 128 : (head + 1) * 128] = table_grad[head : head + 1]
    if meshed:
        mark = lax.broadcasted_iota(jnp.int32, (1, width), 1) == image * 128 + MARK
        stamp = jnp.where(band == 0, r.step_index[0], 0).astype(F32)
        r.small_own[10:11] += jnp.where(mark, stamp, 0.0)
    finish(down_copy)
    lowered = r.down_own[...].astype(F32) + r.down_other[...].astype(F32)
    r.output[...] = (r.resid[...] + lowered + line_of(r.down_shift)).astype(BF16)

    if meshed:
        r.resid_turned[...] = jnp.transpose(r.tokens_grad[...])
        for k, at in enumerate([spot] + spots):
            lines = [
                r.resid_turned[pl.ds(pl.multiple_of(line * rows4 + owners * at, 8), owners)]
                for line in range(4)
            ]
            r.resid_stage[k] = jnp.concatenate(lines, axis=0).astype(BF16)
        r.resid_all[:, 0:count] = r.resid_stage[0]
        base = links(3)
        resid_copies = started(
            [
                remote(
                    base + k,
                    r.resid_stage.at[k + 1],
                    r.resid_all.at[:, pl.ds((k + 1) * count, count)],
                    plane[k],
                )
                for k in range(3)
            ]
        )
    first_sum = dot_nn(r.query_low[...], r.in_w[0:local])
    unit, inv = normed(r.tokens[...].astype(F32))
    tokens4 = 4 * count
    if meshed:
        finish(near_copies)
        cot_flat[:, count : 2 * count] = jnp.transpose(r.cot_all[0])
        second_flat[:, count : 2 * count] = jnp.transpose(r.second_all[0])

        def near_piece(t):
            piece = slice(t * step, (t + 1) * step)
            upper = dot_nn(r.second_all[0], r.up_w[:, piece]) + line_of(r.up_shift, piece)
            active, slope = gelu_pair(upper)
            r.active_low[count:, piece] = active.astype(BF16)
            grad = dot_nt(r.cot_all[0], r.down_w[piece]) * slope
            r.upper_low[count:, piece] = grad.astype(BF16)

        near_piece(0)
        near_piece(1)
    finish(halo_copy)
    if meshed:
        finish(cot_copies[1:])
        cot_copies = pass_half(r.cot_all, 1, 2)
    edge_at = pl.multiple_of(HALO + edge, HALO)
    arrived = r.halo_other[...].astype(F32)
    r.key_grad[pl.ds(edge_at, HALO)] += arrived[:, :local]
    r.value_grad[pl.ds(edge_at, HALO)] += arrived[:, local:]
    low = r.key_grad[pl.ds(HALO, count)].astype(BF16)
    r.key_low[...] = low
    if meshed:
        r.mixed_all[0, :, 256:384] = r.key_low[:, own_lanes]
        key_copies = deal(r.key_low, 256)
        r.rest[2, :, : local - full] = low[:, full:]
    low = r.value_grad[pl.ds(HALO, count)].astype(BF16)
    r.value_low[...] = low
    if meshed:
        r.mixed_all[0, :, 384:512] = r.value_low[:, own_lanes]
        value_copies = deal(r.value_low, 384)
        r.rest[3, :, : local - full] = low[:, full:]
        r.mixed_all[0, :, 512:640] = r.rest[spot]
        base = links(3)
        rest_copies = started(
            [
                remote(
                    base + k,
                    r.rest.at[spots[k]],
                    r.mixed_all.at[k + 1, :, pl.ds(512, 128)],
                    plane[k],
                )
                for k in range(3)
            ]
        )
    r.small_own[8:9, local:] = column_sum(low.astype(F32))

    def first_back():
        total = first_sum + dot_nn(r.key_low[...], r.in_w[local : 2 * local])
        total = total + dot_nn(r.value_low[...], r.in_w[2 * local :])
        r.first_own[...] = total.astype(BF16)
        return sent(r.first_own, r.first_other, sibling)

    def first_norm_back():
        back = r.first_own[...].astype(F32) + r.first_other[...].astype(F32)
        r.small_own[0:1] = column_sum(back * unit)
        r.small_own[1:2] = column_sum(back)
        r.tokens_grad[...] += normed_back(unit, inv, line_of(r.first_gain), back)

    if not meshed:
        finish(first_back())
        first_norm_back()
        return

    def mixed(start, stop):
        return r.mixed_all[:, :, start:stop].reshape(tokens4, stop - start)

    near, far = plane[:2]
    starts = [sum(tiles[:t]) for t in range(len(tiles))]

    def wide_lanes(t):
        return pl.ds(starts[t] // 2, tiles[t] // 2)

    def wide_first(t):
        base, lanes = links(4), wide_lanes(t)
        return started(
            [
                remote(
                    base + k,
                    part.at[target, :, lanes],
                    arrived.at[k % 2, :, lanes],
                    near if k < 2 else far,
                )
                for k, (part, arrived, target) in enumerate(
                    (
                        (r.wide_a, r.wide_a_in, spots[0]),
                        (r.wide_a, r.wide_a_in, spots[2]),
                        (r.wide_b, r.wide_b_in, spots[1]),
                        (r.wide_b, r.wide_b_in, spots[2]),
                    )
                )
            ]
        )

    def wide_piece(t):
        piece, lanes = slice(starts[t], starts[t] + tiles[t]), wide_lanes(t)
        upper = dot_nn(r.second_all[1:].reshape(2 * count, width), r.up_w[:, piece])
        active, slope = gelu_pair(upper + line_of(r.up_shift, piece))
        grad = dot_nt(r.cot_all[1:].reshape(2 * count, width), r.down_w[piece]) * slope
        down = dot_nn(cot_flat[own_rows, : 2 * count], r.active_low[:, piece])
        down = down + dot_nn(cot_flat[own_rows, 2 * count :], active.astype(BF16))
        up = dot_nn(second_flat[own_rows, : 2 * count], r.upper_low[:, piece])
        up = up + dot_nn(second_flat[own_rows, 2 * count :], grad.astype(BF16))
        part = tiles[t] // 2
        for k in range(4):
            rows_here = slice(k * owners, (k + 1) * owners)
            both = jnp.concatenate([down[rows_here], up[rows_here]], axis=0).astype(BF16)
            r.wide_a[k, :, lanes] = both[:, :part]
            r.wide_b[k, :, lanes] = both[:, part:]
        return wide_first(t)

    def wide_second(t):
        lanes = wide_lanes(t)
        finish(wide_copies[t])
        total = joined(r.wide_a[spots[1], :, lanes], r.wide_a_in[1, :, lanes])
        r.wide_a_sum[:, lanes] = total.astype(BF16)
        total = joined(r.wide_b[spots[0], :, lanes], r.wide_b_in[1, :, lanes])
        r.wide_b_sum[:, lanes] = total.astype(BF16)
        return sent(r.wide_a_sum.at[:, lanes], r.wide_a_last.at[:, lanes], far) + sent(
            r.wide_b_sum.at[:, lanes], r.wide_b_last.at[:, lanes], near
        )

    def wide_total(t):
        finish(last_copies[t])
        lanes, at = wide_lanes(t), starts[t]
        for part, arrived, last in (
            (r.wide_a, r.wide_a_in, r.wide_a_last),
            (r.wide_b, r.wide_b_in, r.wide_b_last),
        ):
            total = joined(part[spot, :, lanes], arrived[0, :, lanes])
            total = total + last[:, lanes].astype(F32)
            r.down_share[:, at : at + tiles[t] // 2] = total[:owners]
            r.up_share[:, at : at + tiles[t] // 2] = total[owners:]
            at += tiles[t] // 2

    finish(query_copies)
    keep_part("query", dot_nn(r.first_flat[...], mixed(128, 256)))
    query_copies = column_first("query")
    finish(second_copies[1:])
    far_copies = pass_half(r.second_all, 1, 2)
    finish(cot_copies)
    cot_flat[:, 2 * count :] = jnp.transpose(r.cot_all[1:].reshape(2 * count, width))
    near_piece(2)
    finish(key_copies)
    keep_part("key", dot_nn(r.first_flat[...], mixed(256, 384)))
    key_copies = column_first("key")
    finish(far_copies)
    second_flat[:, 2 * count :] = jnp.transpose(r.second_all[1:].reshape(2 * count, width))
    wide_copies = [wide_piece(0)]
    finish(query_copies)
    query_copies = column_second("query")
    wide_copies.append(wide_piece(1))
    finish(value_copies)
    keep_part("value", dot_nn(r.first_flat[...], mixed(384, 512)))
    value_copies = column_first("value")
    wide_copies.append(wide_piece(2))
    first_copy = first_back()
    finish(key_copies)
    key_copies = column_second("key")
    finish(rest_copies)
    term = dot_nn(r.first_flat[...], mixed(512, 640))
    for k in range(4):
        upper_half = term[k * rows4 : k * rows4 + rows4 // 2, : local - full]
        lower_half = term[k * rows4 + rows4 // 2 : (k + 1) * rows4, : local - full]
        r.rest_part[k] = jnp.concatenate([upper_half, lower_half], axis=1).astype(BF16)
    base = links(3)
    rest_copies = started(
        [remote(base + k, r.rest_part.at[heights[k]], r.rest_in.at[k], column[k]) for k in range(3)]
    )
    wide_copies.append(wide_piece(3))
    finish(value_copies)
    value_copies = column_second("value")
    wide_copies.append(wide_piece(4))
    finish(first_copy)
    first_norm_back()
    r.small_send[0:3] = jnp.where(half == 0, r.small_own[0:3], r.small_own[3:6])
    r.small_send[3:5] = r.small_own[6:8]
    r.small_send[5:6] = r.small_own[10:11]
    r.small_send[6:8] = jnp.broadcast_to(r.small_own[8:9], (2, width))
    small_copies = spread(r.small_send, r.small_plane, plane)
    last_copies = [wide_second(0)]
    last_copies.append(wide_second(1))
    finish(attended_copies)
    finish(resid_copies)
    keep_part("attended", dot_nn(r.resid_all[...], r.attended_all[...].reshape(tokens4, local)))
    attended_copies = column_first("attended")
    finish(query_copies)
    total = column_total("query")
    for k in range(4):
        r.front_stage[k] = total[k * owners : (k + 1) * owners].astype(BF16)
    r.front_done[spot] = r.front_stage[spot]
    front_copies = hand_out(r.front_stage, r.front_done)
    finish(rest_copies)
    total = joined(r.rest_part[z], r.rest_in[0]) + joined(r.rest_in[1], r.rest_in[2])
    for k in range(4):
        lanes = slice(k // 2 * (local - full), (k // 2 + 1) * (local - full))
        rows_here = slice(k % 2 * owners, (k % 2 + 1) * owners)
        r.back_stage[k, :, 256 : 256 + local - full] = total[rows_here, lanes].astype(BF16)
    last_copies.append(wide_second(2))
    finish(key_copies)
    total = column_total("key")
    for k in range(4):
        r.back_stage[k, :, :128] = total[k * owners : (k + 1) * owners].astype(BF16)
    last_copies.append(wide_second(3))
    finish(value_copies)
    total = column_total("value")
    for k in range(4):
        r.back_stage[k, :, 128:256] = total[k * owners : (k + 1) * owners].astype(BF16)
    r.back_done[spot] = r.back_stage[spot]
    back_copies = hand_out(r.back_stage, r.back_done)
    last_copies.append(wide_second(4))
    finish(small_copies)
    small_sum = r.small_send[0:6]
    for k in range(3):
        small_sum = small_sum + r.small_plane[k, 0:6]
    r.small_z[0:6] = small_sum
    r.small_z[6:7] = r.small_send[6:7] + r.small_plane[1, 6:7]
    r.small_z[7:8] = r.small_plane[0, 6:7] + r.small_plane[2, 6:7]
    column_copies = spread(r.small_z, r.small_column, column)
    finish(attended_copies)
    attended_copies = column_second("attended")
    wide_total(0)
    wide_total(1)
    finish(column_copies)
    small_sum = r.small_z[0:6]
    for k in range(3):
        small_sum = small_sum + r.small_column[k, 0:6]
    r.small_half[0:6] = small_sum
    small_copies = sent(r.small_half, r.small_other, sibling)
    steps = [small_sum[5:6, k * 128 + MARK : k * 128 + MARK + 1] for k in range(8)]
    cosine, sine = cos_sin(jnp.concatenate(steps, axis=0) * line_of(r.frequencies))
    r.time_lines[:, : width // 2] = cosine.astype(BF16).astype(F32)
    r.time_lines[:, width // 2 :] = sine.astype(BF16).astype(F32)
    r.time_flat[...] = jnp.transpose(r.time_lines[...])
    time_cut = r.time_flat[pl.ds(pl.multiple_of(z * rows4 + spot * owners, 8), owners)]
    time_share = jnp.zeros((owners, width), F32)
    for k in range(4):
        source = r.small_z if k == 0 else r.small_column.at[k - 1]
        at = z if k == 0 else heights[k - 1]
        r.time_sums[pl.ds(2 * at + x, 1)] = source[6:7]
        r.time_sums[pl.ds(2 * at + 1 - x, 1)] = source[7:8]
    for k in range(8):
        time_share = time_share + time_cut[:, k : k + 1] * r.time_sums[k : k + 1]
    r.time_share[0] = time_share[:, :local]
    r.time_share[1] = time_share[:, local:]
    wide_total(2)
    finish(small_copies)
    low_half, high_half = r.small_half[0:3], r.small_other[0:3]
    r.small_sums[0:3] = jnp.where(half == 0, low_half, high_half)
    r.small_sums[3:6] = jnp.where(half == 0, high_half, low_half)
    r.small_sums[6:8] = r.small_half[3:5]
    r.small_sums[8:16] = jnp.broadcast_to(r.small_half[5:6], (8, width))
    finish(front_copies)
    for k in range(4):
        r.in_share[0, :, k * 128 : (k + 1) * 128] = r.front_done[k].astype(F32)
    finish(attended_copies)
    r.out_share[...] = column_total("attended")
    wide_total(3)
    finish(back_copies)
    for k in range(4):
        for line in range(2):
            lanes = slice(line * 128, (line + 1) * 128)
            share = r.back_done[k, :, lanes].astype(F32)
            r.in_share[1 + line, :, k * 128 : (k + 1) * 128] = share
        if k > 0:
            rest = r.back_done[k, :, 256 : 256 + local - full].astype(F32)
            r.in_share[k - 1, :, full:] = rest
    wide_total(4)


def final_kernel(heads, names, *refs):
    r = types.SimpleNamespace(**dict(zip(names, refs, strict=True)))
    copies = [
        pltpu.make_async_copy(source, target, r.sems.at[i])
        for i, (source, target) in enumerate(
            (
                (r.output, r.output_done),
                (r.tokens_grad, r.tokens_done),
                (r.in_share, r.in_done),
                (r.out_share, r.out_done),
                (r.up_share, r.up_done),
                (r.down_share, r.down_done),
            )
        )
    ]
    for copy in copies:
        copy.start()
    width = r.small_sums.shape[1]
    for line, target in enumerate(
        (
            r.first_gain_done,
            r.first_shift_done,
            r.out_shift_done,
            r.second_gain_done,
            r.second_shift_done,
            r.down_shift_done,
        )
    ):
        target[...] = r.small_sums[line]
    for line in range(r.up_shift_done.shape[0] // width):
        r.up_shift_done[line * width : (line + 1) * width] = r.small_sums[6 + line]
    for head in range(heads):
        r.bias_done[head : head + 1] = r.small_sums[8:9, head * 128 : head * 128 + TAPS]
    local = r.time_share.shape[2]
    for k in range(2):
        r.time_done[:, k, :] = r.time_share[k]
    for copy in copies:
        copy.wait()


def final_call(results, heads, hidden):
    inputs = dict(
        output=results.output,
        tokens_grad=results.tokens_grad,
        in_share=results.in_share,
        out_share=results.out_share,
        up_share=results.up_share,
        down_share=results.down_share,
        small_sums=results.small_sums,
        time_share=results.time_share,
    )
    width = results.small_sums.shape[1]
    _, owners, local = results.time_share.shape
    struct = jax.ShapeDtypeStruct
    line = struct((width,), F32)
    outs = dict(
        output_done=struct(results.output.shape, BF16),
        tokens_done=struct(results.tokens_grad.shape, F32),
        in_done=struct(results.in_share.shape, F32),
        out_done=struct(results.out_share.shape, F32),
        up_done=struct(results.up_share.shape, F32),
        down_done=struct(results.down_share.shape, F32),
        first_gain_done=line,
        first_shift_done=line,
        out_shift_done=line,
        second_gain_done=line,
        second_shift_done=line,
        down_shift_done=line,
        up_shift_done=struct((hidden,), F32),
        bias_done=struct((heads, TAPS), F32),
        time_done=struct((owners, 2, local), F32),
    )
    vmem = pl.BlockSpec(memory_space=pltpu.VMEM)
    hbm = pl.BlockSpec(memory_space=pltpu.HBM)
    done = pl.pallas_call(
        functools.partial(final_kernel, heads, [*inputs, *outs, "sems"]),
        out_shape=list(outs.values()),
        in_specs=[vmem] * 8,
        out_specs=[hbm] * 6 + [vmem] * (len(outs) - 6),
        scratch_shapes=[pltpu.SemaphoreType.DMA((6,))],
        name="final",
        compiler_params=pltpu.CompilerParams(vmem_limit_bytes=8 * 1024 * 1024),
    )(*inputs.values())
    return types.SimpleNamespace(**dict(zip(outs, done, strict=True)))


def layer_call(meshed, timesteps, inputs, smalls, weights):
    count, width = inputs["tokens"].shape
    local = weights["out_w"].shape[0]
    hidden = weights["up_w"].shape[1]
    heads = smalls["bias_table"].shape[0]
    tokens4, rows4 = 4 * count, width // 4
    owners = rows4 // 4
    outs = dict(output=((count, width), BF16), tokens_grad=((count, width), F32))
    feed_rows = 2 * count if meshed else count
    kept = dict(
        first_low=((count, width), BF16),
        second_low=((count, width), BF16),
        active_low=((feed_rows, hidden), BF16),
        upper_low=((feed_rows, hidden), BF16),
        resid_low=((count, width), BF16),
        attended_low=((count, local), BF16),
        query_low=((count, local), BF16),
        key_low=((count, local), BF16),
        value_low=((count, local), BF16),
        small_own=((16, width), F32),
    )
    loads = inputs | weights
    scratch = {name: (array.shape, array.dtype) for name, array in loads.items()}
    scratch |= dict(
        time_low=((1, width), BF16),
        halo_tokens=((HALO, width), BF16),
        query=((count, local), BF16),
        keys=((KEYS, local), BF16),
        values=((KEYS, local), BF16),
        prob=((heads, count, KEYS), F32),
        key_grad=((KEYS, local), F32),
        value_grad=((KEYS, local), F32),
        attended_grad=((count, local), BF16),
        query_grad=((count, local), F32),
        attended=((count, local), F32),
        active_grad=((count, hidden), F32),
        resid=((count, width), F32),
        part_own=((count, width), F32),
        part_other=((count, width), F32),
        halo_own=((HALO, 2 * local), BF16),
        halo_other=((HALO, 2 * local), BF16),
        bias_tiles=((heads, COLS, 128), F32),
    )
    scratch |= dict(
        down_own=((count, width), BF16),
        down_other=((count, width), BF16),
        second_own=((count, width), BF16),
        second_other=((count, width), BF16),
        first_own=((count, width), BF16),
        first_other=((count, width), BF16),
    )
    if meshed:
        outs |= dict(
            small_sums=((16, width), F32),
            in_share=((3, owners, local), F32),
            time_share=((2, owners, local), F32),
            out_share=((owners, local), F32),
            up_share=((owners, hidden), F32),
            down_share=((owners, hidden), F32),
        )
        scratch |= kept
        scratch |= dict(
            cot_all=((3, count, width), BF16),
            second_all=((3, count, width), BF16),
            first_all=((4, count, width), BF16),
            first_flat=((width, tokens4), BF16),
            attended_all=((4, count, local), BF16),
            resid_turned=((width, count), F32),
            resid_stage=((4, rows4, count), BF16),
            resid_all=((rows4, tokens4), BF16),
            small_send=((8, width), F32),
            small_plane=((3, 8, width), F32),
            small_z=((8, width), F32),
            small_column=((3, 8, width), F32),
            time_sums=((8, width), F32),
            time_lines=((8, width), F32),
            small_half=((8, width), F32),
            small_other=((8, width), F32),
            time_flat=((width, 8), F32),
            mixed_all=((4, count, 640), BF16),
            rest=((4, count, 128), BF16),
            rest_part=((4, rows4 // 2, 128), BF16),
            rest_in=((3, rows4 // 2, 128), BF16),
            front_stage=((4, owners, 128), BF16),
            front_done=((4, owners, 128), BF16),
            back_stage=((4, owners, 384), BF16),
            back_done=((4, owners, 384), BF16),
        )
        for name, rows, wide in (
            ("attended", owners, local),
            ("query", rows4, 128),
            ("key", rows4, 128),
            ("value", rows4, 128),
        ):
            scratch[name + "_part"] = ((4, rows, wide), BF16)
            scratch[name + "_in"] = ((2, rows, wide), BF16)
            scratch[name + "_sum"] = ((rows, wide), BF16)
            scratch[name + "_last"] = ((rows, wide), BF16)
        for name in ("wide_a", "wide_b"):
            scratch[name] = ((4, 2 * owners, hidden // 2), BF16)
            scratch[name + "_in"] = ((2, 2 * owners, hidden // 2), BF16)
            scratch[name + "_sum"] = ((2 * owners, hidden // 2), BF16)
            scratch[name + "_last"] = ((2 * owners, hidden // 2), BF16)
    else:
        outs |= kept
    links = 112 if meshed else 6
    sems = dict(load_sems=len(loads | smalls), send_sems=links, recv_sems=links)
    vmem = pl.BlockSpec(memory_space=pltpu.VMEM)
    smem = pl.BlockSpec(memory_space=pltpu.SMEM)
    hbm = pl.BlockSpec(memory_space=pltpu.HBM)
    names = [name + "_hbm" for name in (*loads, *smalls)]
    names = ["step_index", *names, *outs, *smalls, *scratch, *sems]
    results = pl.pallas_call(
        functools.partial(layer_kernel, names, [*inputs], [*smalls], [*weights], meshed),
        out_shape=[jax.ShapeDtypeStruct(*shape) for shape in outs.values()],
        in_specs=[smem] + [hbm] * len(loads | smalls),
        out_specs=[vmem] * len(outs),
        scratch_shapes=[pltpu.SMEM(array.shape, array.dtype) for array in smalls.values()]
        + [pltpu.VMEM(*shape) for shape in scratch.values()]
        + [pltpu.SemaphoreType.DMA((number,)) for number in sems.values()],
        name="layer",
        compiler_params=pltpu.CompilerParams(
            collective_id=0, has_side_effects=True, vmem_limit_bytes=50 * 1024 * 1024
        ),
    )(
        timesteps,
        *[
            pltpu.with_memory_space_constraint(array, pltpu.HBM)
            for array in (loads | smalls).values()
        ],
    )
    return types.SimpleNamespace(**dict(zip(outs, results, strict=True)))


def on_device(
    tokens,
    timesteps,
    first_gain,
    first_shift,
    project_in,
    time_weight,
    bias_table,
    bias_index,
    project_out,
    out_shift,
    second_gain,
    second_shift,
    up_weight,
    up_shift,
    down_weight,
    down_shift,
    cotangent,
):
    batch, band_rows, columns, width = tokens.shape
    local = project_in.shape[2]
    count = batch * band_rows * columns
    assert batch == 1 and columns == COLS
    half = width // 2
    frequencies = np.exp(np.arange(half) * (-math.log(10000.0) / half)).astype(np.float32)
    meshed = lax.axis_size("img") == 8 and lax.axis_size("band") == 2
    cot = cotangent.reshape(count, width)
    inputs = dict(
        tokens=tokens.reshape(count, width),
        first_gain=first_gain,
        first_shift=first_shift,
        frequencies=jnp.asarray(frequencies),
        cotangent=cot,
        out_shift=out_shift,
        second_gain=second_gain,
        second_shift=second_shift,
        up_shift=up_shift,
        down_shift=down_shift,
    )
    smalls = dict(bias_table=bias_table, bias_index=bias_index)
    weights = dict(
        time_w=jnp.transpose(time_weight, (1, 2, 0)).reshape(2 * local, width),
        in_w=jnp.transpose(project_in, (1, 2, 0)).reshape(3 * local, width),
        out_w=project_out,
        up_w=up_weight,
        down_w=down_weight,
    )
    r = layer_call(meshed, timesteps, inputs, smalls, weights)
    heads = bias_table.shape[0]
    if meshed:
        f = final_call(r, heads, up_shift.shape[0])
        return (
            f.output_done.reshape(tokens.shape),
            f.tokens_done.reshape(tokens.shape),
            f.first_gain_done,
            f.first_shift_done,
            jnp.transpose(f.in_done, (1, 0, 2)),
            f.time_done,
            f.bias_done,
            jnp.transpose(f.out_done),
            f.out_shift_done,
            f.second_gain_done,
            f.second_shift_done,
            f.up_done,
            f.up_shift_done,
            jnp.transpose(f.down_done),
            f.down_shift_done,
        )
    axes = ("img", "band")
    grads = (
        dot_tn(r.first_low, jnp.concatenate([r.query_low, r.key_low, r.value_low], axis=1)),
        dot_tn(r.resid_low, r.attended_low),
        dot_tn(r.second_low, r.upper_low),
        dot_tn(cot, r.active_low),
    )
    in_share, out_share, up_share, down_share = [
        lax.psum_scatter(g.astype(BF16), axes, scatter_dimension=0, tiled=True).astype(F32)
        for g in grads
    ]
    rows = in_share.shape[0]
    in_share = in_share.reshape(rows, 3, local)
    times = lax.all_gather(r.small_own[8:10], axes, axis=0)
    here = lax.axis_index(axes) * rows
    time_cut = lax.dynamic_slice_in_dim(times[:, 1], here, rows, axis=1)
    time_share = jnp.einsum("nd,nk->dk", time_cut, times[:, 0], precision=HIGHEST)
    time_share = time_share.reshape(rows, 2, local)
    small = lax.psum(r.small_own, axes)
    return (
        r.output.reshape(tokens.shape),
        r.tokens_grad.reshape(tokens.shape),
        small[0],
        small[1],
        in_share,
        time_share,
        small[10, : heads * 128].reshape(heads, 128)[:, :TAPS],
        jnp.transpose(out_share),
        small[2],
        small[3],
        small[4],
        up_share,
        small[6:8].reshape(-1)[: up_shift.shape[0]],
        jnp.transpose(down_share),
        small[5],
    )


def solution(mesh):
    return jax.shard_map(
        on_device,
        mesh=mesh,
        in_specs=(
            P("img", "band", None, None),
            P("img"),
            P(),
            P(),
            P(None, None, "head"),
            P(None, None, "head"),
            P("head", None),
            P(),
            P("head", None),
            P(),
            P(),
            P(),
            P(None, "head"),
            P("head"),
            P("head", None),
            P(),
            P("img", "band", None, None),
        ),
        out_specs=(
            P("img", "band", None, None),
            P("img", "band", None, None),
            P(),
            P(),
            P(("img", "band"), None, "head"),
            P(("img", "band"), None, "head"),
            P("head", None),
            P("head", ("img", "band")),
            P(),
            P(),
            P(),
            P(("img", "band"), "head"),
            P("head"),
            P("head", ("img", "band")),
            P(),
        ),
        check_vma=False,
    )
```

```python
import functools
import math
import types

import jax
import jax.numpy as jnp
import numpy as np
from jax import lax
from jax.experimental import pallas as pl
from jax.experimental.pallas import tpu as pltpu
from jax.sharding import PartitionSpec as P

HD = 72
ROWS = 16
COLS = 16
WIN = 5
REACH = WIN // 2
TAPS = WIN * WIN
HALO = REACH * COLS
KEYS = 256

EPSILON = 1e-05
MASKED = -1000000000.0
HIGHEST = lax.Precision.HIGHEST
MESH = pl.DeviceIdType.MESH
BF16 = jnp.bfloat16
F32 = jnp.float32
GELU_A = math.sqrt(2.0 / math.pi)
GELU_B = 0.044715
MARK = 100
WIDE_TILES = (256, 512, 768, 512, 256)
TURN = (6.28125, 0.0019350051879882812, 3.019916e-07)


def dot_nn(a, b):
    return lax.dot_general(a, b, (((1,), (0,)), ((), ())), preferred_element_type=F32)


def dot_nt(a, b):
    return lax.dot_general(a, b, (((1,), (1,)), ((), ())), preferred_element_type=F32)


def dot_tn(a, b):
    return lax.dot_general(a, b, (((0,), (0,)), ((), ())), preferred_element_type=F32)


def normed(values):
    center = values - jnp.mean(values, axis=-1, keepdims=True)
    inv = lax.rsqrt(jnp.mean(center * center, axis=-1, keepdims=True) + EPSILON)
    return center * inv, inv


def normed_back(unit, inv, gain, grad):
    unit_grad = grad * gain
    return inv * (
        unit_grad
        - jnp.mean(unit_grad, axis=-1, keepdims=True)
        - unit * jnp.mean(unit_grad * unit, axis=-1, keepdims=True)
    )


def gelu_pair(u):
    square = u * u
    t = jnp.tanh(GELU_A * u * (1.0 + GELU_B * square))
    half = 0.5 * (1.0 + t)
    slope = half + (0.5 * GELU_A) * u * (1.0 - t * t) * (1.0 + (3.0 * GELU_B) * square)
    return u * half, slope


def column_sum(values):
    return jnp.sum(values, axis=0, keepdims=True)


def cos_sin(angle):
    turns = jnp.floor(angle * (0.5 / math.pi) + 0.5)
    rest = ((angle - turns * TURN[0]) - turns * TURN[1]) - turns * TURN[2]
    square = rest * rest
    cosine = jnp.full(angle.shape, 1.0 / math.factorial(18), F32)
    sine = jnp.full(angle.shape, 1.0 / math.factorial(19), F32)
    for power in range(16, -1, -2):
        cosine = 1.0 / math.factorial(power) - cosine * square
        sine = 1.0 / math.factorial(power + 1) - sine * square
    return cosine, sine * rest


def line_of(vector, piece=slice(None)):
    return vector[piece][None, :]


def head_window(head, width):
    first = head * HD // 128 * 128
    last = min(-(-(head + 1) * HD // 128) * 128, width)
    return first, last


def layer_kernel(names, inputs, small_names, weight_names, meshed, *refs):
    r = types.SimpleNamespace(**dict(zip(names, refs, strict=True)))
    count, width = r.tokens.shape
    local = r.query.shape[1]
    heads = r.bias_table.shape[0]
    hidden = r.up_shift.shape[0]
    scale = HD ** (-0.5)
    image = lax.axis_index("img")
    band = lax.axis_index("band")
    half = lax.axis_index("head")
    sibling = (image, band, 1 - half)
    beside = (image, 1 - band, half)
    peers = [sibling, beside]
    if meshed:
        x, z = image % 2, image // 2
        across = z * 2 + 1 - x
        plane = [(across, band, half), beside, (across, 1 - band, half)]
        spot = 2 * x + band
        spots = [2 * (1 - x) + band, 2 * x + 1 - band, 2 * (1 - x) + 1 - band]
        heights = [z + 1 - 2 * (z % 2), 3 - z, (z + 2) % 4]
        column = [(at * 2 + x, band, half) for at in heights]
        peers = [sibling, *plane, *column]

    loads = {}
    for name in (*inputs[:4], *weight_names[:2], *small_names, *inputs[4:], *weight_names[2:]):
        source, target = getattr(r, name + "_hbm"), getattr(r, name)
        loads[name] = pltpu.make_async_copy(source, target, r.load_sems.at[len(loads)])
        loads[name].start()

    def loaded(*wanted):
        for name in wanted:
            loads.pop(name).wait()

    barrier = pltpu.get_barrier_semaphore()
    for other in peers:
        pl.semaphore_signal(barrier, inc=1, device_id=other, device_id_type=MESH)

    used = [0]

    def links(number):
        used[0] += number
        assert used[0] <= r.send_sems.shape[0]
        return used[0] - number

    def remote(index, source, target, device):
        return pltpu.make_async_remote_copy(
            src_ref=source,
            dst_ref=target,
            send_sem=r.send_sems.at[index],
            recv_sem=r.recv_sems.at[index],
            device_id=device,
            device_id_type=MESH,
        )

    def started(copies):
        for copy in copies:
            copy.start()
        return copies

    def sent(source, target, device):
        return started([remote(links(1), source, target, device)])

    def finish(copies):
        for copy in copies:
            copy.wait()

    def spread(source, slots, group):
        base = links(3)
        return started([remote(base + k, source, slots.at[k], group[k]) for k in range(3)])

    def deal(source, lanes):
        base = links(3)
        return started(
            [
                remote(
                    base + k,
                    source.at[:, pl.ds(pl.multiple_of(spots[k] * 128, 128), 128)],
                    r.mixed_all.at[k + 1, :, pl.ds(lanes, 128)],
                    plane[k],
                )
                for k in range(3)
            ]
        )

    def column_first(name):
        part, arrived = getattr(r, name + "_part"), getattr(r, name + "_in")
        base = links(2)
        return started(
            [remote(base + k, part.at[heights[k]], arrived.at[k], column[0]) for k in range(2)]
        )

    def column_second(name):
        part, arrived = getattr(r, name + "_part"), getattr(r, name + "_in")
        summed = getattr(r, name + "_sum")
        summed[...] = joined(part[heights[2]], arrived[1]).astype(BF16)
        return sent(summed, getattr(r, name + "_last"), column[2])

    def column_total(name):
        part, arrived = getattr(r, name + "_part"), getattr(r, name + "_in")
        return joined(part[z], arrived[0]) + getattr(r, name + "_last")[...].astype(F32)

    def joined(left, right):
        return left.astype(F32) + right.astype(F32)

    def keep_part(name, values):
        part = getattr(r, name + "_part")
        part[...] = values.astype(BF16).reshape(part.shape)

    def hand_out(stage, slots):
        base = links(3)
        return started(
            [remote(base + k, stage.at[spots[k]], slots.at[spot], plane[k]) for k in range(3)]
        )

    if meshed:
        mine = pl.ds(pl.multiple_of(half * (count // 2), count // 2), count // 2)
        full = local // 128 * 128
        own_lanes = pl.ds(pl.multiple_of(spot * 128, 128), 128)

    def spread_half(source, slots, group):
        base = links(3)
        return started(
            [remote(base + k, source.at[mine], slots.at[k, mine], group[k]) for k in range(3)]
        )

    def pass_half(slots, slot, number):
        part = slots.at[pl.ds(slot, number), mine]
        return sent(part, part, sibling)

    loaded(*inputs[:3])
    unit, _ = normed(r.tokens[...].astype(F32))
    own_low = (unit * line_of(r.first_gain) + line_of(r.first_shift)).astype(BF16)
    r.first_low[...] = own_low

    loaded(inputs[3])
    angle = r.step_index[0].astype(F32) * line_of(r.frequencies)
    cosine, sine = cos_sin(angle)
    r.time_low[:, : width // 2] = cosine.astype(BF16)
    r.time_low[:, width // 2 :] = sine.astype(BF16)
    pl.semaphore_wait(barrier, len(peers))
    edge = pl.multiple_of((1 - band) * (count - HALO), HALO)
    token_copy = sent(r.tokens.at[pl.ds(edge, HALO)], r.halo_tokens, beside)
    loaded(inputs[4])
    if meshed:
        cot_copies = spread_half(r.cotangent, r.cot_all, column)
        r.first_all[0] = own_low
        first_copies = spread_half(r.first_low, r.first_all.at[pl.ds(1, 3)], plane)
        rows4 = width // 4
        owners = rows4 // 4
        cot_flat = r.time_w.at[:, pl.ds(0, 4 * count)]
        second_flat = r.time_w.at[:, pl.ds(4 * count, 4 * count)]
        own_rows = pl.ds(pl.multiple_of(z * rows4, 32), rows4)
    loaded(weight_names[0])
    time_rows = jnp.broadcast_to(r.time_low[...], (8, width))
    time_proj = dot_nt(time_rows, r.time_w[...])[0:1]
    halo_at = pl.multiple_of((1 - band) * (count + HALO), HALO)
    blank_at = pl.multiple_of(band * (count + HALO), HALO)
    tail = KEYS - count - 2 * HALO
    loaded(weight_names[1])
    r.query[...] = (dot_nt(own_low, r.in_w[0:local]) + time_proj[:, :local]).astype(BF16)
    r.keys[pl.ds(HALO, count)] = dot_nt(own_low, r.in_w[local : 2 * local]).astype(BF16)
    projected = dot_nt(own_low, r.in_w[2 * local : 3 * local]) + time_proj[:, local:]
    r.values[pl.ds(HALO, count)] = projected.astype(BF16)
    for kept in (r.keys, r.values):
        kept[pl.ds(blank_at, HALO)] = jnp.zeros((HALO, local), BF16)
        kept[pl.ds(count + 2 * HALO, tail)] = jnp.zeros((tail, local), BF16)
    finish(token_copy)
    unit, _ = normed(r.halo_tokens[...].astype(F32))
    halo_low = (unit * line_of(r.first_gain) + line_of(r.first_shift)).astype(BF16)
    r.keys[pl.ds(halo_at, HALO)] = dot_nt(halo_low, r.in_w[local : 2 * local]).astype(BF16)
    projected = dot_nt(halo_low, r.in_w[2 * local : 3 * local]) + time_proj[:, local:]
    r.values[pl.ds(halo_at, HALO)] = projected.astype(BF16)

    loaded(*small_names)
    lane = lax.broadcasted_iota(jnp.int32, (COLS, 128), 1)
    row = lax.broadcasted_iota(jnp.int32, (COLS, 128), 0)
    col_step = lane % COLS - row
    row_step = lane // COLS
    inside = (col_step >= -REACH) & (col_step <= REACH) & (row_step < WIN)
    tap_of = jnp.where(inside, row_step * WIN + col_step + REACH, -1)
    key_lane = lax.broadcasted_iota(jnp.int32, (1, KEYS), 1)
    absent = jnp.where(key_lane < HALO, 1 - band, 0) + jnp.where(
        (key_lane >= count + HALO) & (key_lane < count + 2 * HALO), band, 0
    )
    absent = absent.astype(F32) * MASKED
    masked_half = jnp.full((COLS, 128), MASKED, F32)
    bands_here = count // COLS
    nothing = jnp.zeros((), BF16)

    def in_head(head, shape):
        first, _ = head_window(head, local)
        at = lax.broadcasted_iota(jnp.int32, shape, 1) + first
        return (at >= head * HD) & (at < (head + 1) * HD)

    r.attended[...] = jnp.zeros(r.attended.shape, F32)
    for head in range(heads):
        first, last = head_window(head, local)
        own = in_head(head, (count, last - first))
        tile = jnp.full((COLS, 128), MASKED, F32)
        for tap in range(TAPS):
            tile = jnp.where(tap_of == tap, r.bias_table[head, r.bias_index[tap]], tile)
        tile = jnp.concatenate([tile, masked_half], axis=1)
        bias = jnp.concatenate(
            [tile] + [pltpu.roll(tile, COLS * k, 1) for k in range(1, bands_here)], axis=0
        )
        queries = jnp.where(own, r.query[:, first:last], nothing)
        scores = dot_nt(queries, r.keys[:, first:last]) * scale + (bias + absent)
        top = jnp.max(scores, axis=-1, keepdims=True)
        weights = jnp.exp(scores - top)
        weights = weights * (1.0 / jnp.sum(weights, axis=-1, keepdims=True))
        r.prob[head] = weights
        mixed = dot_nn(weights.astype(BF16), r.values[:, first:last])
        r.attended[:, first:last] += jnp.where(own, mixed, 0.0)

    r.attended_low[...] = r.attended[...].astype(BF16)
    loaded(weight_names[2], *inputs[5:8])
    r.part_own[...] = dot_nn(r.attended_low[...], r.out_w[...])
    part_copy = sent(r.part_own, r.part_other, sibling)
    if meshed:
        r.attended_all[0] = r.attended_low[...]
        attended_copies = spread(r.attended_low, r.attended_all.at[pl.ds(1, 3)], plane)
        r.rest[...] = jnp.zeros(r.rest.shape, BF16)
        r.back_stage[...] = jnp.zeros(r.back_stage.shape, BF16)
        r.small_half[6:8] = jnp.zeros((2, width), F32)
    loaded(*weight_names[3:], *inputs[8:])
    r.active_grad[...] = dot_nt(r.cotangent[...], r.down_w[...])
    if meshed:
        cot_flat[:, :count] = jnp.transpose(r.cotangent[...])
    finish(part_copy)
    after = r.tokens[...].astype(F32) + (r.part_own[...] + r.part_other[...]) + line_of(r.out_shift)
    r.resid[...] = after
    unit, _ = normed(after)
    r.second_low[...] = (unit * line_of(r.second_gain) + line_of(r.second_shift)).astype(BF16)
    if meshed:
        second_copies = spread_half(r.second_low, r.second_all, column)

    if meshed:
        finish(first_copies)
        first_copies = pass_half(r.first_all, 1, 3)
    step = hidden // 3
    tiles = WIDE_TILES
    second_sum = None
    for at in range(0, hidden, step):
        piece = slice(at, at + step)
        upper = dot_nn(r.second_low[...], r.up_w[:, piece]) + line_of(r.up_shift, piece)
        active, slope = gelu_pair(upper)
        active = active.astype(BF16)
        r.active_low[0:count, piece] = active
        grad = r.active_grad[:, piece] * slope
        sums = column_sum(grad)
        for line in range(-(-hidden // width)):
            low_at, high_at = max(at, line * width), min(at + step, (line + 1) * width)
            if low_at < high_at:
                r.small_own[6 + line : 7 + line, low_at - line * width : high_at - line * width] = (
                    sums[:, low_at - at : high_at - at]
                )
        grad = grad.astype(BF16)
        r.upper_low[0:count, piece] = grad
        term = dot_nt(grad, r.up_w[:, piece])
        second_sum = term if second_sum is None else second_sum + term
    r.second_own[...] = second_sum.astype(BF16)
    second_copy = sent(r.second_own, r.second_other, sibling)
    r.down_own[...] = dot_nn(r.active_low[0:count], r.down_w[...]).astype(BF16)
    down_copy = sent(r.down_own, r.down_other, sibling)
    if meshed:
        finish(first_copies)
        r.first_flat[...] = jnp.transpose(r.first_all[...].reshape(4 * count, width))
        second_flat[:, :count] = jnp.transpose(r.second_low[...])
    cot = r.cotangent[...].astype(F32)
    r.small_own[5:6] = column_sum(cot)
    finish(second_copy)
    back = r.second_own[...].astype(F32) + r.second_other[...].astype(F32)
    unit, inv = normed(r.resid[...])
    r.small_own[3:4] = column_sum(back * unit)
    r.small_own[4:5] = column_sum(back)
    grad = cot + normed_back(unit, inv, line_of(r.second_gain), back)
    r.tokens_grad[...] = grad
    r.small_own[2:3] = column_sum(grad)
    r.resid_low[...] = grad.astype(BF16)
    r.attended_grad[...] = dot_nt(r.resid_low[...], r.out_w[...]).astype(BF16)
    r.query_grad[...] = jnp.zeros(r.query_grad.shape, F32)
    r.key_grad[...] = jnp.zeros(r.key_grad.shape, F32)
    r.value_grad[...] = jnp.zeros(r.value_grad.shape, F32)
    for head in range(heads):
        first, last = head_window(head, local)
        own = in_head(head, (count, last - first))
        queries = jnp.where(own, r.query[:, first:last], nothing)
        grads = jnp.where(own, r.attended_grad[:, first:last], nothing)
        weights = r.prob[head]
        prob_grad = dot_nt(grads, r.values[:, first:last])
        r.value_grad[:, first:last] += dot_tn(weights.astype(BF16), grads)
        product = weights * prob_grad
        score_grad = product - weights * jnp.sum(product, axis=-1, keepdims=True)
        tile = score_grad[0:COLS]
        for k in range(1, bands_here):
            tile = tile + pltpu.roll(score_grad[k * COLS : (k + 1) * COLS], KEYS - COLS * k, 1)
        r.bias_tiles[head] = tile[:, :128]
        low = (score_grad * scale).astype(BF16)
        r.query_grad[:, first:last] += jnp.where(own, dot_nn(low, r.keys[:, first:last]), 0.0)
        r.key_grad[:, first:last] += dot_tn(low, queries)

    if meshed:
        finish(cot_copies[:1] + second_copies[:1])
        near_copies = pass_half(r.cot_all, 0, 1) + pass_half(r.second_all, 0, 1)
    r.halo_own[:, :local] = r.key_grad[pl.ds(halo_at, HALO)].astype(BF16)
    r.halo_own[:, local:] = r.value_grad[pl.ds(halo_at, HALO)].astype(BF16)
    halo_copy = sent(r.halo_own, r.halo_other, beside)
    low = r.query_grad[...].astype(BF16)
    r.query_low[...] = low
    if meshed:
        r.mixed_all[0, :, 128:256] = r.query_low[:, own_lanes]
        query_copies = deal(r.query_low, 128)
        r.rest[1, :, : local - full] = low[:, full:]
    r.small_own[8:9, :local] = column_sum(low.astype(F32))
    out_lane = lax.broadcasted_iota(jnp.int32, (heads, 128), 1)
    table_grad = jnp.zeros((heads, 128), F32)
    for dc in range(WIN):
        diagonal = inside & (col_step == dc - REACH)
        sums = jnp.sum(jnp.where(diagonal[None], r.bias_tiles[...], 0.0), axis=1)
        for dr in range(WIN):
            group = (out_lane >= dr * COLS) & (out_lane < (dr + 1) * COLS)
            total = jnp.sum(jnp.where(group, sums, 0.0), axis=-1, keepdims=True)
            table_grad = jnp.where(out_lane == r.bias_index[dr * WIN + dc], total, table_grad)
    r.small_own[9:10] = r.time_low[...].astype(F32)
    r.small_own[10:16] = jnp.zeros((6, width), F32)
    for head in range(heads):
        r.small_own[10:11, head * 128 : (head + 1) * 128] = table_grad[head : head + 1]
    if meshed:
        mark = lax.broadcasted_iota(jnp.int32, (1, width), 1) == image * 128 + MARK
        stamp = jnp.where(band == 0, r.step_index[0], 0).astype(F32)
        r.small_own[10:11] += jnp.where(mark, stamp, 0.0)
    finish(down_copy)
    lowered = r.down_own[...].astype(F32) + r.down_other[...].astype(F32)
    r.output[...] = (r.resid[...] + lowered + line_of(r.down_shift)).astype(BF16)

    if meshed:
        r.resid_turned[...] = jnp.transpose(r.tokens_grad[...])
        for k, at in enumerate([spot] + spots):
            lines = [
                r.resid_turned[pl.ds(pl.multiple_of(line * rows4 + owners * at, 8), owners)]
                for line in range(4)
            ]
            r.resid_stage[k] = jnp.concatenate(lines, axis=0).astype(BF16)
        r.resid_all[:, 0:count] = r.resid_stage[0]

        def resid_send():
            base = links(3)
            return started(
                [
                    remote(
                        base + k,
                        r.resid_stage.at[k + 1],
                        r.resid_all.at[:, pl.ds((k + 1) * count, count)],
                        plane[k],
                    )
                    for k in range(3)
                ]
            )

    first_sum = dot_nn(r.query_low[...], r.in_w[0:local])
    unit, inv = normed(r.tokens[...].astype(F32))
    tokens4 = 4 * count
    if meshed:
        finish(near_copies)
        cot_flat[:, count : 2 * count] = jnp.transpose(r.cot_all[0])
        second_flat[:, count : 2 * count] = jnp.transpose(r.second_all[0])

        def near_piece(t):
            piece = slice(t * step, (t + 1) * step)
            upper = dot_nn(r.second_all[0], r.up_w[:, piece]) + line_of(r.up_shift, piece)
            active, slope = gelu_pair(upper)
            r.active_low[count:, piece] = active.astype(BF16)
            grad = dot_nt(r.cot_all[0], r.down_w[piece]) * slope
            r.upper_low[count:, piece] = grad.astype(BF16)

        near_piece(0)
        resid_copies = resid_send()
        near_piece(1)
    finish(halo_copy)
    if meshed:
        finish(cot_copies[1:])
        cot_copies = pass_half(r.cot_all, 1, 2)
    edge_at = pl.multiple_of(HALO + edge, HALO)
    arrived = r.halo_other[...].astype(F32)
    r.key_grad[pl.ds(edge_at, HALO)] += arrived[:, :local]
    r.value_grad[pl.ds(edge_at, HALO)] += arrived[:, local:]
    low = r.key_grad[pl.ds(HALO, count)].astype(BF16)
    r.key_low[...] = low
    if meshed:
        r.mixed_all[0, :, 256:384] = r.key_low[:, own_lanes]
        key_copies = deal(r.key_low, 256)
        r.rest[2, :, : local - full] = low[:, full:]
    low = r.value_grad[pl.ds(HALO, count)].astype(BF16)
    r.value_low[...] = low
    if meshed:
        r.mixed_all[0, :, 384:512] = r.value_low[:, own_lanes]
        value_copies = deal(r.value_low, 384)
        r.rest[3, :, : local - full] = low[:, full:]
        r.mixed_all[0, :, 512:640] = r.rest[spot]
        base = links(3)
        rest_copies = started(
            [
                remote(
                    base + k,
                    r.rest.at[spots[k]],
                    r.mixed_all.at[k + 1, :, pl.ds(512, 128)],
                    plane[k],
                )
                for k in range(3)
            ]
        )
    r.small_own[8:9, local:] = column_sum(low.astype(F32))

    def first_back():
        total = first_sum + dot_nn(r.key_low[...], r.in_w[local : 2 * local])
        total = total + dot_nn(r.value_low[...], r.in_w[2 * local :])
        r.first_own[...] = total.astype(BF16)
        return sent(r.first_own, r.first_other, sibling)

    def first_norm_back():
        back = r.first_own[...].astype(F32) + r.first_other[...].astype(F32)
        r.small_own[0:1] = column_sum(back * unit)
        r.small_own[1:2] = column_sum(back)
        r.tokens_grad[...] += normed_back(unit, inv, line_of(r.first_gain), back)

    if not meshed:
        finish(first_back())
        first_norm_back()
        return

    def mixed(start, stop):
        return r.mixed_all[:, :, start:stop].reshape(tokens4, stop - start)

    near, far = plane[:2]
    starts = [sum(tiles[:t]) for t in range(len(tiles))]

    def wide_lanes(t):
        return pl.ds(starts[t] // 2, tiles[t] // 2)

    def wide_first(t):
        base, lanes = links(4), wide_lanes(t)
        return started(
            [
                remote(
                    base + k,
                    part.at[target, :, lanes],
                    arrived.at[k % 2, :, lanes],
                    near if k < 2 else far,
                )
                for k, (part, arrived, target) in enumerate(
                    (
                        (r.wide_a, r.wide_a_in, spots[0]),
                        (r.wide_a, r.wide_a_in, spots[2]),
                        (r.wide_b, r.wide_b_in, spots[1]),
                        (r.wide_b, r.wide_b_in, spots[2]),
                    )
                )
            ]
        )

    def wide_piece(t):
        piece, lanes = slice(starts[t], starts[t] + tiles[t]), wide_lanes(t)
        upper = dot_nn(r.second_all[1:].reshape(2 * count, width), r.up_w[:, piece])
        active, slope = gelu_pair(upper + line_of(r.up_shift, piece))
        grad = dot_nt(r.cot_all[1:].reshape(2 * count, width), r.down_w[piece]) * slope
        down = dot_nn(cot_flat[own_rows, : 2 * count], r.active_low[:, piece])
        down = down + dot_nn(cot_flat[own_rows, 2 * count :], active.astype(BF16))
        up = dot_nn(second_flat[own_rows, : 2 * count], r.upper_low[:, piece])
        up = up + dot_nn(second_flat[own_rows, 2 * count :], grad.astype(BF16))
        part = tiles[t] // 2
        for k in range(4):
            rows_here = slice(k * owners, (k + 1) * owners)
            both = jnp.concatenate([down[rows_here], up[rows_here]], axis=0).astype(BF16)
            r.wide_a[k, :, lanes] = both[:, :part]
            r.wide_b[k, :, lanes] = both[:, part:]
        return wide_first(t)

    def wide_second(t):
        lanes = wide_lanes(t)
        finish(wide_copies[t])
        total = joined(r.wide_a[spots[1], :, lanes], r.wide_a_in[1, :, lanes])
        r.wide_a_sum[:, lanes] = total.astype(BF16)
        total = joined(r.wide_b[spots[0], :, lanes], r.wide_b_in[1, :, lanes])
        r.wide_b_sum[:, lanes] = total.astype(BF16)
        return sent(r.wide_a_sum.at[:, lanes], r.wide_a_last.at[:, lanes], far) + sent(
            r.wide_b_sum.at[:, lanes], r.wide_b_last.at[:, lanes], near
        )

    def wide_total(t):
        finish(last_copies[t])
        lanes, at = wide_lanes(t), starts[t]
        for part, arrived, last in (
            (r.wide_a, r.wide_a_in, r.wide_a_last),
            (r.wide_b, r.wide_b_in, r.wide_b_last),
        ):
            total = joined(part[spot, :, lanes], arrived[0, :, lanes])
            total = total + last[:, lanes].astype(F32)
            r.down_share[:, at : at + tiles[t] // 2] = total[:owners]
            r.up_share[:, at : at + tiles[t] // 2] = total[owners:]
            at += tiles[t] // 2

    finish(query_copies)
    keep_part("query", dot_nn(r.first_flat[...], mixed(128, 256)))
    query_copies = column_first("query")
    finish(second_copies[1:])
    far_copies = pass_half(r.second_all, 1, 2)
    finish(cot_copies)
    cot_flat[:, 2 * count :] = jnp.transpose(r.cot_all[1:].reshape(2 * count, width))
    near_piece(2)
    finish(key_copies)
    keep_part("key", dot_nn(r.first_flat[...], mixed(256, 384)))
    key_copies = column_first("key")
    finish(far_copies)
    second_flat[:, 2 * count :] = jnp.transpose(r.second_all[1:].reshape(2 * count, width))
    wide_copies = [wide_piece(0)]
    finish(query_copies)
    query_copies = column_second("query")
    wide_copies.append(wide_piece(1))
    finish(value_copies)
    keep_part("value", dot_nn(r.first_flat[...], mixed(384, 512)))
    value_copies = column_first("value")
    wide_copies.append(wide_piece(2))
    first_copy = first_back()
    finish(key_copies)
    key_copies = column_second("key")
    finish(rest_copies)
    term = dot_nn(r.first_flat[...], mixed(512, 640))
    for k in range(4):
        upper_half = term[k * rows4 : k * rows4 + rows4 // 2, : local - full]
        lower_half = term[k * rows4 + rows4 // 2 : (k + 1) * rows4, : local - full]
        r.rest_part[k] = jnp.concatenate([upper_half, lower_half], axis=1).astype(BF16)
    base = links(3)
    rest_copies = started(
        [remote(base + k, r.rest_part.at[heights[k]], r.rest_in.at[k], column[k]) for k in range(3)]
    )
    wide_copies.append(wide_piece(3))
    finish(value_copies)
    value_copies = column_second("value")
    wide_copies.append(wide_piece(4))
    finish(first_copy)
    first_norm_back()
    r.small_send[0:3] = jnp.where(half == 0, r.small_own[0:3], r.small_own[3:6])
    r.small_send[3:5] = r.small_own[6:8]
    r.small_send[5:6] = r.small_own[10:11]
    r.small_send[6:8] = jnp.broadcast_to(r.small_own[8:9], (2, width))
    small_copies = spread(r.small_send, r.small_plane, plane)
    last_copies = [wide_second(0)]
    last_copies.append(wide_second(1))
    finish(attended_copies)
    finish(resid_copies)
    keep_part("attended", dot_nn(r.resid_all[...], r.attended_all[...].reshape(tokens4, local)))
    attended_copies = column_first("attended")
    finish(query_copies)
    total = column_total("query")
    for k in range(4):
        r.front_stage[k] = total[k * owners : (k + 1) * owners].astype(BF16)
    r.front_done[spot] = r.front_stage[spot]
    front_copies = hand_out(r.front_stage, r.front_done)
    finish(rest_copies)
    total = joined(r.rest_part[z], r.rest_in[0]) + joined(r.rest_in[1], r.rest_in[2])
    for k in range(4):
        lanes = slice(k // 2 * (local - full), (k // 2 + 1) * (local - full))
        rows_here = slice(k % 2 * owners, (k % 2 + 1) * owners)
        r.back_stage[k, :, 256 : 256 + local - full] = total[rows_here, lanes].astype(BF16)
    last_copies.append(wide_second(2))
    finish(key_copies)
    total = column_total("key")
    for k in range(4):
        r.back_stage[k, :, :128] = total[k * owners : (k + 1) * owners].astype(BF16)
    last_copies.append(wide_second(3))
    finish(value_copies)
    total = column_total("value")
    for k in range(4):
        r.back_stage[k, :, 128:256] = total[k * owners : (k + 1) * owners].astype(BF16)
    r.back_done[spot] = r.back_stage[spot]
    back_copies = hand_out(r.back_stage, r.back_done)
    last_copies.append(wide_second(4))
    finish(small_copies)
    small_sum = r.small_send[0:6]
    for k in range(3):
        small_sum = small_sum + r.small_plane[k, 0:6]
    r.small_z[0:6] = small_sum
    r.small_z[6:7] = r.small_send[6:7] + r.small_plane[1, 6:7]
    r.small_z[7:8] = r.small_plane[0, 6:7] + r.small_plane[2, 6:7]
    column_copies = spread(r.small_z, r.small_column, column)
    finish(attended_copies)
    attended_copies = column_second("attended")
    wide_total(0)
    wide_total(1)
    finish(column_copies)
    small_sum = r.small_z[0:6]
    for k in range(3):
        small_sum = small_sum + r.small_column[k, 0:6]
    r.small_half[0:6] = small_sum
    small_copies = sent(r.small_half, r.small_other, sibling)
    steps = [small_sum[5:6, k * 128 + MARK : k * 128 + MARK + 1] for k in range(8)]
    cosine, sine = cos_sin(jnp.concatenate(steps, axis=0) * line_of(r.frequencies))
    r.time_lines[:, : width // 2] = cosine.astype(BF16).astype(F32)
    r.time_lines[:, width // 2 :] = sine.astype(BF16).astype(F32)
    r.time_flat[...] = jnp.transpose(r.time_lines[...])
    time_cut = r.time_flat[pl.ds(pl.multiple_of(z * rows4 + spot * owners, 8), owners)]
    time_share = jnp.zeros((owners, width), F32)
    for k in range(4):
        source = r.small_z if k == 0 else r.small_column.at[k - 1]
        at = z if k == 0 else heights[k - 1]
        r.time_sums[pl.ds(2 * at + x, 1)] = source[6:7]
        r.time_sums[pl.ds(2 * at + 1 - x, 1)] = source[7:8]
    for k in range(8):
        time_share = time_share + time_cut[:, k : k + 1] * r.time_sums[k : k + 1]
    for k in range(2):
        r.time_share[:, k, :] = time_share[:, k * local : (k + 1) * local]
    wide_total(2)
    finish(small_copies)
    low_half, high_half = r.small_half[0:3], r.small_other[0:3]
    mixed_low = jnp.where(half == 0, low_half, high_half)
    mixed_high = jnp.where(half == 0, high_half, low_half)
    for line, target in enumerate((r.first_gain_grad, r.first_shift_grad, r.out_shift_grad)):
        target[...] = mixed_low[line]
    for line, target in enumerate((r.second_gain_grad, r.second_shift_grad, r.down_shift_grad)):
        target[...] = mixed_high[line]
    for line in range(hidden // width):
        r.up_shift_grad[line * width : (line + 1) * width] = r.small_half[3 + line]
    for head in range(heads):
        r.bias_grad[head : head + 1] = r.small_half[5:6, head * 128 : head * 128 + TAPS]
    finish(front_copies)
    for k in range(4):
        r.in_share[0, :, k * 128 : (k + 1) * 128] = r.front_done[k].astype(F32)
    finish(attended_copies)
    r.out_share[...] = column_total("attended")
    wide_total(3)
    finish(back_copies)
    for k in range(4):
        for line in range(2):
            lanes = slice(line * 128, (line + 1) * 128)
            share = r.back_done[k, :, lanes].astype(F32)
            r.in_share[1 + line, :, k * 128 : (k + 1) * 128] = share
        if k > 0:
            rest = r.back_done[k, :, 256 : 256 + local - full].astype(F32)
            r.in_share[k - 1, :, full:] = rest
    wide_total(4)


def final_kernel(*refs):
    sems = refs[-1]
    number = (len(refs) - 1) // 2
    copies = [
        pltpu.make_async_copy(refs[k], refs[number + k], sems.at[k]) for k in range(number)
    ]
    for copy in copies:
        copy.start()
    for copy in copies:
        copy.wait()


def final_call(results):
    arrays = list(vars(results).values())
    done = pl.pallas_call(
        final_kernel,
        out_shape=[jax.ShapeDtypeStruct(array.shape, array.dtype) for array in arrays],
        in_specs=[pl.BlockSpec(memory_space=pltpu.VMEM)] * len(arrays),
        out_specs=[pl.BlockSpec(memory_space=pltpu.HBM)] * len(arrays),
        scratch_shapes=[pltpu.SemaphoreType.DMA((len(arrays),))],
        name="final",
        compiler_params=pltpu.CompilerParams(vmem_limit_bytes=8 * 1024 * 1024),
    )(*arrays)
    return types.SimpleNamespace(**dict(zip(vars(results), done, strict=True)))


def layer_call(meshed, timesteps, inputs, smalls, weights):
    count, width = inputs["tokens"].shape
    local = weights["out_w"].shape[0]
    hidden = weights["up_w"].shape[1]
    heads = smalls["bias_table"].shape[0]
    tokens4, rows4 = 4 * count, width // 4
    owners = rows4 // 4
    outs = dict(output=((count, width), BF16), tokens_grad=((count, width), F32))
    feed_rows = 2 * count if meshed else count
    kept = dict(
        first_low=((count, width), BF16),
        second_low=((count, width), BF16),
        active_low=((feed_rows, hidden), BF16),
        upper_low=((feed_rows, hidden), BF16),
        resid_low=((count, width), BF16),
        attended_low=((count, local), BF16),
        query_low=((count, local), BF16),
        key_low=((count, local), BF16),
        value_low=((count, local), BF16),
        small_own=((16, width), F32),
    )
    loads = inputs | weights
    scratch = {name: (array.shape, array.dtype) for name, array in loads.items()}
    scratch |= dict(
        time_low=((1, width), BF16),
        halo_tokens=((HALO, width), BF16),
        query=((count, local), BF16),
        keys=((KEYS, local), BF16),
        values=((KEYS, local), BF16),
        prob=((heads, count, KEYS), F32),
        key_grad=((KEYS, local), F32),
        value_grad=((KEYS, local), F32),
        attended_grad=((count, local), BF16),
        query_grad=((count, local), F32),
        attended=((count, local), F32),
        active_grad=((count, hidden), F32),
        resid=((count, width), F32),
        part_own=((count, width), F32),
        part_other=((count, width), F32),
        halo_own=((HALO, 2 * local), BF16),
        halo_other=((HALO, 2 * local), BF16),
        bias_tiles=((heads, COLS, 128), F32),
    )
    scratch |= dict(
        down_own=((count, width), BF16),
        down_other=((count, width), BF16),
        second_own=((count, width), BF16),
        second_other=((count, width), BF16),
        first_own=((count, width), BF16),
        first_other=((count, width), BF16),
    )
    if meshed:
        outs |= dict(
            first_gain_grad=((width,), F32),
            first_shift_grad=((width,), F32),
            out_shift_grad=((width,), F32),
            second_gain_grad=((width,), F32),
            second_shift_grad=((width,), F32),
            down_shift_grad=((width,), F32),
            up_shift_grad=((hidden,), F32),
            bias_grad=((heads, TAPS), F32),
            in_share=((3, owners, local), F32),
            time_share=((owners, 2, local), F32),
            out_share=((owners, local), F32),
            up_share=((owners, hidden), F32),
            down_share=((owners, hidden), F32),
        )
        scratch |= kept
        scratch |= dict(
            cot_all=((3, count, width), BF16),
            second_all=((3, count, width), BF16),
            first_all=((4, count, width), BF16),
            first_flat=((width, tokens4), BF16),
            attended_all=((4, count, local), BF16),
            resid_turned=((width, count), F32),
            resid_stage=((4, rows4, count), BF16),
            resid_all=((rows4, tokens4), BF16),
            small_send=((8, width), F32),
            small_plane=((3, 8, width), F32),
            small_z=((8, width), F32),
            small_column=((3, 8, width), F32),
            time_sums=((8, width), F32),
            time_lines=((8, width), F32),
            small_half=((8, width), F32),
            small_other=((8, width), F32),
            time_flat=((width, 8), F32),
            mixed_all=((4, count, 640), BF16),
            rest=((4, count, 128), BF16),
            rest_part=((4, rows4 // 2, 128), BF16),
            rest_in=((3, rows4 // 2, 128), BF16),
            front_stage=((4, owners, 128), BF16),
            front_done=((4, owners, 128), BF16),
            back_stage=((4, owners, 384), BF16),
            back_done=((4, owners, 384), BF16),
        )
        for name, rows, wide in (
            ("attended", owners, local),
            ("query", rows4, 128),
            ("key", rows4, 128),
            ("value", rows4, 128),
        ):
            scratch[name + "_part"] = ((4, rows, wide), BF16)
            scratch[name + "_in"] = ((2, rows, wide), BF16)
            scratch[name + "_sum"] = ((rows, wide), BF16)
            scratch[name + "_last"] = ((rows, wide), BF16)
        for name in ("wide_a", "wide_b"):
            scratch[name] = ((4, 2 * owners, hidden // 2), BF16)
            scratch[name + "_in"] = ((2, 2 * owners, hidden // 2), BF16)
            scratch[name + "_sum"] = ((2 * owners, hidden // 2), BF16)
            scratch[name + "_last"] = ((2 * owners, hidden // 2), BF16)
    else:
        outs |= kept
    links = 112 if meshed else 6
    sems = dict(load_sems=len(loads | smalls), send_sems=links, recv_sems=links)
    vmem = pl.BlockSpec(memory_space=pltpu.VMEM)
    smem = pl.BlockSpec(memory_space=pltpu.SMEM)
    hbm = pl.BlockSpec(memory_space=pltpu.HBM)
    names = [name + "_hbm" for name in (*loads, *smalls)]
    names = ["step_index", *names, *outs, *smalls, *scratch, *sems]
    results = pl.pallas_call(
        functools.partial(layer_kernel, names, [*inputs], [*smalls], [*weights], meshed),
        out_shape=[jax.ShapeDtypeStruct(*shape) for shape in outs.values()],
        in_specs=[smem] + [hbm] * len(loads | smalls),
        out_specs=[vmem] * len(outs),
        scratch_shapes=[pltpu.SMEM(array.shape, array.dtype) for array in smalls.values()]
        + [pltpu.VMEM(*shape) for shape in scratch.values()]
        + [pltpu.SemaphoreType.DMA((number,)) for number in sems.values()],
        name="layer",
        compiler_params=pltpu.CompilerParams(
            collective_id=0, has_side_effects=True, vmem_limit_bytes=50 * 1024 * 1024
        ),
    )(
        timesteps,
        *[
            pltpu.with_memory_space_constraint(array, pltpu.HBM)
            for array in (loads | smalls).values()
        ],
    )
    return types.SimpleNamespace(**dict(zip(outs, results, strict=True)))


def on_device(
    tokens,
    timesteps,
    first_gain,
    first_shift,
    project_in,
    time_weight,
    bias_table,
    bias_index,
    project_out,
    out_shift,
    second_gain,
    second_shift,
    up_weight,
    up_shift,
    down_weight,
    down_shift,
    cotangent,
):
    batch, band_rows, columns, width = tokens.shape
    local = project_in.shape[2]
    count = batch * band_rows * columns
    assert batch == 1 and columns == COLS
    half = width // 2
    frequencies = np.exp(np.arange(half) * (-math.log(10000.0) / half)).astype(np.float32)
    meshed = lax.axis_size("img") == 8 and lax.axis_size("band") == 2
    cot = cotangent.reshape(count, width)
    inputs = dict(
        tokens=tokens.reshape(count, width),
        first_gain=first_gain,
        first_shift=first_shift,
        frequencies=jnp.asarray(frequencies),
        cotangent=cot,
        out_shift=out_shift,
        second_gain=second_gain,
        second_shift=second_shift,
        up_shift=up_shift,
        down_shift=down_shift,
    )
    smalls = dict(bias_table=bias_table, bias_index=bias_index)
    weights = dict(
        time_w=jnp.transpose(time_weight, (1, 2, 0)).reshape(2 * local, width),
        in_w=jnp.transpose(project_in, (1, 2, 0)).reshape(3 * local, width),
        out_w=project_out,
        up_w=up_weight,
        down_w=down_weight,
    )
    r = layer_call(meshed, timesteps, inputs, smalls, weights)
    heads = bias_table.shape[0]
    if meshed:
        f = final_call(r)
        return (
            f.output.reshape(tokens.shape),
            f.tokens_grad.reshape(tokens.shape),
            f.first_gain_grad,
            f.first_shift_grad,
            jnp.transpose(f.in_share, (1, 0, 2)),
            f.time_share,
            f.bias_grad,
            jnp.transpose(f.out_share),
            f.out_shift_grad,
            f.second_gain_grad,
            f.second_shift_grad,
            f.up_share,
            f.up_shift_grad,
            jnp.transpose(f.down_share),
            f.down_shift_grad,
        )
    axes = ("img", "band")
    grads = (
        dot_tn(r.first_low, jnp.concatenate([r.query_low, r.key_low, r.value_low], axis=1)),
        dot_tn(r.resid_low, r.attended_low),
        dot_tn(r.second_low, r.upper_low),
        dot_tn(cot, r.active_low),
    )
    in_share, out_share, up_share, down_share = [
        lax.psum_scatter(g.astype(BF16), axes, scatter_dimension=0, tiled=True).astype(F32)
        for g in grads
    ]
    rows = in_share.shape[0]
    in_share = in_share.reshape(rows, 3, local)
    times = lax.all_gather(r.small_own[8:10], axes, axis=0)
    here = lax.axis_index(axes) * rows
    time_cut = lax.dynamic_slice_in_dim(times[:, 1], here, rows, axis=1)
    time_share = jnp.einsum("nd,nk->dk", time_cut, times[:, 0], precision=HIGHEST)
    time_share = time_share.reshape(rows, 2, local)
    small = lax.psum(r.small_own, axes)
    return (
        r.output.reshape(tokens.shape),
        r.tokens_grad.reshape(tokens.shape),
        small[0],
        small[1],
        in_share,
        time_share,
        small[10, : heads * 128].reshape(heads, 128)[:, :TAPS],
        jnp.transpose(out_share),
        small[2],
        small[3],
        small[4],
        up_share,
        small[6:8].reshape(-1)[: up_shift.shape[0]],
        jnp.transpose(down_share),
        small[5],
    )


def solution(mesh):
    return jax.shard_map(
        on_device,
        mesh=mesh,
        in_specs=(
            P("img", "band", None, None),
            P("img"),
            P(),
            P(),
            P(None, None, "head"),
            P(None, None, "head"),
            P("head", None),
            P(),
            P("head", None),
            P(),
            P(),
            P(),
            P(None, "head"),
            P("head"),
            P("head", None),
            P(),
            P("img", "band", None, None),
        ),
        out_specs=(
            P("img", "band", None, None),
            P("img", "band", None, None),
            P(),
            P(),
            P(("img", "band"), None, "head"),
            P(("img", "band"), None, "head"),
            P("head", None),
            P("head", ("img", "band")),
            P(),
            P(),
            P(),
            P(("img", "band"), "head"),
            P("head"),
            P("head", ("img", "band")),
            P(),
        ),
        check_vma=False,
    )
```

```python
import functools
import math
import types

import jax
import jax.numpy as jnp
import numpy as np
from jax import lax
from jax.experimental import pallas as pl
from jax.experimental.pallas import tpu as pltpu
from jax.sharding import PartitionSpec as P

HD = 72
ROWS = 16
COLS = 16
WIN = 5
REACH = WIN // 2
TAPS = WIN * WIN
HALO = REACH * COLS
KEYS = 256

EPSILON = 1e-05
MASKED = -1000000000.0
HIGHEST = lax.Precision.HIGHEST
MESH = pl.DeviceIdType.MESH
BF16 = jnp.bfloat16
F32 = jnp.float32
GELU_A = math.sqrt(2.0 / math.pi)
GELU_B = 0.044715
MARK = 100
WIDE_TILES = (256, 512, 768, 512, 256)
TURN = (6.28125, 0.0019350051879882812, 3.019916e-07)


def dot_nn(a, b):
    return lax.dot_general(a, b, (((1,), (0,)), ((), ())), preferred_element_type=F32)


def dot_nt(a, b):
    return lax.dot_general(a, b, (((1,), (1,)), ((), ())), preferred_element_type=F32)


def dot_tn(a, b):
    return lax.dot_general(a, b, (((0,), (0,)), ((), ())), preferred_element_type=F32)


def normed(values):
    center = values - jnp.mean(values, axis=-1, keepdims=True)
    inv = lax.rsqrt(jnp.mean(center * center, axis=-1, keepdims=True) + EPSILON)
    return center * inv, inv


def normed_back(unit, inv, gain, grad):
    unit_grad = grad * gain
    return inv * (
        unit_grad
        - jnp.mean(unit_grad, axis=-1, keepdims=True)
        - unit * jnp.mean(unit_grad * unit, axis=-1, keepdims=True)
    )


def gelu_pair(u):
    square = u * u
    t = jnp.tanh(GELU_A * u * (1.0 + GELU_B * square))
    half = 0.5 * (1.0 + t)
    slope = half + (0.5 * GELU_A) * u * (1.0 - t * t) * (1.0 + (3.0 * GELU_B) * square)
    return u * half, slope


def column_sum(values):
    return jnp.sum(values, axis=0, keepdims=True)


def cos_sin(angle):
    turns = jnp.floor(angle * (0.5 / math.pi) + 0.5)
    rest = ((angle - turns * TURN[0]) - turns * TURN[1]) - turns * TURN[2]
    square = rest * rest
    cosine = jnp.full(angle.shape, 1.0 / math.factorial(18), F32)
    sine = jnp.full(angle.shape, 1.0 / math.factorial(19), F32)
    for power in range(16, -1, -2):
        cosine = 1.0 / math.factorial(power) - cosine * square
        sine = 1.0 / math.factorial(power + 1) - sine * square
    return cosine, sine * rest


def line_of(vector, piece=slice(None)):
    return vector[piece][None, :]


def head_window(head, width):
    first = head * HD // 128 * 128
    last = min(-(-(head + 1) * HD // 128) * 128, width)
    return first, last


def layer_kernel(names, inputs, small_names, weight_names, meshed, *refs):
    r = types.SimpleNamespace(**dict(zip(names, refs, strict=True)))
    count, width = r.tokens.shape
    local = r.query.shape[1]
    heads = r.bias_table.shape[0]
    hidden = r.up_shift.shape[0]
    scale = HD ** (-0.5)
    image = lax.axis_index("img")
    band = lax.axis_index("band")
    half = lax.axis_index("head")
    sibling = (image, band, 1 - half)
    beside = (image, 1 - band, half)
    peers = [sibling, beside]
    if meshed:
        x, z = image % 2, image // 2
        across = z * 2 + 1 - x
        plane = [(across, band, half), beside, (across, 1 - band, half)]
        spot = 2 * x + band
        spots = [2 * (1 - x) + band, 2 * x + 1 - band, 2 * (1 - x) + 1 - band]
        heights = [z + 1 - 2 * (z % 2), 3 - z, (z + 2) % 4]
        column = [(at * 2 + x, band, half) for at in heights]
        peers = [sibling, *plane, *column]

    loads = {}
    for name in (*inputs[:4], *weight_names[:2], *small_names, *inputs[4:], *weight_names[2:]):
        source, target = getattr(r, name + "_hbm"), getattr(r, name)
        loads[name] = pltpu.make_async_copy(source, target, r.load_sems.at[len(loads)])
        loads[name].start()

    def loaded(*wanted):
        for name in wanted:
            loads.pop(name).wait()

    barrier = pltpu.get_barrier_semaphore()
    for other in peers:
        pl.semaphore_signal(barrier, inc=1, device_id=other, device_id_type=MESH)

    used = [0]

    def links(number):
        used[0] += number
        assert used[0] <= r.send_sems.shape[0]
        return used[0] - number

    def remote(index, source, target, device):
        return pltpu.make_async_remote_copy(
            src_ref=source,
            dst_ref=target,
            send_sem=r.send_sems.at[index],
            recv_sem=r.recv_sems.at[index],
            device_id=device,
            device_id_type=MESH,
        )

    def started(copies):
        for copy in copies:
            copy.start()
        return copies

    def sent(source, target, device):
        return started([remote(links(1), source, target, device)])

    def finish(copies):
        for copy in copies:
            copy.wait()

    def spread(source, slots, group):
        base = links(3)
        return started([remote(base + k, source, slots.at[k], group[k]) for k in range(3)])

    def deal(source, lanes):
        base = links(3)
        return started(
            [
                remote(
                    base + k,
                    source.at[:, pl.ds(pl.multiple_of(spots[k] * 128, 128), 128)],
                    r.mixed_all.at[k + 1, :, pl.ds(lanes, 128)],
                    plane[k],
                )
                for k in range(3)
            ]
        )

    def column_first(name):
        part, arrived = getattr(r, name + "_part"), getattr(r, name + "_in")
        base = links(2)
        return started(
            [remote(base + k, part.at[heights[k]], arrived.at[k], column[0]) for k in range(2)]
        )

    def column_second(name):
        part, arrived = getattr(r, name + "_part"), getattr(r, name + "_in")
        summed = getattr(r, name + "_sum")
        summed[...] = joined(part[heights[2]], arrived[1]).astype(BF16)
        return sent(summed, getattr(r, name + "_last"), column[2])

    def column_total(name):
        part, arrived = getattr(r, name + "_part"), getattr(r, name + "_in")
        return joined(part[z], arrived[0]) + getattr(r, name + "_last")[...].astype(F32)

    def joined(left, right):
        return left.astype(F32) + right.astype(F32)

    def keep_part(name, values):
        part = getattr(r, name + "_part")
        part[...] = values.astype(BF16).reshape(part.shape)

    def hand_out(stage, slots):
        base = links(3)
        return started(
            [remote(base + k, stage.at[spots[k]], slots.at[spot], plane[k]) for k in range(3)]
        )

    if meshed:
        mine = pl.ds(pl.multiple_of(half * (count // 2), count // 2), count // 2)
        full = local // 128 * 128
        own_lanes = pl.ds(pl.multiple_of(spot * 128, 128), 128)

    def spread_half(source, slots, group):
        base = links(3)
        return started(
            [remote(base + k, source.at[mine], slots.at[k, mine], group[k]) for k in range(3)]
        )

    def pass_half(slots, slot, number):
        part = slots.at[pl.ds(slot, number), mine]
        return sent(part, part, sibling)

    loaded(*inputs[:3])
    unit, _ = normed(r.tokens[...].astype(F32))
    own_low = (unit * line_of(r.first_gain) + line_of(r.first_shift)).astype(BF16)
    r.first_low[...] = own_low

    loaded(inputs[3])
    angle = r.step_index[0].astype(F32) * line_of(r.frequencies)
    cosine, sine = cos_sin(angle)
    r.time_low[:, : width // 2] = cosine.astype(BF16)
    r.time_low[:, width // 2 :] = sine.astype(BF16)
    pl.semaphore_wait(barrier, len(peers))
    edge = pl.multiple_of((1 - band) * (count - HALO), HALO)
    token_copy = sent(r.tokens.at[pl.ds(edge, HALO)], r.halo_tokens, beside)
    loaded(inputs[4])
    if meshed:
        cot_copies = spread_half(r.cotangent, r.cot_all, column)
        r.first_all[0] = own_low
        first_copies = spread_half(r.first_low, r.first_all.at[pl.ds(1, 3)], plane)
        rows4 = width // 4
        owners = rows4 // 4
        cot_flat = r.time_w.at[:, pl.ds(0, 4 * count)]
        second_flat = r.time_w.at[:, pl.ds(4 * count, 4 * count)]
        own_rows = pl.ds(pl.multiple_of(z * rows4, 32), rows4)
    loaded(weight_names[0])
    time_rows = jnp.broadcast_to(r.time_low[...], (8, width))
    time_proj = dot_nt(time_rows, r.time_w[...])[0:1]
    halo_at = pl.multiple_of((1 - band) * (count + HALO), HALO)
    blank_at = pl.multiple_of(band * (count + HALO), HALO)
    tail = KEYS - count - 2 * HALO
    loaded(weight_names[1])
    r.query[...] = (dot_nt(own_low, r.in_w[0:local]) + time_proj[:, :local]).astype(BF16)
    r.keys[pl.ds(HALO, count)] = dot_nt(own_low, r.in_w[local : 2 * local]).astype(BF16)
    projected = dot_nt(own_low, r.in_w[2 * local : 3 * local]) + time_proj[:, local:]
    r.values[pl.ds(HALO, count)] = projected.astype(BF16)
    for kept in (r.keys, r.values):
        kept[pl.ds(blank_at, HALO)] = jnp.zeros((HALO, local), BF16)
        kept[pl.ds(count + 2 * HALO, tail)] = jnp.zeros((tail, local), BF16)
    finish(token_copy)
    unit, _ = normed(r.halo_tokens[...].astype(F32))
    halo_low = (unit * line_of(r.first_gain) + line_of(r.first_shift)).astype(BF16)
    r.keys[pl.ds(halo_at, HALO)] = dot_nt(halo_low, r.in_w[local : 2 * local]).astype(BF16)
    projected = dot_nt(halo_low, r.in_w[2 * local : 3 * local]) + time_proj[:, local:]
    r.values[pl.ds(halo_at, HALO)] = projected.astype(BF16)

    loaded(*small_names)
    lane = lax.broadcasted_iota(jnp.int32, (COLS, 128), 1)
    row = lax.broadcasted_iota(jnp.int32, (COLS, 128), 0)
    col_step = lane % COLS - row
    row_step = lane // COLS
    inside = (col_step >= -REACH) & (col_step <= REACH) & (row_step < WIN)
    tap_of = jnp.where(inside, row_step * WIN + col_step + REACH, -1)
    key_lane = lax.broadcasted_iota(jnp.int32, (1, KEYS), 1)
    absent = jnp.where(key_lane < HALO, 1 - band, 0) + jnp.where(
        (key_lane >= count + HALO) & (key_lane < count + 2 * HALO), band, 0
    )
    absent = absent.astype(F32) * MASKED
    masked_half = jnp.full((COLS, 128), MASKED, F32)
    bands_here = count // COLS
    nothing = jnp.zeros((), BF16)

    def in_head(head, shape):
        first, _ = head_window(head, local)
        at = lax.broadcasted_iota(jnp.int32, shape, 1) + first
        return (at >= head * HD) & (at < (head + 1) * HD)

    r.attended[...] = jnp.zeros(r.attended.shape, F32)
    for head in range(heads):
        first, last = head_window(head, local)
        own = in_head(head, (count, last - first))
        tile = jnp.full((COLS, 128), MASKED, F32)
        for tap in range(TAPS):
            tile = jnp.where(tap_of == tap, r.bias_table[head, r.bias_index[tap]], tile)
        tile = jnp.concatenate([tile, masked_half], axis=1)
        bias = jnp.concatenate(
            [tile] + [pltpu.roll(tile, COLS * k, 1) for k in range(1, bands_here)], axis=0
        )
        queries = jnp.where(own, r.query[:, first:last], nothing)
        scores = dot_nt(queries, r.keys[:, first:last]) * scale + (bias + absent)
        top = jnp.max(scores, axis=-1, keepdims=True)
        weights = jnp.exp(scores - top)
        weights = weights * (1.0 / jnp.sum(weights, axis=-1, keepdims=True))
        r.prob[head] = weights
        mixed = dot_nn(weights.astype(BF16), r.values[:, first:last])
        r.attended[:, first:last] += jnp.where(own, mixed, 0.0)

    r.attended_low[...] = r.attended[...].astype(BF16)
    loaded(weight_names[2], *inputs[5:8])
    r.part_own[...] = dot_nn(r.attended_low[...], r.out_w[...])
    part_copy = sent(r.part_own, r.part_other, sibling)
    if meshed:
        r.attended_all[0] = r.attended_low[...]
        attended_copies = spread(r.attended_low, r.attended_all.at[pl.ds(1, 3)], plane)
        r.rest[...] = jnp.zeros(r.rest.shape, BF16)
        r.back_stage[...] = jnp.zeros(r.back_stage.shape, BF16)
        r.small_half[6:8] = jnp.zeros((2, width), F32)
    loaded(*weight_names[3:], *inputs[8:])
    r.active_grad[...] = dot_nt(r.cotangent[...], r.down_w[...])
    if meshed:
        cot_flat[:, :count] = jnp.transpose(r.cotangent[...])
    finish(part_copy)
    after = r.tokens[...].astype(F32) + (r.part_own[...] + r.part_other[...]) + line_of(r.out_shift)
    r.resid[...] = after
    unit, _ = normed(after)
    r.second_low[...] = (unit * line_of(r.second_gain) + line_of(r.second_shift)).astype(BF16)
    if meshed:
        second_copies = spread_half(r.second_low, r.second_all, column)

    if meshed:
        finish(first_copies)
        first_copies = pass_half(r.first_all, 1, 3)
    step = hidden // 3
    tiles = WIDE_TILES
    second_sum = None
    for at in range(0, hidden, step):
        piece = slice(at, at + step)
        upper = dot_nn(r.second_low[...], r.up_w[:, piece]) + line_of(r.up_shift, piece)
        active, slope = gelu_pair(upper)
        active = active.astype(BF16)
        r.active_low[0:count, piece] = active
        grad = r.active_grad[:, piece] * slope
        sums = column_sum(grad)
        for line in range(-(-hidden // width)):
            low_at, high_at = max(at, line * width), min(at + step, (line + 1) * width)
            if low_at < high_at:
                r.small_own[6 + line : 7 + line, low_at - line * width : high_at - line * width] = (
                    sums[:, low_at - at : high_at - at]
                )
        grad = grad.astype(BF16)
        r.upper_low[0:count, piece] = grad
        term = dot_nt(grad, r.up_w[:, piece])
        second_sum = term if second_sum is None else second_sum + term
    r.second_own[...] = second_sum.astype(BF16)
    second_copy = sent(r.second_own, r.second_other, sibling)
    r.down_own[...] = dot_nn(r.active_low[0:count], r.down_w[...]).astype(BF16)
    down_copy = sent(r.down_own, r.down_other, sibling)
    if meshed:
        finish(first_copies)
        r.first_flat[...] = jnp.transpose(r.first_all[...].reshape(4 * count, width))
        second_flat[:, :count] = jnp.transpose(r.second_low[...])
    cot = r.cotangent[...].astype(F32)
    r.small_own[5:6] = column_sum(cot)
    finish(second_copy)
    back = r.second_own[...].astype(F32) + r.second_other[...].astype(F32)
    unit, inv = normed(r.resid[...])
    r.small_own[3:4] = column_sum(back * unit)
    r.small_own[4:5] = column_sum(back)
    grad = cot + normed_back(unit, inv, line_of(r.second_gain), back)
    r.tokens_grad[...] = grad
    r.small_own[2:3] = column_sum(grad)
    r.resid_low[...] = grad.astype(BF16)
    r.attended_grad[...] = dot_nt(r.resid_low[...], r.out_w[...]).astype(BF16)
    r.query_grad[...] = jnp.zeros(r.query_grad.shape, F32)
    r.key_grad[...] = jnp.zeros(r.key_grad.shape, F32)
    r.value_grad[...] = jnp.zeros(r.value_grad.shape, F32)
    for head in range(heads):
        first, last = head_window(head, local)
        own = in_head(head, (count, last - first))
        queries = jnp.where(own, r.query[:, first:last], nothing)
        grads = jnp.where(own, r.attended_grad[:, first:last], nothing)
        weights = r.prob[head]
        prob_grad = dot_nt(grads, r.values[:, first:last])
        r.value_grad[:, first:last] += dot_tn(weights.astype(BF16), grads)
        product = weights * prob_grad
        score_grad = product - weights * jnp.sum(product, axis=-1, keepdims=True)
        tile = score_grad[0:COLS]
        for k in range(1, bands_here):
            tile = tile + pltpu.roll(score_grad[k * COLS : (k + 1) * COLS], KEYS - COLS * k, 1)
        r.bias_tiles[head] = tile[:, :128]
        low = (score_grad * scale).astype(BF16)
        r.query_grad[:, first:last] += jnp.where(own, dot_nn(low, r.keys[:, first:last]), 0.0)
        r.key_grad[:, first:last] += dot_tn(low, queries)

    if meshed:
        finish(cot_copies[:1] + second_copies[:1])
        near_copies = pass_half(r.cot_all, 0, 1) + pass_half(r.second_all, 0, 1)
    r.halo_own[:, :local] = r.key_grad[pl.ds(halo_at, HALO)].astype(BF16)
    r.halo_own[:, local:] = r.value_grad[pl.ds(halo_at, HALO)].astype(BF16)
    halo_copy = sent(r.halo_own, r.halo_other, beside)
    low = r.query_grad[...].astype(BF16)
    r.query_low[...] = low
    if meshed:
        r.mixed_all[0, :, 128:256] = r.query_low[:, own_lanes]
        query_copies = deal(r.query_low, 128)
        r.rest[1, :, : local - full] = low[:, full:]
    r.small_own[8:9, :local] = column_sum(low.astype(F32))
    out_lane = lax.broadcasted_iota(jnp.int32, (heads, 128), 1)
    table_grad = jnp.zeros((heads, 128), F32)
    for dc in range(WIN):
        diagonal = inside & (col_step == dc - REACH)
        sums = jnp.sum(jnp.where(diagonal[None], r.bias_tiles[...], 0.0), axis=1)
        for dr in range(WIN):
            group = (out_lane >= dr * COLS) & (out_lane < (dr + 1) * COLS)
            total = jnp.sum(jnp.where(group, sums, 0.0), axis=-1, keepdims=True)
            table_grad = jnp.where(out_lane == r.bias_index[dr * WIN + dc], total, table_grad)
    r.small_own[9:10] = r.time_low[...].astype(F32)
    r.small_own[10:16] = jnp.zeros((6, width), F32)
    for head in range(heads):
        r.small_own[10:11, head * 128 : (head + 1) * 128] = table_grad[head : head + 1]
    if meshed:
        mark = lax.broadcasted_iota(jnp.int32, (1, width), 1) == image * 128 + MARK
        stamp = jnp.where(band == 0, r.step_index[0], 0).astype(F32)
        r.small_own[10:11] += jnp.where(mark, stamp, 0.0)
    finish(down_copy)
    lowered = r.down_own[...].astype(F32) + r.down_other[...].astype(F32)
    r.output[...] = (r.resid[...] + lowered + line_of(r.down_shift)).astype(BF16)

    if meshed:
        r.resid_turned[...] = jnp.transpose(r.tokens_grad[...])
        for k, at in enumerate([spot] + spots):
            lines = [
                r.resid_turned[pl.ds(pl.multiple_of(line * rows4 + owners * at, 8), owners)]
                for line in range(4)
            ]
            r.resid_stage[k] = jnp.concatenate(lines, axis=0).astype(BF16)
        r.resid_all[:, 0:count] = r.resid_stage[0]

        def resid_send():
            base = links(3)
            return started(
                [
                    remote(
                        base + k,
                        r.resid_stage.at[k + 1],
                        r.resid_all.at[:, pl.ds((k + 1) * count, count)],
                        plane[k],
                    )
                    for k in range(3)
                ]
            )

    first_sum = dot_nn(r.query_low[...], r.in_w[0:local])
    unit, inv = normed(r.tokens[...].astype(F32))
    tokens4 = 4 * count
    if meshed:
        finish(near_copies)
        cot_flat[:, count : 2 * count] = jnp.transpose(r.cot_all[0])
        second_flat[:, count : 2 * count] = jnp.transpose(r.second_all[0])

        def near_piece(t):
            piece = slice(t * step, (t + 1) * step)
            upper = dot_nn(r.second_all[0], r.up_w[:, piece]) + line_of(r.up_shift, piece)
            active, slope = gelu_pair(upper)
            r.active_low[count:, piece] = active.astype(BF16)
            grad = dot_nt(r.cot_all[0], r.down_w[piece]) * slope
            r.upper_low[count:, piece] = grad.astype(BF16)

        near_piece(0)
        resid_copies = resid_send()
        near_piece(1)
    finish(halo_copy)
    if meshed:
        finish(cot_copies[1:])
        cot_copies = pass_half(r.cot_all, 1, 2)
    edge_at = pl.multiple_of(HALO + edge, HALO)
    arrived = r.halo_other[...].astype(F32)
    r.key_grad[pl.ds(edge_at, HALO)] += arrived[:, :local]
    r.value_grad[pl.ds(edge_at, HALO)] += arrived[:, local:]
    low = r.key_grad[pl.ds(HALO, count)].astype(BF16)
    r.key_low[...] = low
    if meshed:
        r.mixed_all[0, :, 256:384] = r.key_low[:, own_lanes]
        key_copies = deal(r.key_low, 256)
        r.rest[2, :, : local - full] = low[:, full:]
    low = r.value_grad[pl.ds(HALO, count)].astype(BF16)
    r.value_low[...] = low
    if meshed:
        r.mixed_all[0, :, 384:512] = r.value_low[:, own_lanes]
        value_copies = deal(r.value_low, 384)
        r.rest[3, :, : local - full] = low[:, full:]
        r.mixed_all[0, :, 512:640] = r.rest[spot]
        base = links(3)
        rest_copies = started(
            [
                remote(
                    base + k,
                    r.rest.at[spots[k]],
                    r.mixed_all.at[k + 1, :, pl.ds(512, 128)],
                    plane[k],
                )
                for k in range(3)
            ]
        )
    r.small_own[8:9, local:] = column_sum(low.astype(F32))

    def first_back():
        total = first_sum + dot_nn(r.key_low[...], r.in_w[local : 2 * local])
        total = total + dot_nn(r.value_low[...], r.in_w[2 * local :])
        r.first_own[...] = total.astype(BF16)
        return sent(r.first_own, r.first_other, sibling)

    def first_norm_back():
        back = r.first_own[...].astype(F32) + r.first_other[...].astype(F32)
        r.small_own[0:1] = column_sum(back * unit)
        r.small_own[1:2] = column_sum(back)
        r.tokens_grad[...] += normed_back(unit, inv, line_of(r.first_gain), back)

    if not meshed:
        finish(first_back())
        first_norm_back()
        return

    def mixed(start, stop):
        return r.mixed_all[:, :, start:stop].reshape(tokens4, stop - start)

    near, far = plane[:2]
    starts = [sum(tiles[:t]) for t in range(len(tiles))]

    def wide_lanes(t):
        return pl.ds(starts[t] // 2, tiles[t] // 2)

    def wide_first(t):
        base, lanes = links(4), wide_lanes(t)
        return started(
            [
                remote(
                    base + k,
                    part.at[target, :, lanes],
                    arrived.at[k % 2, :, lanes],
                    near if k < 2 else far,
                )
                for k, (part, arrived, target) in enumerate(
                    (
                        (r.wide_a, r.wide_a_in, spots[0]),
                        (r.wide_a, r.wide_a_in, spots[2]),
                        (r.wide_b, r.wide_b_in, spots[1]),
                        (r.wide_b, r.wide_b_in, spots[2]),
                    )
                )
            ]
        )

    def wide_piece(t):
        piece, lanes = slice(starts[t], starts[t] + tiles[t]), wide_lanes(t)
        upper = dot_nn(r.second_all[1:].reshape(2 * count, width), r.up_w[:, piece])
        active, slope = gelu_pair(upper + line_of(r.up_shift, piece))
        grad = dot_nt(r.cot_all[1:].reshape(2 * count, width), r.down_w[piece]) * slope
        down = dot_nn(cot_flat[own_rows, : 2 * count], r.active_low[:, piece])
        down = down + dot_nn(cot_flat[own_rows, 2 * count :], active.astype(BF16))
        up = dot_nn(second_flat[own_rows, : 2 * count], r.upper_low[:, piece])
        up = up + dot_nn(second_flat[own_rows, 2 * count :], grad.astype(BF16))
        part = tiles[t] // 2
        for k in range(4):
            rows_here = slice(k * owners, (k + 1) * owners)
            both = jnp.concatenate([down[rows_here], up[rows_here]], axis=0).astype(BF16)
            r.wide_a[k, :, lanes] = both[:, :part]
            r.wide_b[k, :, lanes] = both[:, part:]
        return wide_first(t)

    def wide_second(t):
        lanes = wide_lanes(t)
        finish(wide_copies[t])
        total = joined(r.wide_a[spots[1], :, lanes], r.wide_a_in[1, :, lanes])
        r.wide_a_sum[:, lanes] = total.astype(BF16)
        total = joined(r.wide_b[spots[0], :, lanes], r.wide_b_in[1, :, lanes])
        r.wide_b_sum[:, lanes] = total.astype(BF16)
        return sent(r.wide_a_sum.at[:, lanes], r.wide_a_last.at[:, lanes], far) + sent(
            r.wide_b_sum.at[:, lanes], r.wide_b_last.at[:, lanes], near
        )

    def wide_total(t):
        finish(last_copies[t])
        lanes, at = wide_lanes(t), starts[t]
        for part, arrived, last in (
            (r.wide_a, r.wide_a_in, r.wide_a_last),
            (r.wide_b, r.wide_b_in, r.wide_b_last),
        ):
            total = joined(part[spot, :, lanes], arrived[0, :, lanes])
            total = total + last[:, lanes].astype(F32)
            r.down_share[:, at : at + tiles[t] // 2] = total[:owners]
            r.up_share[:, at : at + tiles[t] // 2] = total[owners:]
            at += tiles[t] // 2

    finish(query_copies)
    keep_part("query", dot_nn(r.first_flat[...], mixed(128, 256)))
    query_copies = column_first("query")
    near_piece(2)
    finish(second_copies[1:])
    far_copies = pass_half(r.second_all, 1, 2)
    finish(cot_copies)
    cot_flat[:, 2 * count :] = jnp.transpose(r.cot_all[1:].reshape(2 * count, width))
    finish(key_copies)
    keep_part("key", dot_nn(r.first_flat[...], mixed(256, 384)))
    key_copies = column_first("key")
    finish(far_copies)
    second_flat[:, 2 * count :] = jnp.transpose(r.second_all[1:].reshape(2 * count, width))
    wide_copies = [wide_piece(0)]
    finish(query_copies)
    query_copies = column_second("query")
    wide_copies.append(wide_piece(1))
    finish(value_copies)
    keep_part("value", dot_nn(r.first_flat[...], mixed(384, 512)))
    value_copies = column_first("value")
    wide_copies.append(wide_piece(2))
    first_copy = first_back()
    finish(key_copies)
    key_copies = column_second("key")
    finish(rest_copies)
    term = dot_nn(r.first_flat[...], mixed(512, 640))
    for k in range(4):
        upper_half = term[k * rows4 : k * rows4 + rows4 // 2, : local - full]
        lower_half = term[k * rows4 + rows4 // 2 : (k + 1) * rows4, : local - full]
        r.rest_part[k] = jnp.concatenate([upper_half, lower_half], axis=1).astype(BF16)
    base = links(3)
    rest_copies = started(
        [remote(base + k, r.rest_part.at[heights[k]], r.rest_in.at[k], column[k]) for k in range(3)]
    )
    wide_copies.append(wide_piece(3))
    finish(value_copies)
    value_copies = column_second("value")
    finish(first_copy)
    first_norm_back()
    r.small_send[0:3] = jnp.where(half == 0, r.small_own[0:3], r.small_own[3:6])
    r.small_send[3:5] = r.small_own[6:8]
    r.small_send[5:6] = r.small_own[10:11]
    r.small_send[6:8] = jnp.broadcast_to(r.small_own[8:9], (2, width))
    small_copies = spread(r.small_send, r.small_plane, plane)
    wide_copies.append(wide_piece(4))
    last_copies = [wide_second(0)]
    last_copies.append(wide_second(1))
    finish(attended_copies)
    finish(resid_copies)
    keep_part("attended", dot_nn(r.resid_all[...], r.attended_all[...].reshape(tokens4, local)))
    attended_copies = column_first("attended")
    finish(query_copies)
    total = column_total("query")
    for k in range(4):
        r.front_stage[k] = total[k * owners : (k + 1) * owners].astype(BF16)
    r.front_done[spot] = r.front_stage[spot]
    front_copies = hand_out(r.front_stage, r.front_done)
    finish(rest_copies)
    total = joined(r.rest_part[z], r.rest_in[0]) + joined(r.rest_in[1], r.rest_in[2])
    for k in range(4):
        lanes = slice(k // 2 * (local - full), (k // 2 + 1) * (local - full))
        rows_here = slice(k % 2 * owners, (k % 2 + 1) * owners)
        r.back_stage[k, :, 256 : 256 + local - full] = total[rows_here, lanes].astype(BF16)
    last_copies.append(wide_second(2))
    finish(key_copies)
    total = column_total("key")
    for k in range(4):
        r.back_stage[k, :, :128] = total[k * owners : (k + 1) * owners].astype(BF16)
    finish(small_copies)
    small_sum = r.small_send[0:6]
    for k in range(3):
        small_sum = small_sum + r.small_plane[k, 0:6]
    r.small_z[0:6] = small_sum
    r.small_z[6:7] = r.small_send[6:7] + r.small_plane[1, 6:7]
    r.small_z[7:8] = r.small_plane[0, 6:7] + r.small_plane[2, 6:7]
    column_copies = spread(r.small_z, r.small_column, column)
    last_copies.append(wide_second(3))
    finish(value_copies)
    total = column_total("value")
    for k in range(4):
        r.back_stage[k, :, 128:256] = total[k * owners : (k + 1) * owners].astype(BF16)
    r.back_done[spot] = r.back_stage[spot]
    back_copies = hand_out(r.back_stage, r.back_done)
    last_copies.append(wide_second(4))
    finish(attended_copies)
    attended_copies = column_second("attended")
    wide_total(0)
    wide_total(1)
    finish(column_copies)
    small_sum = r.small_z[0:6]
    for k in range(3):
        small_sum = small_sum + r.small_column[k, 0:6]
    r.small_half[0:6] = small_sum
    small_copies = sent(r.small_half, r.small_other, sibling)
    steps = [small_sum[5:6, k * 128 + MARK : k * 128 + MARK + 1] for k in range(8)]
    cosine, sine = cos_sin(jnp.concatenate(steps, axis=0) * line_of(r.frequencies))
    r.time_lines[:, : width // 2] = cosine.astype(BF16).astype(F32)
    r.time_lines[:, width // 2 :] = sine.astype(BF16).astype(F32)
    r.time_flat[...] = jnp.transpose(r.time_lines[...])
    time_cut = r.time_flat[pl.ds(pl.multiple_of(z * rows4 + spot * owners, 8), owners)]
    time_share = jnp.zeros((owners, width), F32)
    for k in range(4):
        source = r.small_z if k == 0 else r.small_column.at[k - 1]
        at = z if k == 0 else heights[k - 1]
        r.time_sums[pl.ds(2 * at + x, 1)] = source[6:7]
        r.time_sums[pl.ds(2 * at + 1 - x, 1)] = source[7:8]
    for k in range(8):
        time_share = time_share + time_cut[:, k : k + 1] * r.time_sums[k : k + 1]
    for k in range(2):
        r.time_share[:, k, :] = time_share[:, k * local : (k + 1) * local]
    wide_total(2)
    finish(small_copies)
    low_half, high_half = r.small_half[0:3], r.small_other[0:3]
    mixed_low = jnp.where(half == 0, low_half, high_half)
    mixed_high = jnp.where(half == 0, high_half, low_half)
    for line, target in enumerate((r.first_gain_grad, r.first_shift_grad, r.out_shift_grad)):
        target[...] = mixed_low[line]
    for line, target in enumerate((r.second_gain_grad, r.second_shift_grad, r.down_shift_grad)):
        target[...] = mixed_high[line]
    for line in range(hidden // width):
        r.up_shift_grad[line * width : (line + 1) * width] = r.small_half[3 + line]
    for head in range(heads):
        r.bias_grad[head : head + 1] = r.small_half[5:6, head * 128 : head * 128 + TAPS]
    finish(front_copies)
    for k in range(4):
        r.in_share[0, :, k * 128 : (k + 1) * 128] = r.front_done[k].astype(F32)
    finish(attended_copies)
    r.out_share[...] = column_total("attended")
    wide_total(3)
    finish(back_copies)
    for k in range(4):
        for line in range(2):
            lanes = slice(line * 128, (line + 1) * 128)
            share = r.back_done[k, :, lanes].astype(F32)
            r.in_share[1 + line, :, k * 128 : (k + 1) * 128] = share
        if k > 0:
            rest = r.back_done[k, :, 256 : 256 + local - full].astype(F32)
            r.in_share[k - 1, :, full:] = rest
    wide_total(4)


def final_kernel(*refs):
    sems = refs[-1]
    number = (len(refs) - 1) // 2
    copies = [
        pltpu.make_async_copy(refs[k], refs[number + k], sems.at[k]) for k in range(number)
    ]
    for copy in copies:
        copy.start()
    for copy in copies:
        copy.wait()


def final_call(results):
    arrays = list(vars(results).values())
    done = pl.pallas_call(
        final_kernel,
        out_shape=[jax.ShapeDtypeStruct(array.shape, array.dtype) for array in arrays],
        in_specs=[pl.BlockSpec(memory_space=pltpu.VMEM)] * len(arrays),
        out_specs=[pl.BlockSpec(memory_space=pltpu.HBM)] * len(arrays),
        scratch_shapes=[pltpu.SemaphoreType.DMA((len(arrays),))],
        name="final",
        compiler_params=pltpu.CompilerParams(vmem_limit_bytes=8 * 1024 * 1024),
    )(*arrays)
    return types.SimpleNamespace(**dict(zip(vars(results), done, strict=True)))


def layer_call(meshed, timesteps, inputs, smalls, weights):
    count, width = inputs["tokens"].shape
    local = weights["out_w"].shape[0]
    hidden = weights["up_w"].shape[1]
    heads = smalls["bias_table"].shape[0]
    tokens4, rows4 = 4 * count, width // 4
    owners = rows4 // 4
    outs = dict(output=((count, width), BF16), tokens_grad=((count, width), F32))
    feed_rows = 2 * count if meshed else count
    kept = dict(
        first_low=((count, width), BF16),
        second_low=((count, width), BF16),
        active_low=((feed_rows, hidden), BF16),
        upper_low=((feed_rows, hidden), BF16),
        resid_low=((count, width), BF16),
        attended_low=((count, local), BF16),
        query_low=((count, local), BF16),
        key_low=((count, local), BF16),
        value_low=((count, local), BF16),
        small_own=((16, width), F32),
    )
    loads = inputs | weights
    scratch = {name: (array.shape, array.dtype) for name, array in loads.items()}
    scratch |= dict(
        time_low=((1, width), BF16),
        halo_tokens=((HALO, width), BF16),
        query=((count, local), BF16),
        keys=((KEYS, local), BF16),
        values=((KEYS, local), BF16),
        prob=((heads, count, KEYS), F32),
        key_grad=((KEYS, local), F32),
        value_grad=((KEYS, local), F32),
        attended_grad=((count, local), BF16),
        query_grad=((count, local), F32),
        attended=((count, local), F32),
        active_grad=((count, hidden), F32),
        resid=((count, width), F32),
        part_own=((count, width), F32),
        part_other=((count, width), F32),
        halo_own=((HALO, 2 * local), BF16),
        halo_other=((HALO, 2 * local), BF16),
        bias_tiles=((heads, COLS, 128), F32),
    )
    scratch |= dict(
        down_own=((count, width), BF16),
        down_other=((count, width), BF16),
        second_own=((count, width), BF16),
        second_other=((count, width), BF16),
        first_own=((count, width), BF16),
        first_other=((count, width), BF16),
    )
    if meshed:
        outs |= dict(
            first_gain_grad=((width,), F32),
            first_shift_grad=((width,), F32),
            out_shift_grad=((width,), F32),
            second_gain_grad=((width,), F32),
            second_shift_grad=((width,), F32),
            down_shift_grad=((width,), F32),
            up_shift_grad=((hidden,), F32),
            bias_grad=((heads, TAPS), F32),
            in_share=((3, owners, local), F32),
            time_share=((owners, 2, local), F32),
            out_share=((owners, local), F32),
            up_share=((owners, hidden), F32),
            down_share=((owners, hidden), F32),
        )
        scratch |= kept
        scratch |= dict(
            cot_all=((3, count, width), BF16),
            second_all=((3, count, width), BF16),
            first_all=((4, count, width), BF16),
            first_flat=((width, tokens4), BF16),
            attended_all=((4, count, local), BF16),
            resid_turned=((width, count), F32),
            resid_stage=((4, rows4, count), BF16),
            resid_all=((rows4, tokens4), BF16),
            small_send=((8, width), F32),
            small_plane=((3, 8, width), F32),
            small_z=((8, width), F32),
            small_column=((3, 8, width), F32),
            time_sums=((8, width), F32),
            time_lines=((8, width), F32),
            small_half=((8, width), F32),
            small_other=((8, width), F32),
            time_flat=((width, 8), F32),
            mixed_all=((4, count, 640), BF16),
            rest=((4, count, 128), BF16),
            rest_part=((4, rows4 // 2, 128), BF16),
            rest_in=((3, rows4 // 2, 128), BF16),
            front_stage=((4, owners, 128), BF16),
            front_done=((4, owners, 128), BF16),
            back_stage=((4, owners, 384), BF16),
            back_done=((4, owners, 384), BF16),
        )
        for name, rows, wide in (
            ("attended", owners, local),
            ("query", rows4, 128),
            ("key", rows4, 128),
            ("value", rows4, 128),
        ):
            scratch[name + "_part"] = ((4, rows, wide), BF16)
            scratch[name + "_in"] = ((2, rows, wide), BF16)
            scratch[name + "_sum"] = ((rows, wide), BF16)
            scratch[name + "_last"] = ((rows, wide), BF16)
        for name in ("wide_a", "wide_b"):
            scratch[name] = ((4, 2 * owners, hidden // 2), BF16)
            scratch[name + "_in"] = ((2, 2 * owners, hidden // 2), BF16)
            scratch[name + "_sum"] = ((2 * owners, hidden // 2), BF16)
            scratch[name + "_last"] = ((2 * owners, hidden // 2), BF16)
    else:
        outs |= kept
    links = 112 if meshed else 6
    sems = dict(load_sems=len(loads | smalls), send_sems=links, recv_sems=links)
    vmem = pl.BlockSpec(memory_space=pltpu.VMEM)
    smem = pl.BlockSpec(memory_space=pltpu.SMEM)
    hbm = pl.BlockSpec(memory_space=pltpu.HBM)
    names = [name + "_hbm" for name in (*loads, *smalls)]
    names = ["step_index", *names, *outs, *smalls, *scratch, *sems]
    results = pl.pallas_call(
        functools.partial(layer_kernel, names, [*inputs], [*smalls], [*weights], meshed),
        out_shape=[jax.ShapeDtypeStruct(*shape) for shape in outs.values()],
        in_specs=[smem] + [hbm] * len(loads | smalls),
        out_specs=[vmem] * len(outs),
        scratch_shapes=[pltpu.SMEM(array.shape, array.dtype) for array in smalls.values()]
        + [pltpu.VMEM(*shape) for shape in scratch.values()]
        + [pltpu.SemaphoreType.DMA((number,)) for number in sems.values()],
        name="layer",
        compiler_params=pltpu.CompilerParams(
            collective_id=0, has_side_effects=True, vmem_limit_bytes=50 * 1024 * 1024
        ),
    )(
        timesteps,
        *[
            pltpu.with_memory_space_constraint(array, pltpu.HBM)
            for array in (loads | smalls).values()
        ],
    )
    return types.SimpleNamespace(**dict(zip(outs, results, strict=True)))


def on_device(
    tokens,
    timesteps,
    first_gain,
    first_shift,
    project_in,
    time_weight,
    bias_table,
    bias_index,
    project_out,
    out_shift,
    second_gain,
    second_shift,
    up_weight,
    up_shift,
    down_weight,
    down_shift,
    cotangent,
):
    batch, band_rows, columns, width = tokens.shape
    local = project_in.shape[2]
    count = batch * band_rows * columns
    assert batch == 1 and columns == COLS
    half = width // 2
    frequencies = np.exp(np.arange(half) * (-math.log(10000.0) / half)).astype(np.float32)
    meshed = lax.axis_size("img") == 8 and lax.axis_size("band") == 2
    cot = cotangent.reshape(count, width)
    inputs = dict(
        tokens=tokens.reshape(count, width),
        first_gain=first_gain,
        first_shift=first_shift,
        frequencies=jnp.asarray(frequencies),
        cotangent=cot,
        out_shift=out_shift,
        second_gain=second_gain,
        second_shift=second_shift,
        up_shift=up_shift,
        down_shift=down_shift,
    )
    smalls = dict(bias_table=bias_table, bias_index=bias_index)
    weights = dict(
        time_w=jnp.transpose(time_weight, (1, 2, 0)).reshape(2 * local, width),
        in_w=jnp.transpose(project_in, (1, 2, 0)).reshape(3 * local, width),
        out_w=project_out,
        up_w=up_weight,
        down_w=down_weight,
    )
    r = layer_call(meshed, timesteps, inputs, smalls, weights)
    heads = bias_table.shape[0]
    if meshed:
        f = final_call(r)
        return (
            f.output.reshape(tokens.shape),
            f.tokens_grad.reshape(tokens.shape),
            f.first_gain_grad,
            f.first_shift_grad,
            jnp.transpose(f.in_share, (1, 0, 2)),
            f.time_share,
            f.bias_grad,
            jnp.transpose(f.out_share),
            f.out_shift_grad,
            f.second_gain_grad,
            f.second_shift_grad,
            f.up_share,
            f.up_shift_grad,
            jnp.transpose(f.down_share),
            f.down_shift_grad,
        )
    axes = ("img", "band")
    grads = (
        dot_tn(r.first_low, jnp.concatenate([r.query_low, r.key_low, r.value_low], axis=1)),
        dot_tn(r.resid_low, r.attended_low),
        dot_tn(r.second_low, r.upper_low),
        dot_tn(cot, r.active_low),
    )
    in_share, out_share, up_share, down_share = [
        lax.psum_scatter(g.astype(BF16), axes, scatter_dimension=0, tiled=True).astype(F32)
        for g in grads
    ]
    rows = in_share.shape[0]
    in_share = in_share.reshape(rows, 3, local)
    times = lax.all_gather(r.small_own[8:10], axes, axis=0)
    here = lax.axis_index(axes) * rows
    time_cut = lax.dynamic_slice_in_dim(times[:, 1], here, rows, axis=1)
    time_share = jnp.einsum("nd,nk->dk", time_cut, times[:, 0], precision=HIGHEST)
    time_share = time_share.reshape(rows, 2, local)
    small = lax.psum(r.small_own, axes)
    return (
        r.output.reshape(tokens.shape),
        r.tokens_grad.reshape(tokens.shape),
        small[0],
        small[1],
        in_share,
        time_share,
        small[10, : heads * 128].reshape(heads, 128)[:, :TAPS],
        jnp.transpose(out_share),
        small[2],
        small[3],
        small[4],
        up_share,
        small[6:8].reshape(-1)[: up_shift.shape[0]],
        jnp.transpose(down_share),
        small[5],
    )


def solution(mesh):
    return jax.shard_map(
        on_device,
        mesh=mesh,
        in_specs=(
            P("img", "band", None, None),
            P("img"),
            P(),
            P(),
            P(None, None, "head"),
            P(None, None, "head"),
            P("head", None),
            P(),
            P("head", None),
            P(),
            P(),
            P(),
            P(None, "head"),
            P("head"),
            P("head", None),
            P(),
            P("img", "band", None, None),
        ),
        out_specs=(
            P("img", "band", None, None),
            P("img", "band", None, None),
            P(),
            P(),
            P(("img", "band"), None, "head"),
            P(("img", "band"), None, "head"),
            P("head", None),
            P("head", ("img", "band")),
            P(),
            P(),
            P(),
            P(("img", "band"), "head"),
            P("head"),
            P("head", ("img", "band")),
            P(),
        ),
        check_vma=False,
    )
```
